32 devices in a mesh: dp: 2 (over core), row: 4 (over y, x), col: 4 (over z).
Axes of the slice: x: 2, y: 2, z: 4, core: 2. Of those that a mesh axis runs over, the one named last changes fastest.
Arguments:
- x_in: bfloat16 [4, 768, 4096], P('dp', 'col', 'row'), may hold values from -6 to 6
- prefix: int32 [4], P('dp'), may hold values from 409 to 2048
- enc_bank: bfloat16 [4, 768, 4096], P('dp', 'col'), may hold values from -6 to 6
- bank_rows: int32 [4, 1024], P('dp'), may hold values from 0 to 4095, as said below
- w_qkv: bfloat16 [768, 3, 12, 64], P('col', None, 'row', 'dp'), may hold values from -0.3125 to 0.3125
- w_out: bfloat16 [12, 64, 768], P('row', 'dp', 'col'), may hold values from -0.625 to 0.625
- w_cross_q: bfloat16 [768, 12, 64], P('col', 'row', 'dp'), may hold values from -0.3125 to 0.3125
- w_cross_kv: bfloat16 [768, 2, 12, 64], P('col', None, 'row', 'dp'), may hold values from -0.3125 to 0.3125
- w_cross_out: bfloat16 [12, 64, 768], P('row', 'dp', 'col'), may hold values from -0.625 to 0.625
- w_up: bfloat16 [768, 3072], P('col', ('dp', 'row')), may hold values from -0.21875 to 0.21875
- w_down: bfloat16 [3072, 768], P(('dp', 'row'), 'col'), may hold values from -0.109375 to 0.109375
- ln_gains: bfloat16 [3, 768], P(None, 'col'), may hold values from 0.25 to 1.75
- out_grad: bfloat16 [4, 768, 4096], P('dp', 'col', 'row'), may hold values from -6 to 6
Outputs:
- block_out: bfloat16 [4, 768, 4096], P('dp', 'col', 'row')
- x_grad: float32 [4, 768, 4096], P('dp', 'col', 'row')
- bank_grad: float32 [4, 768, 4096], P('dp', 'col')
- w_qkv_grad: float32 [768, 3, 12, 64], P('col', None, 'row', 'dp')
- w_out_grad: float32 [12, 64, 768], P('row', 'dp', 'col')
- w_cross_q_grad: float32 [768, 12, 64], P('col', 'row', 'dp')
- w_cross_kv_grad: float32 [768, 2, 12, 64], P('col', None, 'row', 'dp')
- w_cross_out_grad: float32 [12, 64, 768], P('row', 'dp', 'col')
- w_up_grad: float32 [768, 3072], P('col', ('dp', 'row'))
- w_down_grad: float32 [3072, 768], P(('dp', 'row'), 'col')
- ln_gains_grad: float32 [3, 768], P(None, 'col')
The draws below stay inside these ranges and needn't reach their ends.
Inputs may be any that keep to these rules, and one draw needn't show every extreme that they name: `bank_rows`: within a sequence the 1024 rows are distinct.
All inputs are finite; a program needn't handle non-finite values.
Results may differ from the reference program's by a relative error of at most 0.025.
Values may be sent and summed in bfloat16 or wider, within the bound.
No kernel may reach another device: no remote copies, remote signals or barrier semaphores. Data moves between devices by JAX's collectives and lax.ppermute only.
A program may use at most 512 MiB of HBM per device.

```python
import jax
import jax.numpy as jnp
from jax import lax

D = 768
H = 12
HD = 64
FF = 3072
LEN = 4096
BANK = 4096
NSEL = 1024
SEQS = 4


def draw_bank_rows(key, part):
    seq_keys = jax.random.split(key, SEQS)

    def one_seq(seq_key):
        key_inner, key_order = jax.random.split(seq_key)
        inner = jax.random.permutation(key_inner, BANK - 2)[:NSEL - 2].astype(jnp.int32) + 1
        full_set = jnp.concatenate([jnp.zeros((1,), jnp.int32), inner, jnp.full((1,), BANK - 1, jnp.int32)])
        order = jax.random.permutation(key_order, NSEL)
        return full_set[order]
    return jax.vmap(one_seq)(seq_keys)


def with_ends(entries, rng, smallest, top_value):
    shape = entries.shape
    spot = [jax.random.randint(jax.random.fold_in(rng, axis), (), 0, shape[axis]) for axis in range(len(shape))]
    entries = entries.at[tuple(spot)].set(smallest)
    longest = shape.index(max(shape))
    spot[longest] = (spot[longest] + 1) % shape[longest]
    return entries.at[tuple(spot)].set(top_value)


def steps_of(key, shape, shards, least, top_value):
    def one(position, parts):
        steps = jax.random.uniform(jax.random.fold_in(jax.random.fold_in(key, 6), position), (parts,), jnp.float32, least / len(shards), top_value / len(shards))
        return jnp.repeat(jnp.exp(steps), shape[position] // parts).reshape((-1,) + (1,) * (len(shape) - position - 1))

    level = one(*shards[0])
    for cut in shards[1:]:
        level = level * one(*cut)
    return level


def gaussian(own_key, extent, spread, reach, cuts=(), held_as=jnp.bfloat16):
    values = spread * jax.random.normal(own_key, extent, jnp.float32)
    if cuts:
        values = values * steps_of(own_key, extent, cuts, -0.22, 0.18)
    return jnp.clip(values, -reach, reach).astype(held_as)


def setup_inputs(seed: int = 0) -> dict:
    arg_keys = jax.random.split(jax.random.key(seed), 14)
    return {
        "x_in": gaussian(arg_keys[0], (SEQS, D, LEN), 1.0, 6.0, ((0, 2), (1, 4), (2, 4))),
        "prefix": with_ends(jax.random.randint(arg_keys[1], (SEQS,), LEN // 10, LEN // 2 + 1), jax.random.fold_in(arg_keys[1], 1), LEN // 10, (LEN // 2 + 1) - 1).astype(jnp.int32),
        "enc_bank": gaussian(arg_keys[2], (SEQS, D, BANK), 1.0, 6.0, ((0, 2), (1, 4))),
        "bank_rows": draw_bank_rows(jax.random.fold_in(arg_keys[13], 71), 0),
        "w_qkv": gaussian(arg_keys[4], (D, 3, H, HD), (D // 2) ** -0.5, 0.3125, ((0, 4), (2, 4), (3, 2))),
        "w_out": gaussian(arg_keys[5], (H, HD, D), (D // 8) ** -0.5, 0.625, ((0, 4), (1, 2), (2, 4))),
        "w_cross_q": gaussian(arg_keys[6], (D, H, HD), (D // 2) ** -0.5, 0.3125, ((0, 4), (1, 4), (2, 2))),
        "w_cross_kv": gaussian(arg_keys[7], (D, 2, H, HD), (D // 2) ** -0.5, 0.3125, ((0, 4), (2, 4), (3, 2))),
        "w_cross_out": gaussian(arg_keys[8], (H, HD, D), (D // 8) ** -0.5, 0.625, ((0, 4), (1, 2), (2, 4))),
        "w_up": gaussian(arg_keys[9], (D, FF), D ** -0.5, 0.21875, ((0, 4), (1, 8))),
        "w_down": gaussian(arg_keys[10], (FF, D), FF ** -0.5, 0.109375, ((0, 8), (1, 4))),
        "ln_gains": jnp.clip(1.0 + 0.15 * jax.random.normal(arg_keys[11], (3, D), jnp.float32), 0.25, 1.75).astype(jnp.bfloat16),
        "out_grad": gaussian(arg_keys[12], (SEQS, D, LEN), 1.0, 6.0, ((0, 2), (1, 4), (2, 4))),
    }


@jax.custom_vjp
def low(v):
    return lax.optimization_barrier(v.astype(jnp.bfloat16)).astype(jnp.float32)

@jax.custom_vjp
def low_back(v):
    return v

def low_keep(v):
    return (low(v), None)

def low_pass(kept, grad):
    return (grad,)

def back_keep(v):
    return (v, None)

def back_low(kept, grad):
    return (low(grad),)
low.defvjp(low_keep, low_pass)
low_back.defvjp(back_keep, back_low)
NORM_EPS = 1e-05
NEG_FILL = -1e+30

def matmul(left_in, right_in):
    return jnp.dot(left_in, right_in, precision=lax.Precision.HIGHEST, preferred_element_type=jnp.float32)

def layer_norm(resid_in, gain_vec):
    row_mean = lax.optimization_barrier(jnp.mean(resid_in, -1, keepdims=True))
    row_var = lax.optimization_barrier(jnp.mean(resid_in * resid_in, -1, keepdims=True)) - row_mean * row_mean
    return (resid_in - row_mean) * lax.rsqrt(row_var + NORM_EPS) * gain_vec

def attend_heads(query_in, keys_in, values_in, allowed):
    q_rows = query_in.shape[0]
    k_rows = keys_in.shape[0]
    query_h = query_in.reshape(q_rows, H, HD).transpose(1, 0, 2)
    keys_h = keys_in.reshape(k_rows, H, HD).transpose(1, 0, 2)
    values_h = values_in.reshape(k_rows, H, HD).transpose(1, 0, 2)

    def one_head(items):
        q_head, k_head, v_head = items
        raw_scores = low_back(matmul(q_head, k_head.T) * 0.125)
        raw_scores = jnp.where(allowed, raw_scores, NEG_FILL)
        probs_low = low(jax.nn.softmax(raw_scores, axis=-1))
        return matmul(probs_low, v_head)
    mixed = lax.map(jax.checkpoint(one_head), (query_h, keys_h, values_h))
    return mixed.transpose(1, 0, 2).reshape(q_rows, H * HD)

def block_fwd(x_seq, bank_seq, weights, pick_seq, allowed, cross_allowed):
    w_qkv, w_out, w_cq, w_ckv, w_cout, w_up, w_down, gains = weights
    proj = low(low_back(matmul(x_seq, w_qkv)))
    attn = low(low_back(attend_heads(proj[:, :D], proj[:, D:2 * D], proj[:, 2 * D:], allowed)))
    resid_one = x_seq + low_back(matmul(attn, w_out))
    h_one = layer_norm(resid_one, gains[0])
    cross_q = low(low_back(matmul(low(h_one), w_cq)))
    chosen = jnp.take(bank_seq, pick_seq, axis=0)
    cross_kv = low(low_back(matmul(chosen, w_ckv)))
    cross_att = low(low_back(attend_heads(cross_q, cross_kv[:, :D], cross_kv[:, D:], cross_allowed)))
    resid_two = h_one + low_back(matmul(cross_att, w_cout))
    h_two = layer_norm(resid_two, gains[1])
    upper = low_back(matmul(low(h_two), w_up))
    act = low(jax.nn.gelu(upper, approximate=False))
    resid_three = h_two + low_back(matmul(act, w_down))
    return layer_norm(resid_three, gains[2])

def reference(x_in, prefix, enc_bank, bank_rows, w_qkv, w_out, w_cross_q, w_cross_kv, w_cross_out, w_up, w_down, ln_gains, out_grad):
    f_type = jnp.float32
    weights = (w_qkv.astype(f_type).reshape(D, 3 * D), w_out.astype(f_type).reshape(D, D), w_cross_q.astype(f_type).reshape(D, D), w_cross_kv.astype(f_type).reshape(D, 2 * D), w_cross_out.astype(f_type).reshape(D, D), w_up.astype(f_type), w_down.astype(f_type), ln_gains.astype(f_type))
    positions = jnp.arange(LEN, dtype=jnp.int32)
    cross_allowed = jnp.ones((LEN, NSEL), dtype=bool)

    def per_seq(grad_total, items):
        x_seq, bank_seq, pick_seq, pre_len, cot_seq = items
        allowed = (positions[None, :] <= positions[:, None]) | (positions[None, :] < pre_len)

        def seq_fn(x_value, bank_value, weight_value):
            return block_fwd(x_value, bank_value, weight_value, pick_seq, allowed, cross_allowed)
        seq_out, pull_back = jax.vjp(seq_fn, x_seq.astype(f_type), bank_seq.astype(f_type), weights)
        grad_x, grad_bank, grad_w = pull_back(cot_seq.astype(f_type))
        grad_total = jax.tree.map(jnp.add, grad_total, grad_w)
        return (grad_total, (seq_out.astype(jnp.bfloat16), grad_x, grad_bank))
    zero_total = jax.tree.map(jnp.zeros_like, weights)
    grad_total, (outs_all, grads_x, grads_bank) = lax.scan(per_seq, zero_total, (x_in.transpose(0, 2, 1), enc_bank.transpose(0, 2, 1), bank_rows, prefix, out_grad.transpose(0, 2, 1)))
    return (outs_all.transpose(0, 2, 1), grads_x.transpose(0, 2, 1), grads_bank.transpose(0, 2, 1), grad_total[0].reshape(D, 3, H, HD), grad_total[1].reshape(H, HD, D), grad_total[2].reshape(D, H, HD), grad_total[3].reshape(D, 2, H, HD), grad_total[4].reshape(H, HD, D), grad_total[5], grad_total[6], grad_total[7])
```

```python
import functools

import jax
import jax.numpy as jnp
from jax import lax
from jax.experimental import pallas as pl
from jax.experimental.pallas import tpu as pltpu
from jax.sharding import PartitionSpec as P

bf16 = jnp.bfloat16
f32 = jnp.float32
HD = 64
HALF = 32
NORM_EPS = 1e-05
NEG = -1e30
LIMIT = 90.0
LN2 = 0.6931471805599453
LOG2E = 1.4426950408889634
KB = 512


def dot(left, right, left_dim, right_dim):
    return lax.dot_general(
        left, right, (((left_dim,), (right_dim,)), ((), ())), preferred_element_type=f32
    )


def ones_rows(count, shape, dim):
    return jnp.where(lax.broadcasted_iota(jnp.int32, shape, dim) < count, 1.0, 0.0).astype(bf16)


def allowed_block(meta, i, start, width, cols):
    k_pos = start + lax.broadcasted_iota(jnp.int32, (width, cols), 0)
    q_pos = meta[1 + i] + lax.broadcasted_iota(jnp.int32, (1, cols), 1)
    return k_pos <= jnp.maximum(q_pos, meta[0] - 1)


def block_range(meta, i, cols):
    full = jnp.maximum(meta[1 + i], meta[0]) // KB
    total = (jnp.maximum(meta[1 + i] + cols, meta[0]) + KB - 1) // KB
    return full, total


def over_keys(meta, i, cols, keys, masked, step, carry):
    if not masked:
        for start in range(0, keys, KB):
            carry = step(start, carry, False, KB)
        return carry
    full, total = block_range(meta, i, cols)
    pairs = full // 2
    carry = lax.fori_loop(0, pairs, lambda j, c: step(j * 2 * KB, c, False, 2 * KB), carry)
    carry = lax.fori_loop(2 * pairs, full, lambda j, c: step(j * KB, c, False, KB), carry)
    return lax.fori_loop(full, total, lambda j, c: step(j * KB, c, True, KB), carry)


def pieces(kv_refs, masked):
    out = []
    for ref in kv_refs:
        count = ref.shape[0]
        for b in range(count):
            out.append((ref, b))
    return out


def piece_start(meta, n_query, index, length, masked):
    if masked:
        return pl.multiple_of(meta[1 + n_query + index] * length, length)
    return index * length


def attend_kernel(*refs, sources, n_query, masked):
    meta, q_ref = refs[:2]
    kv_refs = refs[2 : 2 + sources]
    o_ref, l_ref, key_rows, val_cols = refs[2 + sources :]
    i = pl.program_id(1)
    cols = q_ref.shape[-1]
    keys = val_cols.shape[-1]

    @pl.when(i == 0)
    def _():
        key_rows[:, HD:] = ones_rows(1, (keys, 16), 1)
        val_cols[HD:, :] = ones_rows(1, (16, keys), 0)
        for index, (ref, b) in enumerate(pieces(kv_refs, masked)):
            length = ref.shape[-1]
            at = pl.ds(piece_start(meta, n_query, index, length, masked), length)
            key_rows[at, :HD] = ref[b, :, 0, 0].reshape(HD, length).T
            val_cols[:HD, at] = ref[b, :, 1, 0].reshape(HD, length)

    query = q_ref[0, :, 0].reshape(HD, cols)
    first = dot(key_rows[0:128, :HD], query, 1, 0)
    shift = jnp.max(first, axis=0, keepdims=True).astype(bf16).astype(f32)
    row = lax.broadcasted_iota(jnp.int32, (16, cols), 0)
    query_more = jnp.concatenate([query, jnp.where(row == 0, -shift, 0.0).astype(bf16)], axis=0)

    def step(start, carry, mask, width):
        top, acc = carry
        at = pl.ds(pl.multiple_of(start, KB), width)
        scores = dot(key_rows[at, :], query_more, 1, 0)
        if mask:
            scores = jnp.where(allowed_block(meta, i, start, width, cols), scores, NEG)
        top = jnp.maximum(top, jnp.max(scores, axis=0, keepdims=True))
        acc = acc + dot(val_cols[:, at], jnp.exp2(scores).astype(bf16), 1, 0)
        return top, acc

    def put(shift, acc):
        total = acc[HD : HD + 1, :]
        mixed = (acc[:HD] * (1.0 / total)).astype(bf16)
        o_ref[0, :, 0] = mixed.reshape(2, HALF, cols)
        l_ref[0, 0] = shift + jnp.log2(total)

    start = (jnp.full((1, cols), NEG, f32), jnp.zeros((HD + 16, cols), f32))
    top, acc = over_keys(meta, i, cols, keys, masked, step, start)
    put(shift, acc)

    @pl.when(jnp.max(top) > LIMIT)
    def _():
        def careful(j, carry):
            high, acc = carry
            at = pl.ds(pl.multiple_of(j * KB, KB), KB)
            scores = dot(key_rows[at, :HD], query, 1, 0)
            if masked:
                scores = jnp.where(allowed_block(meta, i, j * KB, KB, cols), scores, NEG)
            new = jnp.maximum(high, jnp.max(scores, axis=0, keepdims=True))
            part = dot(val_cols[:, at], jnp.exp2(scores - new).astype(bf16), 1, 0)
            return new, acc * jnp.exp2(high - new) + part

        total = block_range(meta, i, cols)[1] if masked else keys // KB
        put(*lax.fori_loop(0, total, careful, start))


def attend_back_kernel(*refs, sources, n_query, masked):
    meta, q_ref = refs[:2]
    kv_refs = refs[2 : 2 + sources]
    g_ref, o_ref, l_ref = refs[2 + sources : 5 + sources]
    dq_ref = refs[5 + sources]
    dkv_refs = refs[6 + sources : 6 + 2 * sources]
    key_rows, val_rows, key_cols, dk_acc, dv_acc = refs[6 + 2 * sources :]
    i = pl.program_id(1)
    cols = q_ref.shape[-1]
    keys = key_cols.shape[-1]

    @pl.when(i == 0)
    def _():
        key_rows[:, HD:] = ones_rows(3, (keys, 16), 1)
        val_rows[:, HD:] = ones_rows(3, (keys, 16), 1)
        for index, (ref, b) in enumerate(pieces(kv_refs, masked)):
            length = ref.shape[-1]
            at = pl.ds(piece_start(meta, n_query, index, length, masked), length)
            k_part = ref[b, :, 0, 0].reshape(HD, length)
            key_cols[:, at] = k_part
            key_rows[at, :HD] = k_part.T
            val_rows[at, :HD] = ref[b, :, 1, 0].reshape(HD, length).T
        dk_acc[...] = jnp.zeros_like(dk_acc)
        dv_acc[...] = jnp.zeros_like(dv_acc)

    query = q_ref[0, :, 0].reshape(HD, cols)
    grad = g_ref[0, :, 0].reshape(HD, cols)
    delta = jnp.sum(
        grad.astype(f32) * o_ref[0, :, 0].reshape(HD, cols).astype(f32), axis=0, keepdims=True
    )

    def with_shift(value, shift):
        high = shift.astype(bf16).astype(f32)
        mid = (shift - high).astype(bf16).astype(f32)
        low = shift - high - mid
        row = lax.broadcasted_iota(jnp.int32, (16, cols), 0)
        more = jnp.where(row == 0, -high, jnp.where(row == 1, -mid, jnp.where(row == 2, -low, 0.0)))
        return jnp.concatenate([value, more.astype(bf16)], axis=0)

    query_more = with_shift(query, l_ref[0, 0])
    grad_more = with_shift(grad, delta)

    def step(start, dq, mask, width):
        at = pl.ds(pl.multiple_of(start, KB), width)
        scores = dot(key_rows[at, :], query_more, 1, 0)
        if mask:
            scores = jnp.where(allowed_block(meta, i, start, width, cols), scores, NEG)
        probs = jnp.exp2(scores)
        grad_scores = (probs * dot(val_rows[at, :], grad_more, 1, 0)).astype(bf16)
        dv_acc[:, at] += dot(grad, probs.astype(bf16), 1, 1)
        dk_acc[:, at] += dot(query, grad_scores, 1, 1)
        return dq + dot(key_cols[:, at], grad_scores, 1, 0)

    dq = over_keys(meta, i, cols, keys, masked, step, jnp.zeros((HD, cols), f32))
    dq_ref[0, :, 0] = (dq * 0.125).astype(bf16).reshape(2, HALF, cols)

    @pl.when(i == n_query - 1)
    def _():
        for index, (ref, b) in enumerate(pieces(dkv_refs, masked)):
            length = ref.shape[-1]
            at = pl.ds(piece_start(meta, n_query, index, length, masked), length)
            ref[b, :, 0, 0] = (dk_acc[:, at] * LN2).astype(ref.dtype).reshape(2, HALF, length)
            ref[b, :, 1, 0] = dv_acc[:, at].astype(ref.dtype).reshape(2, HALF, length)


def attention_specs(query, kv_list, masked):
    cols = query.shape[-1]
    if masked:
        n_query, _, heads = query.shape[:3]
        grid = (heads, n_query)
        q_spec = pl.BlockSpec((1, 2, 1, HALF, cols), lambda h, i, m: (i, 0, h, 0, 0))
        kv_specs = [
            pl.BlockSpec(kv.shape[:3] + (1,) + kv.shape[4:], lambda h, i, m: (0, 0, 0, h, 0, 0))
            for kv in kv_list
        ]
        l_spec = pl.BlockSpec((1, 1, 1, cols), lambda h, i, m: (h, i, 0, 0))
        l_shape = (heads, n_query, 1, cols)
        keys = sum(kv.shape[0] * kv.shape[-1] for kv in kv_list)
    else:
        n_query = 1
        _, _, rows, heads = query.shape[:4]
        grid = (rows * heads, 1)
        q_spec = pl.BlockSpec(
            (1, 2, None, 1, HALF, cols), lambda g, i, m: (0, 0, g // heads, g % heads, 0, 0)
        )
        kv_specs = [
            pl.BlockSpec(
                (kv.shape[0], 2, None, 2, 1) + kv.shape[5:],
                lambda g, i, m: (0, 0, g // heads, 0, g % heads, 0, 0),
            )
            for kv in kv_list
        ]
        l_spec = pl.BlockSpec((1, 1, 1, cols), lambda g, i, m: (g, 0, 0, 0))
        l_shape = (rows * heads, 1, 1, cols)
        keys = sum(kv.shape[0] * kv.shape[-1] for kv in kv_list)
    return n_query, grid, q_spec, kv_specs, l_spec, l_shape, keys


def cost(query, keys, dots):
    pairs = query.size // HD * keys
    return pl.CostEstimate(
        flops=2 * pairs * 256 * dots // 2, bytes_accessed=query.size * 16, transcendentals=pairs
    )


def attend(meta, query, kv_list, masked, name):
    n_query, grid, q_spec, kv_specs, l_spec, l_shape, keys = attention_specs(query, kv_list, masked)
    return pl.pallas_call(
        functools.partial(attend_kernel, sources=len(kv_list), n_query=n_query, masked=masked),
        grid_spec=pltpu.PrefetchScalarGridSpec(
            num_scalar_prefetch=1,
            grid=grid,
            in_specs=[q_spec] + kv_specs,
            out_specs=[q_spec, l_spec],
            scratch_shapes=[pltpu.VMEM((keys, HD + 16), bf16), pltpu.VMEM((HD + 16, keys), bf16)],
        ),
        out_shape=[
            jax.ShapeDtypeStruct(query.shape, bf16),
            jax.ShapeDtypeStruct(l_shape, f32),
        ],
        compiler_params=pltpu.CompilerParams(vmem_limit_bytes=48 << 20),
        cost_estimate=cost(query, keys, 2),
        name=name,
    )(meta, query, *kv_list)


def attend_back(meta, query, kv_list, grad, out, lse, masked, types, name):
    n_query, grid, q_spec, kv_specs, l_spec, l_shape, keys = attention_specs(query, kv_list, masked)
    return pl.pallas_call(
        functools.partial(attend_back_kernel, sources=len(kv_list), n_query=n_query, masked=masked),
        grid_spec=pltpu.PrefetchScalarGridSpec(
            num_scalar_prefetch=1,
            grid=grid,
            in_specs=[q_spec] + kv_specs + [q_spec, q_spec, l_spec],
            out_specs=[q_spec] + kv_specs,
            scratch_shapes=[
                pltpu.VMEM((keys, HD + 16), bf16),
                pltpu.VMEM((keys, HD + 16), bf16),
                pltpu.VMEM((HD, keys), bf16),
                pltpu.VMEM((HD, keys), f32),
                pltpu.VMEM((HD, keys), f32),
            ],
        ),
        out_shape=[jax.ShapeDtypeStruct(query.shape, bf16)]
        + [jax.ShapeDtypeStruct(kv.shape, t) for kv, t in zip(kv_list, types)],
        compiler_params=pltpu.CompilerParams(vmem_limit_bytes=48 << 20),
        cost_estimate=cost(query, keys, 5),
        name=name,
    )(meta, query, *kv_list, grad, out, lse)


def norm_stats(resid, width):
    mean = jnp.sum(resid, -1, keepdims=True) / width
    square = jnp.sum(resid * resid, -1, keepdims=True) / width
    inv_std = lax.rsqrt(square - mean * mean + NORM_EPS)
    return (resid - mean) * inv_std, inv_std


def norm_back(grad, gain, normed, inv_std, width):
    scaled = grad * gain
    total = jnp.sum(scaled, -1, keepdims=True) / width
    cross = jnp.sum(scaled * normed, -1, keepdims=True) / width
    return inv_std * (scaled - total - normed * cross), jnp.sum(grad * normed, axis=0)


def mm(spec, left, right):
    return jnp.einsum(spec, left, right, preferred_element_type=f32)


def per_device(
    x_in,
    prefix,
    enc_bank,
    bank_rows,
    w_qkv,
    w_out,
    w_cross_q,
    w_cross_kv,
    w_cross_out,
    w_up,
    w_down,
    ln_gains,
    out_grad,
):
    dp, rows, cols = lax.axis_size("dp"), lax.axis_size("row"), lax.axis_size("col")
    d_pos, r_pos, c_pos = lax.axis_index("dp"), lax.axis_index("row"), lax.axis_index("col")
    own_seqs, part_width, row_len = x_in.shape
    seqs = own_seqs * dp
    sub = cols // seqs
    parts = dp * sub
    width = part_width * cols
    tokens = row_len // parts
    heads = w_qkv.shape[2]
    feat = heads * HALF
    units = w_up.shape[1]
    length = row_len * rows
    odd = (r_pos % 2) == 1
    seq_pos = c_pos // sub
    part_pos = d_pos * sub + c_pos % sub
    groups = [[s * sub + k for k in range(sub)] for s in range(seqs)]
    everywhere = ("dp", "row", "col")

    def to_tokens(value):
        take = value.shape[-1] // parts
        value = value.reshape(own_seqs, part_width, parts, take)
        value = jnp.where(odd, value[:, :, ::-1], value)
        value = value.reshape(own_seqs, part_width, dp, sub, take)
        value = lax.all_to_all(value, "dp", 2, 0, tiled=True)
        value = value.reshape(seqs, part_width, sub, take).transpose(0, 2, 1, 3)
        value = lax.all_to_all(value.reshape(cols, part_width, take), "col", 0, 1, tiled=True)
        return value.reshape(width, take)

    def to_home(value):
        take = value.shape[-1]
        value = lax.all_to_all(value.reshape(1, width, take), "col", 1, 0, tiled=True)
        value = value.reshape(seqs, sub, part_width, take).transpose(0, 2, 1, 3)
        value = value.reshape(seqs, part_width, 1, sub, take)
        value = lax.all_to_all(value, "dp", 0, 2, tiled=True)
        value = value.reshape(own_seqs, part_width, parts, take)
        value = jnp.where(odd, value[:, :, ::-1], value)
        return value.reshape(own_seqs, part_width, parts * take)

    qkv_near = lax.all_gather(w_qkv.reshape(part_width, 3 * feat), ("dp", "col"), axis=0)
    x_own = to_tokens(x_in)
    x_rows = lax.all_gather(x_own, "row", axis=0)
    small = jnp.concatenate(
        [
            w_cross_kv.reshape(part_width, 2 * feat),
            w_out.reshape(feat, part_width).T,
            w_cross_q.reshape(part_width, feat),
            w_cross_out.reshape(feat, part_width).T,
        ],
        axis=1,
    )
    small_all = lax.all_gather(small, everywhere, axis=0)
    small_all = small_all.reshape(dp, rows, cols, part_width, 5 * feat)
    large_all = lax.all_gather(jnp.stack([w_up, w_down.T]), everywhere, axis=0)
    large_all = large_all.reshape(dp, rows, cols, 2, part_width, units)
    qkv_all = lax.all_gather(qkv_near, "row", axis=0)

    def standard(first, count):
        piece = small_all[..., first * feat : (first + count) * feat]
        return piece.transpose(2, 3, 0, 1, 4).reshape(width, dp * rows * count * feat)

    wt_ckv = standard(0, 2)
    wt_out_t = standard(1 + 1, 1).reshape(width, dp, rows, feat).transpose(0, 2, 1, 3)
    wt_out_t = wt_out_t.reshape(width, width)
    wt_cq = standard(3, 1)
    wt_cout_t = standard(4, 1)
    wt_up, wt_down_t = (
        large_all[:, :, :, j].transpose(2, 3, 0, 1, 4).reshape(width, dp * rows * units)
        for j in range(2)
    )

    gains_all = lax.all_gather(ln_gains.astype(f32), "col", axis=1, tiled=True)

    near = qkv_near.reshape(dp, width, 3 * feat)
    proj = mm("dwf,rwt->rdft", near, x_rows)
    proj = proj.reshape(rows, dp, 3, heads, HALF, tokens)
    query = (proj[:, :, 0] * (0.125 * LOG2E)).astype(bf16)
    kv_own = proj[:, :, 1:].astype(bf16)

    def index_of(row, part):
        return jnp.where(row % 2 == 1, parts - 1 - part, part) + row * parts

    row_ids = jnp.arange(rows, dtype=jnp.int32)
    if sub == 1:
        kv_list = [kv_own, lax.ppermute(kv_own, "dp", [(0, 1), (1, 0)])]
        owners = [part_pos, 1 - part_pos]
    else:
        kv_all = lax.all_gather(kv_own, "col", axis=0, axis_index_groups=groups)
        kv_all = lax.all_gather(kv_all, "dp", axis=0).reshape((parts,) + kv_own.shape)
        kv_list = [kv_all[j] for j in range(parts)]
        owners = list(range(parts))
    q_start = index_of(row_ids, part_pos) * tokens
    places = [index_of(row_ids, owner) for owner in owners]
    seq_prefix = lax.all_gather(prefix, "dp", axis=0, tiled=True)[seq_pos]
    meta = jnp.concatenate([seq_prefix[None], q_start] + places).astype(jnp.int32)
    mixed, lse = attend(meta, query, kv_list, True, "self_attention")
    attn = lax.all_to_all(mixed, "row", 0, 0, tiled=True)
    attn_flat = attn.reshape(width, tokens)

    resid_one = x_own.T.astype(f32) + mm("ft,wf->tw", attn_flat, wt_out_t)
    normed_one, inv_one = norm_stats(resid_one, width)
    h_one = normed_one * gains_all[0]
    h_one_low = h_one.astype(bf16)

    picked = bank_rows.shape[1] // rows
    row_pick = lax.dynamic_slice_in_dim(bank_rows, r_pos * picked, picked, 1)
    bank_ids = jnp.arange(enc_bank.shape[2], dtype=jnp.int32)
    hot = (bank_ids[None, :, None] == row_pick[:, None, :]).astype(bf16)
    chosen = to_tokens(mm("swn,snp->swp", enc_bank, hot).astype(bf16))
    c_tokens = chosen.shape[1]
    ckv_own = mm("wf,wt->ft", wt_ckv, chosen).astype(bf16)
    ckv_own = ckv_own.reshape(dp, rows, 2, heads, HALF, c_tokens)
    if sub > 1:
        ckv_all = lax.all_gather(ckv_own, "col", axis=0, axis_index_groups=groups)
    else:
        ckv_all = ckv_own
    ckv_all = lax.all_gather(ckv_all, ("dp", "row"), axis=0)
    ckv_all = ckv_all.reshape((dp * rows * sub,) + ckv_own.shape)
    cross_q = (mm("wf,tw->ft", wt_cq, h_one_low) * (0.125 * LOG2E)).astype(bf16)
    cross_q = cross_q.reshape(1, dp, rows, heads, HALF, tokens)
    catt, lse_cross = attend(meta, cross_q, [ckv_all], False, "cross_attention")
    catt_flat = catt.reshape(width, tokens)
    resid_two = h_one + mm("ft,wf->tw", catt_flat, wt_cout_t)
    normed_two, inv_two = norm_stats(resid_two, width)
    h_two = normed_two * gains_all[1]
    h_two_low = h_two.astype(bf16)

    upper = mm("tw,wf->tf", h_two_low, wt_up)
    cdf = 0.5 * (1.0 + lax.erf(upper * 0.7071067811865476))
    act = (upper * cdf).astype(bf16)
    slope = (cdf + upper * (jnp.exp(-0.5 * upper * upper) * 0.3989422804014327)).astype(bf16)
    resid_three = h_two + mm("tf,wf->tw", act, wt_down_t)
    normed_three, inv_three = norm_stats(resid_three, width)
    block_out = to_home((normed_three * gains_all[2]).astype(bf16).T)

    cot = to_tokens(out_grad).T.astype(f32)
    dy_three, dg_three = norm_back(cot, gains_all[2], normed_three, inv_three, width)
    d_ffn = dy_three.astype(bf16)
    g_down_t = mm("tw,tf->wf", d_ffn, act)
    d_upper = (mm("tw,wf->tf", d_ffn, wt_down_t) * slope.astype(f32)).astype(bf16)
    g_up = mm("tw,tf->wf", h_two_low, d_upper)
    dh_two = dy_three + mm("tf,wf->tw", d_upper, wt_up)
    dy_two, dg_two = norm_back(dh_two, gains_all[1], normed_two, inv_two, width)
    d_cross = dy_two.astype(bf16)
    g_cout_t = mm("tw,ft->wf", d_cross, catt_flat)
    d_catt = mm("wf,tw->ft", wt_cout_t, d_cross).astype(bf16).reshape(catt.shape)
    d_cq, d_ckv = attend_back(
        meta, cross_q, [ckv_all], d_catt, catt, lse_cross, False, [bf16], "cross_attention_back"
    )
    d_cq = d_cq.reshape(width, tokens)
    if sub > 1:
        d_ckv = d_ckv.reshape(dp, rows, sub, -1)
        d_ckv = lax.psum_scatter(d_ckv, "dp", scatter_dimension=0, tiled=True)
        d_ckv = lax.psum_scatter(d_ckv, "row", scatter_dimension=1, tiled=True)
        d_ckv = lax.psum_scatter(
            d_ckv, "col", scatter_dimension=2, tiled=True, axis_index_groups=groups
        )
    else:
        d_ckv = lax.psum_scatter(d_ckv, ("dp", "row"), scatter_dimension=0, tiled=True)
    d_ckv = d_ckv.reshape(2 * width, c_tokens)
    dh_one = dy_two + mm("ft,wf->tw", d_cq, wt_cq)
    dy_one, dg_one = norm_back(dh_one, gains_all[0], normed_one, inv_one, width)
    d_attn_out = dy_one.astype(bf16)
    d_attn = mm("wf,tw->ft", wt_out_t, d_attn_out).astype(bf16).reshape(attn.shape)
    d_mixed = lax.all_to_all(d_attn, "row", 0, 0, tiled=True)
    g_cq = mm("tw,ft->wf", h_one_low, d_cq)
    g_out_t = mm("tw,ft->wf", d_attn_out, attn_flat)
    g_out_t = g_out_t.reshape(width, rows, dp, feat).transpose(0, 2, 1, 3).reshape(width, width)
    g_ckv = mm("wt,ft->wf", chosen, d_ckv)
    d_chosen = mm("wf,ft->wt", wt_ckv, d_ckv).astype(bf16)

    d_chosen = lax.all_gather(to_home(d_chosen), "row", axis=2, tiled=True)
    hot_all = (bank_rows[:, :, None] == bank_ids[None, None, :]).astype(bf16)
    bank_grad = mm("swp,spn->swn", d_chosen, hot_all)

    types = [f32] + [bf16] * (len(kv_list) - 1) if sub == 1 else [bf16] * len(kv_list)
    d_query, *d_kv = attend_back(
        meta, query, kv_list, d_mixed, mixed, lse, True, types, "self_attention_back"
    )
    if sub == 1:
        d_kv = d_kv[0] + lax.ppermute(d_kv[1], "dp", [(0, 1), (1, 0)]).astype(f32)
    else:
        d_kv = jnp.stack(d_kv).reshape((dp, sub) + kv_own.shape)
        d_kv = lax.psum_scatter(d_kv, "dp", scatter_dimension=0, tiled=True)
        d_kv = lax.psum_scatter(
            d_kv, "col", scatter_dimension=1, tiled=True, axis_index_groups=groups
        )
    d_kv = d_kv.reshape(kv_own.shape).astype(bf16)
    d_proj = jnp.concatenate([d_query[:, :, None], d_kv], axis=2)
    d_proj = d_proj.reshape(rows, dp, 3 * feat, tokens)
    g_qkv = mm("rwt,rdft->dwf", x_rows, d_proj)
    d_mine = lax.all_to_all(d_proj, "row", 0, 0, tiled=True)
    wt_qkv = qkv_all.reshape(rows, dp, width, 3 * feat)
    dx = dy_one + mm("rdft,rdwf->tw", d_mine, wt_qkv)
    x_grad = to_home(dx.astype(bf16).T).astype(f32)

    def shares(value, count):
        value = value.astype(bf16).reshape(cols, part_width, dp, rows, count)
        return value.transpose(2, 3, 0, 1, 4)

    def scatter(value):
        value = lax.psum_scatter(value, "dp", scatter_dimension=0, tiled=False)
        value = lax.psum_scatter(value, "row", scatter_dimension=0, tiled=False)
        return lax.psum_scatter(value, "col", scatter_dimension=0, tiled=False)

    big = scatter(jnp.stack([shares(g_up, units), shares(g_down_t, units)], axis=3)).astype(f32)
    rest = scatter(
        jnp.concatenate(
            [shares(g_ckv, 2 * feat), shares(g_out_t, feat), shares(g_cq, feat), shares(g_cout_t, feat)],
            axis=-1,
        )
    ).astype(f32)
    qkv_grad = g_qkv.astype(bf16).reshape(dp, cols, part_width, 3 * feat)
    qkv_grad = lax.psum_scatter(qkv_grad, "dp", scatter_dimension=0, tiled=False)
    qkv_grad = lax.psum_scatter(qkv_grad, "col", scatter_dimension=0, tiled=False).astype(f32)
    gain_grads = lax.psum(jnp.stack([dg_one, dg_two, dg_three]), everywhere)
    gain_grads = lax.dynamic_slice_in_dim(gain_grads, c_pos * part_width, part_width, 1)

    return (
        block_out,
        x_grad,
        bank_grad,
        qkv_grad.reshape(w_qkv.shape),
        rest[:, 2 * feat : 3 * feat].T.reshape(w_out.shape),
        rest[:, 3 * feat : 4 * feat].reshape(w_cross_q.shape),
        rest[:, : 2 * feat].reshape(w_cross_kv.shape),
        rest[:, 4 * feat :].T.reshape(w_cross_out.shape),
        big[0],
        big[1].T,
        gain_grads,
    )


def solution(mesh):
    placed = (
        P("dp", "col", "row"),
        P("dp"),
        P("dp", "col", None),
        P("dp", None),
        P("col", None, "row", "dp"),
        P("row", "dp", "col"),
        P("col", "row", "dp"),
        P("col", None, "row", "dp"),
        P("row", "dp", "col"),
        P("col", ("dp", "row")),
        P(("dp", "row"), "col"),
        P(None, "col"),
        P("dp", "col", "row"),
    )
    return jax.shard_map(
        per_device,
        mesh=mesh,
        in_specs=placed,
        out_specs=(
            P("dp", "col", "row"),
            P("dp", "col", "row"),
            P("dp", "col", None),
            P("col", None, "row", "dp"),
            P("row", "dp", "col"),
            P("col", "row", "dp"),
            P("col", None, "row", "dp"),
            P("row", "dp", "col"),
            P("col", ("dp", "row")),
            P(("dp", "row"), "col"),
            P(None, "col"),
        ),
        check_vma=False,
    )
```

```python
import functools

import jax
import jax.numpy as jnp
from jax import lax
from jax.experimental import pallas as pl
from jax.experimental.pallas import tpu as pltpu
from jax.sharding import PartitionSpec as P

bf16 = jnp.bfloat16
f32 = jnp.float32
HD = 64
HALF = 32
NORM_EPS = 1e-05
NEG = -1e30
LIMIT = 90.0
LN2 = 0.6931471805599453
LOG2E = 1.4426950408889634
KB = 512


def dot(left, right, left_dim, right_dim):
    return lax.dot_general(
        left, right, (((left_dim,), (right_dim,)), ((), ())), preferred_element_type=f32
    )


def ones_rows(count, shape, dim):
    return jnp.where(lax.broadcasted_iota(jnp.int32, shape, dim) < count, 1.0, 0.0).astype(bf16)


def allowed_block(meta, i, start, width, cols):
    k_pos = start + lax.broadcasted_iota(jnp.int32, (width, cols), 0)
    q_pos = meta[1 + i] + lax.broadcasted_iota(jnp.int32, (1, cols), 1)
    return k_pos <= jnp.maximum(q_pos, meta[0] - 1)


def block_range(meta, i, cols):
    full = jnp.maximum(meta[1 + i], meta[0]) // KB
    total = (jnp.maximum(meta[1 + i] + cols, meta[0]) + KB - 1) // KB
    return full, total


def over_keys(meta, i, cols, keys, masked, step, carry):
    if not masked:
        for start in range(0, keys, KB):
            carry = step(start, carry, False, KB)
        return carry
    full, total = block_range(meta, i, cols)
    pairs = full // 2
    carry = lax.fori_loop(0, pairs, lambda j, c: step(j * 2 * KB, c, False, 2 * KB), carry)
    carry = lax.fori_loop(2 * pairs, full, lambda j, c: step(j * KB, c, False, KB), carry)
    return lax.fori_loop(full, total, lambda j, c: step(j * KB, c, True, KB), carry)


def pieces(kv_refs, masked):
    out = []
    for ref in kv_refs:
        count = ref.shape[0]
        for b in range(count):
            out.append((ref, b))
    return out


def piece_start(meta, n_query, index, length, masked):
    if masked:
        return pl.multiple_of(meta[1 + n_query + index] * length, length)
    return index * length


def attend_kernel(*refs, sources, n_query, masked):
    meta, q_ref = refs[:2]
    kv_refs = refs[2 : 2 + sources]
    o_ref, l_ref, key_rows, val_cols = refs[2 + sources :]
    i = pl.program_id(1)
    cols = q_ref.shape[-1]
    keys = val_cols.shape[-1]

    @pl.when(i == 0)
    def _():
        key_rows[:, HD:] = ones_rows(1, (keys, 16), 1)
        val_cols[HD:, :] = ones_rows(1, (16, keys), 0)
        for index, (ref, b) in enumerate(pieces(kv_refs, masked)):
            length = ref.shape[-1]
            at = pl.ds(piece_start(meta, n_query, index, length, masked), length)
            key_rows[at, :HD] = ref[b, :, 0, 0].reshape(HD, length).T
            val_cols[:HD, at] = ref[b, :, 1, 0].reshape(HD, length)

    query = q_ref[0, :, 0].reshape(HD, cols)
    first = dot(key_rows[0:128, :HD], query, 1, 0)
    shift = jnp.max(first, axis=0, keepdims=True).astype(bf16).astype(f32)
    row = lax.broadcasted_iota(jnp.int32, (16, cols), 0)
    query_more = jnp.concatenate([query, jnp.where(row == 0, -shift, 0.0).astype(bf16)], axis=0)

    def step(start, carry, mask, width):
        top, acc = carry
        at = pl.ds(pl.multiple_of(start, KB), width)
        scores = dot(key_rows[at, :], query_more, 1, 0)
        if mask:
            scores = jnp.where(allowed_block(meta, i, start, width, cols), scores, NEG)
        top = jnp.maximum(top, jnp.max(scores, axis=0, keepdims=True))
        acc = acc + dot(val_cols[:, at], jnp.exp2(scores).astype(bf16), 1, 0)
        return top, acc

    def put(shift, acc):
        total = acc[HD : HD + 1, :]
        mixed = (acc[:HD] * (1.0 / total)).astype(bf16)
        o_ref[0, :, 0] = mixed.reshape(2, HALF, cols)
        l_ref[0, 0] = shift + jnp.log2(total)

    start = (jnp.full((1, cols), NEG, f32), jnp.zeros((HD + 16, cols), f32))
    top, acc = over_keys(meta, i, cols, keys, masked, step, start)
    put(shift, acc)

    @pl.when(jnp.max(top) > LIMIT)
    def _():
        def careful(j, carry):
            high, acc = carry
            at = pl.ds(pl.multiple_of(j * KB, KB), KB)
            scores = dot(key_rows[at, :HD], query, 1, 0)
            if masked:
                scores = jnp.where(allowed_block(meta, i, j * KB, KB, cols), scores, NEG)
            new = jnp.maximum(high, jnp.max(scores, axis=0, keepdims=True))
            part = dot(val_cols[:, at], jnp.exp2(scores - new).astype(bf16), 1, 0)
            return new, acc * jnp.exp2(high - new) + part

        total = block_range(meta, i, cols)[1] if masked else keys // KB
        put(*lax.fori_loop(0, total, careful, start))


def attend_back_kernel(*refs, sources, n_query, masked):
    meta, q_ref = refs[:2]
    kv_refs = refs[2 : 2 + sources]
    g_ref, o_ref, l_ref = refs[2 + sources : 5 + sources]
    dq_ref = refs[5 + sources]
    dkv_refs = refs[6 + sources : 6 + 2 * sources]
    key_rows, val_rows, key_cols, dk_acc, dv_acc = refs[6 + 2 * sources :]
    i = pl.program_id(1)
    cols = q_ref.shape[-1]
    keys = key_cols.shape[-1]

    @pl.when(i == 0)
    def _():
        key_rows[:, HD:] = ones_rows(3, (keys, 16), 1)
        val_rows[:, HD:] = ones_rows(3, (keys, 16), 1)
        for index, (ref, b) in enumerate(pieces(kv_refs, masked)):
            length = ref.shape[-1]
            at = pl.ds(piece_start(meta, n_query, index, length, masked), length)
            k_part = ref[b, :, 0, 0].reshape(HD, length)
            key_cols[:, at] = k_part
            key_rows[at, :HD] = k_part.T
            val_rows[at, :HD] = ref[b, :, 1, 0].reshape(HD, length).T
        dk_acc[...] = jnp.zeros_like(dk_acc)
        dv_acc[...] = jnp.zeros_like(dv_acc)

    query = q_ref[0, :, 0].reshape(HD, cols)
    grad = g_ref[0, :, 0].reshape(HD, cols)
    delta = jnp.sum(
        grad.astype(f32) * o_ref[0, :, 0].reshape(HD, cols).astype(f32), axis=0, keepdims=True
    )

    def with_shift(value, shift):
        high = shift.astype(bf16).astype(f32)
        mid = (shift - high).astype(bf16).astype(f32)
        low = shift - high - mid
        row = lax.broadcasted_iota(jnp.int32, (16, cols), 0)
        more = jnp.where(row == 0, -high, jnp.where(row == 1, -mid, jnp.where(row == 2, -low, 0.0)))
        return jnp.concatenate([value, more.astype(bf16)], axis=0)

    query_more = with_shift(query, l_ref[0, 0])
    grad_more = with_shift(grad, delta)

    def step(start, dq, mask, width):
        at = pl.ds(pl.multiple_of(start, KB), width)
        scores = dot(key_rows[at, :], query_more, 1, 0)
        if mask:
            scores = jnp.where(allowed_block(meta, i, start, width, cols), scores, NEG)
        probs = jnp.exp2(scores)
        grad_scores = (probs * dot(val_rows[at, :], grad_more, 1, 0)).astype(bf16)
        dv_acc[:, at] += dot(grad, probs.astype(bf16), 1, 1)
        dk_acc[:, at] += dot(query, grad_scores, 1, 1)
        return dq + dot(key_cols[:, at], grad_scores, 1, 0)

    dq = over_keys(meta, i, cols, keys, masked, step, jnp.zeros((HD, cols), f32))
    dq_ref[0, :, 0] = (dq * 0.125).astype(bf16).reshape(2, HALF, cols)

    @pl.when(i == n_query - 1)
    def _():
        for index, (ref, b) in enumerate(pieces(dkv_refs, masked)):
            length = ref.shape[-1]
            at = pl.ds(piece_start(meta, n_query, index, length, masked), length)
            ref[b, :, 0, 0] = (dk_acc[:, at] * LN2).astype(ref.dtype).reshape(2, HALF, length)
            ref[b, :, 1, 0] = dv_acc[:, at].astype(ref.dtype).reshape(2, HALF, length)


def attention_specs(query, kv_list, masked):
    cols = query.shape[-1]
    if masked:
        n_query, _, heads = query.shape[:3]
        grid = (heads, n_query)
        q_spec = pl.BlockSpec((1, 2, 1, HALF, cols), lambda h, i, m: (i, 0, h, 0, 0))
        kv_specs = [
            pl.BlockSpec(kv.shape[:3] + (1,) + kv.shape[4:], lambda h, i, m: (0, 0, 0, h, 0, 0))
            for kv in kv_list
        ]
        l_spec = pl.BlockSpec((1, 1, 1, cols), lambda h, i, m: (h, i, 0, 0))
        l_shape = (heads, n_query, 1, cols)
        keys = sum(kv.shape[0] * kv.shape[-1] for kv in kv_list)
    else:
        n_query = 1
        _, _, rows, heads = query.shape[:4]
        grid = (rows * heads, 1)
        q_spec = pl.BlockSpec(
            (1, 2, None, 1, HALF, cols), lambda g, i, m: (0, 0, g // heads, g % heads, 0, 0)
        )
        kv_specs = [
            pl.BlockSpec(
                (kv.shape[0], 2, None, 2, 1) + kv.shape[5:],
                lambda g, i, m: (0, 0, g // heads, 0, g % heads, 0, 0),
            )
            for kv in kv_list
        ]
        l_spec = pl.BlockSpec((1, 1, 1, cols), lambda g, i, m: (g, 0, 0, 0))
        l_shape = (rows * heads, 1, 1, cols)
        keys = sum(kv.shape[0] * kv.shape[-1] for kv in kv_list)
    return n_query, grid, q_spec, kv_specs, l_spec, l_shape, keys


def cost(query, keys, dots):
    pairs = query.size // HD * keys
    return pl.CostEstimate(
        flops=2 * pairs * 256 * dots // 2, bytes_accessed=query.size * 16, transcendentals=pairs
    )


def attend(meta, query, kv_list, masked, name):
    n_query, grid, q_spec, kv_specs, l_spec, l_shape, keys = attention_specs(query, kv_list, masked)
    return pl.pallas_call(
        functools.partial(attend_kernel, sources=len(kv_list), n_query=n_query, masked=masked),
        grid_spec=pltpu.PrefetchScalarGridSpec(
            num_scalar_prefetch=1,
            grid=grid,
            in_specs=[q_spec] + kv_specs,
            out_specs=[q_spec, l_spec],
            scratch_shapes=[pltpu.VMEM((keys, HD + 16), bf16), pltpu.VMEM((HD + 16, keys), bf16)],
        ),
        out_shape=[
            jax.ShapeDtypeStruct(query.shape, bf16),
            jax.ShapeDtypeStruct(l_shape, f32),
        ],
        compiler_params=pltpu.CompilerParams(vmem_limit_bytes=48 << 20),
        cost_estimate=cost(query, keys, 2),
        name=name,
    )(meta, query, *kv_list)


def attend_back(meta, query, kv_list, grad, out, lse, masked, types, name):
    n_query, grid, q_spec, kv_specs, l_spec, l_shape, keys = attention_specs(query, kv_list, masked)
    return pl.pallas_call(
        functools.partial(attend_back_kernel, sources=len(kv_list), n_query=n_query, masked=masked),
        grid_spec=pltpu.PrefetchScalarGridSpec(
            num_scalar_prefetch=1,
            grid=grid,
            in_specs=[q_spec] + kv_specs + [q_spec, q_spec, l_spec],
            out_specs=[q_spec] + kv_specs,
            scratch_shapes=[
                pltpu.VMEM((keys, HD + 16), bf16),
                pltpu.VMEM((keys, HD + 16), bf16),
                pltpu.VMEM((HD, keys), bf16),
                pltpu.VMEM((HD, keys), f32),
                pltpu.VMEM((HD, keys), f32),
            ],
        ),
        out_shape=[jax.ShapeDtypeStruct(query.shape, bf16)]
        + [jax.ShapeDtypeStruct(kv.shape, t) for kv, t in zip(kv_list, types)],
        compiler_params=pltpu.CompilerParams(vmem_limit_bytes=48 << 20),
        cost_estimate=cost(query, keys, 5),
        name=name,
    )(meta, query, *kv_list, grad, out, lse)


def kernel_params():
    return pltpu.CompilerParams(vmem_limit_bytes=60 << 20)


def whole(value):
    return pl.BlockSpec(value.shape, lambda *i: (0,) * value.ndim)


def by_columns(count, body):
    step = min(128, count)

    def one(j, carry):
        body(pl.ds(pl.multiple_of(j * step, step), step))
        return carry

    lax.fori_loop(0, count // step, one, 0)


def norm_stats(resid):
    width = resid.shape[0]
    mean = jnp.sum(resid, 0, keepdims=True) / width
    square = jnp.sum(resid * resid, 0, keepdims=True) / width
    inv_std = lax.rsqrt(square - mean * mean + NORM_EPS)
    return (resid - mean) * inv_std, inv_std


def norm_back(grad, gain, normed, inv_std):
    width = grad.shape[0]
    scaled = grad * gain
    total = jnp.sum(scaled, 0, keepdims=True) / width
    cross = jnp.sum(scaled * normed, 0, keepdims=True) / width
    return inv_std * (scaled - total - normed * cross)


def project_kernel(near_ref, x_ref, q_ref, kv_ref, near_t):
    feat = q_ref.shape[2]

    @pl.when(pl.program_id(0) == 0)
    def _():
        for d in range(near_ref.shape[0]):
            near_t[d] = near_ref[d].T

    for d in range(near_ref.shape[0]):
        proj = dot(near_t[d], x_ref[0], 1, 0)
        q_ref[0, d] = (proj[:feat] * (0.125 * LOG2E)).astype(bf16)
        kv_ref[0, d, 0] = proj[feat : 2 * feat].astype(bf16)
        kv_ref[0, d, 1] = proj[2 * feat :].astype(bf16)


def project(near, x_rows):
    dp, width, cols = near.shape
    rows, _, tokens = x_rows.shape
    feat = cols // 3
    return pl.pallas_call(
        project_kernel,
        grid=(rows,),
        in_specs=[whole(near), pl.BlockSpec((1, width, tokens), lambda r: (r, 0, 0))],
        out_specs=[
            pl.BlockSpec((1, dp, feat, tokens), lambda r: (r, 0, 0, 0)),
            pl.BlockSpec((1, dp, 2, feat, tokens), lambda r: (r, 0, 0, 0, 0)),
        ],
        out_shape=[
            jax.ShapeDtypeStruct((rows, dp, feat, tokens), bf16),
            jax.ShapeDtypeStruct((rows, dp, 2, feat, tokens), bf16),
        ],
        scratch_shapes=[pltpu.VMEM((dp, cols, width), bf16)],
        compiler_params=kernel_params(),
        name="project",
    )(near, x_rows)


def project_back_kernel(*refs, sources):
    near_ref, x_ref, dq_ref = refs[:3]
    dkv_refs = refs[3 : 3 + sources]
    dx_ref, g_ref, acc = refs[3 + sources :]
    r = pl.program_id(0)

    @pl.when(r == 0)
    def _():
        acc[...] = jnp.zeros_like(acc)

    total = None
    for d in range(near_ref.shape[0]):
        parts = [dq_ref[0, d]]
        for kind in range(2):
            value = sum(ref[0, d, kind].astype(f32) for ref in dkv_refs)
            parts.append(value.astype(bf16))
        grad = jnp.concatenate(parts, axis=0)
        acc[d] += dot(x_ref[0], grad, 1, 1)
        part = dot(near_ref[d], grad, 1, 0)
        total = part if total is None else total + part
    dx_ref[0] = total.astype(bf16)

    @pl.when(r == pl.num_programs(0) - 1)
    def _():
        g_ref[...] = acc[...].astype(bf16)


def project_back(near, x_rows, d_query, d_kv):
    dp, width, cols = near.shape
    rows, _, tokens = x_rows.shape
    feat = cols // 3
    kv_spec = pl.BlockSpec((1, dp, 2, feat, tokens), lambda r: (r, 0, 0, 0, 0))
    return pl.pallas_call(
        functools.partial(project_back_kernel, sources=len(d_kv)),
        grid=(rows,),
        in_specs=[
            whole(near),
            pl.BlockSpec((1, width, tokens), lambda r: (r, 0, 0)),
            pl.BlockSpec((1, dp, feat, tokens), lambda r: (r, 0, 0, 0)),
        ]
        + [kv_spec] * len(d_kv),
        out_specs=[pl.BlockSpec((1, width, tokens), lambda r: (r, 0, 0)), whole(near)],
        out_shape=[
            jax.ShapeDtypeStruct(x_rows.shape, bf16),
            jax.ShapeDtypeStruct(near.shape, bf16),
        ],
        scratch_shapes=[pltpu.VMEM(near.shape, f32)],
        compiler_params=kernel_params(),
        name="project_back",
    )(near, x_rows, d_query, *d_kv)


def cross_kv_kernel(w_ref, chosen_ref, o_ref):
    feat2 = o_ref.shape[2]
    weight = w_ref[0][:, :feat2].T
    for n in range(chosen_ref.shape[0]):
        o_ref[n, 0] = dot(weight, chosen_ref[n], 1, 0).astype(bf16)


def cross_kv(small, chosen, feat):
    groups, width, cols = small.shape
    count, _, tokens = chosen.shape
    return pl.pallas_call(
        cross_kv_kernel,
        grid=(groups,),
        in_specs=[pl.BlockSpec((1, width, 2 * 128), lambda g: (g, 0, 0)), whole(chosen)],
        out_specs=pl.BlockSpec((count, 1, 2 * feat, tokens), lambda g: (0, g, 0, 0)),
        out_shape=jax.ShapeDtypeStruct((count, groups, 2 * feat, tokens), bf16),
        compiler_params=kernel_params(),
        name="cross_kv",
    )(small, chosen)


def attn_place(g, rows):
    return g % rows, g // rows


def after_self_kernel(x_ref, attn_ref, w_ref, gain_ref, normed_ref, inv_ref, low_ref, cq_ref, acc):
    groups, feat, tokens = cq_ref.shape
    rows = attn_ref.shape[0]
    total = x_ref[...].astype(f32)
    for g in range(groups):
        r, d = attn_place(g, rows)
        total = total + dot(w_ref[g, :, 2 * feat : 3 * feat], attn_ref[r, d], 1, 0)
    acc[...] = total

    def body(at):
        normed, inv_std = norm_stats(acc[:, at])
        normed_ref[:, at] = normed
        inv_ref[:, at] = inv_std
        low_ref[:, at] = (normed * gain_ref[:, 0:1]).astype(bf16)

    by_columns(tokens, body)
    low = low_ref[...]
    for g in range(groups):
        query = dot(w_ref[g, :, 3 * feat : 4 * feat], low, 0, 0)
        cq_ref[g] = (query * (0.125 * LOG2E)).astype(bf16)


def after_self(x_own, attn, small, gains, feat):
    width, tokens = x_own.shape
    groups = small.shape[0]
    args = (x_own, attn, small, gains)
    outs = [
        jax.ShapeDtypeStruct((width, tokens), f32),
        jax.ShapeDtypeStruct((1, tokens), f32),
        jax.ShapeDtypeStruct((width, tokens), bf16),
        jax.ShapeDtypeStruct((groups, feat, tokens), bf16),
    ]
    return pl.pallas_call(
        after_self_kernel,
        grid=(1,),
        in_specs=[whole(a) for a in args],
        out_specs=[whole(o) for o in outs],
        out_shape=outs,
        scratch_shapes=[pltpu.VMEM((width, tokens), f32)],
        compiler_params=kernel_params(),
        name="after_self",
    )(*args)


def middle_kernel(
    normed_one_ref, catt_ref, wc_ref, up_ref, down_ref, cot_ref, gain_ref,
    out_ref, dcatt_ref, dy_ref, dcross_ref, gup_ref, gdown_ref, dg_two_ref, dg_three_ref,
    acc, normed_two, inv_two, act, slope, h_fm, h_tm, d_fm, d_tm,
):
    i = pl.program_id(0)
    groups, feat, tokens = catt_ref.shape
    units = up_ref.shape[2]
    step = min(256, tokens)

    @pl.when(i == 0)
    def _():
        total = normed_one_ref[...] * gain_ref[:, 0:1]
        for g in range(groups):
            total = total + dot(wc_ref[g, :, :feat], catt_ref[g], 1, 0)
        acc[...] = total

        def body(at):
            normed, inv_std = norm_stats(acc[:, at])
            normed_two[:, at] = normed
            inv_two[:, at] = inv_std
            value = normed * gain_ref[:, 1:2]
            acc[:, at] = value
            h_fm[:, at] = value.astype(bf16)

        by_columns(tokens, body)
        h_tm[...] = h_fm[...].T

    @pl.when(i < groups)
    def _():
        for t in range(0, tokens, step):
            upper = dot(h_tm[t : t + step, :], up_ref[0], 1, 0)
            cdf = 0.5 * (1.0 + lax.erf(upper * 0.7071067811865476))
            density = jnp.exp(-0.5 * upper * upper) * 0.3989422804014327
            act[i, t : t + step, :] = (upper * cdf).astype(bf16)
            slope[i, t : t + step, :] = (cdf + upper * density).astype(bf16)
        acc[...] += dot(down_ref[0], act[i], 1, 1)

    @pl.when(i == groups - 1)
    def _():
        dg_three_ref[...] = jnp.zeros_like(dg_three_ref)
        dg_two_ref[...] = jnp.zeros_like(dg_two_ref)

        def body(at):
            normed, inv_std = norm_stats(acc[:, at])
            gain = gain_ref[:, 2:3]
            out_ref[:, at] = (normed * gain).astype(bf16)
            grad = cot_ref[:, at].astype(f32)
            dg_three_ref[...] += grad * normed
            value = norm_back(grad, gain, normed, inv_std)
            acc[:, at] = value
            d_fm[:, at] = value.astype(bf16)

        by_columns(tokens, body)
        d_tm[...] = d_fm[...].T

    @pl.when(i >= groups)
    def _():
        g = i - groups
        for t in range(0, tokens, step):
            at = slice(t, t + step)
            back = dot(d_tm[at, :], down_ref[0], 1, 0) * slope[g, at, :].astype(f32)
            slope[g, at, :] = back.astype(bf16)
        gdown_ref[0] = dot(d_fm[...], act[g], 1, 0).astype(bf16)
        gup_ref[0] = dot(h_fm[...], slope[g], 1, 0).astype(bf16)
        acc[...] += dot(up_ref[0], slope[g], 1, 1)

    @pl.when(i == 2 * groups - 1)
    def _():
        def body(at):
            grad = acc[:, at]
            normed = normed_two[:, at]
            dg_two_ref[...] += grad * normed
            value = norm_back(grad, gain_ref[:, 1:2], normed, inv_two[:, at])
            dy_ref[:, at] = value
            dcross_ref[:, at] = value.astype(bf16)

        by_columns(tokens, body)
        low = dcross_ref[...]
        for g in range(groups):
            dcatt_ref[g] = dot(wc_ref[g, :, :feat], low, 0, 0).astype(bf16)


def middle(normed_one, catt, small, up, down, cot, gains):
    width, tokens = normed_one.shape
    groups, feat, _ = catt.shape
    units = up.shape[2]
    lanes = min(128, tokens)

    def weight():
        return pl.BlockSpec((1, width, units), lambda i: (i % groups, 0, 0))

    def grad_out():
        return pl.BlockSpec((1, width, units), lambda i: (jnp.maximum(i - groups, 0), 0, 0))

    outs = [
        jax.ShapeDtypeStruct((width, tokens), bf16),
        jax.ShapeDtypeStruct(catt.shape, bf16),
        jax.ShapeDtypeStruct((width, tokens), f32),
        jax.ShapeDtypeStruct((width, tokens), bf16),
        jax.ShapeDtypeStruct(up.shape, bf16),
        jax.ShapeDtypeStruct(up.shape, bf16),
        jax.ShapeDtypeStruct((width, lanes), f32),
        jax.ShapeDtypeStruct((width, lanes), f32),
    ]
    specs = [whole(o) for o in outs]
    specs[4], specs[5] = grad_out(), grad_out()
    return pl.pallas_call(
        middle_kernel,
        grid=(2 * groups,),
        in_specs=[
            whole(normed_one),
            whole(catt),
            pl.BlockSpec((groups, width, 128), lambda i: (0, 0, 3)),
            weight(),
            weight(),
            whole(cot),
            whole(gains),
        ],
        out_specs=specs,
        out_shape=outs,
        scratch_shapes=[
            pltpu.VMEM((width, tokens), f32),
            pltpu.VMEM((width, tokens), f32),
            pltpu.VMEM((1, tokens), f32),
            pltpu.VMEM((groups, tokens, units), bf16),
            pltpu.VMEM((groups, tokens, units), bf16),
            pltpu.VMEM((width, tokens), bf16),
            pltpu.VMEM((tokens, width), bf16),
            pltpu.VMEM((width, tokens), bf16),
            pltpu.VMEM((tokens, width), bf16),
        ],
        compiler_params=kernel_params(),
        cost_estimate=pl.CostEstimate(
            flops=12 * groups * width * units * tokens, bytes_accessed=4 * up.size * 2, transcendentals=0
        ),
        name="middle",
    )(normed_one, catt, small, up, down, cot, gains)


def before_self_kernel(
    dcq_ref, w_ref, dy_ref, normed_ref, inv_ref, gain_ref,
    dattn_ref, dlow_ref, dy_one_ref, dg_ref, acc,
):
    groups, feat, tokens = dcq_ref.shape
    rows = dattn_ref.shape[0]
    total = dy_ref[...]
    for g in range(groups):
        total = total + dot(w_ref[g, :, 3 * feat : 4 * feat], dcq_ref[g], 1, 0)
    acc[...] = total
    dg_ref[...] = jnp.zeros_like(dg_ref)

    def body(at):
        grad = acc[:, at]
        normed = normed_ref[:, at]
        dg_ref[...] += grad * normed
        value = norm_back(grad, gain_ref[:, 0:1], normed, inv_ref[:, at])
        dy_one_ref[:, at] = value
        dlow_ref[:, at] = value.astype(bf16)

    by_columns(tokens, body)
    low = dlow_ref[...]
    for g in range(groups):
        r, d = attn_place(g, rows)
        dattn_ref[r, d] = dot(w_ref[g, :, 2 * feat : 3 * feat], low, 0, 0).astype(bf16)


def before_self(d_cq, small, dy_two, normed_one, inv_one, gains, attn_shape):
    width, tokens = dy_two.shape
    args = (d_cq, small, dy_two, normed_one, inv_one, gains)
    outs = [
        jax.ShapeDtypeStruct(attn_shape, bf16),
        jax.ShapeDtypeStruct((width, tokens), bf16),
        jax.ShapeDtypeStruct((width, tokens), f32),
        jax.ShapeDtypeStruct((width, min(128, tokens)), f32),
    ]
    return pl.pallas_call(
        before_self_kernel,
        grid=(1,),
        in_specs=[whole(a) for a in args],
        out_specs=[whole(o) for o in outs],
        out_shape=outs,
        scratch_shapes=[pltpu.VMEM((width, tokens), f32)],
        compiler_params=kernel_params(),
        name="before_self",
    )(*args)


def small_grads_kernel(
    w_ref, chosen_ref, dckv_ref, attn_ref, dcq_ref, catt_ref, dlow_ref, h_ref, dcross_ref,
    dg_one_ref, dg_two_ref, dg_three_ref, rest_ref, dchosen_ref, acc, gain_cols,
):
    g = pl.program_id(0)
    feat2 = dckv_ref.shape[2]
    feat = feat2 // 2
    count, width, tokens = chosen_ref.shape

    @pl.when(g == 0)
    def _():
        col = lax.broadcasted_iota(jnp.int32, gain_cols.shape, 1)
        total = jnp.zeros(gain_cols.shape, f32)
        for k, ref in enumerate((dg_one_ref, dg_two_ref, dg_three_ref)):
            total = jnp.where(col == k, jnp.sum(ref[...], axis=1, keepdims=True), total)
        gain_cols[...] = total.astype(bf16)
        acc[...] = jnp.zeros_like(acc)

    weight = w_ref[0][:, :feat2]
    total = None
    for n in range(count):
        grad = dckv_ref[n, 0]
        acc[n] += dot(weight, grad, 1, 0)
        part = dot(chosen_ref[n], grad, 1, 1)
        total = part if total is None else total + part
    rest_ref[0, :, :feat2] = total.astype(bf16)
    pairs = ((dlow_ref, attn_ref[0, 0]), (h_ref, dcq_ref[0]), (dcross_ref, catt_ref[0]))
    for k, (left, right) in enumerate(pairs):
        at = feat2 + k * feat
        rest_ref[0, :, at : at + feat] = dot(left[...], right, 1, 1).astype(bf16)
    rest_ref[0, :, 5 * feat :] = gain_cols[...]

    @pl.when(g == pl.num_programs(0) - 1)
    def _():
        dchosen_ref[...] = acc[...].astype(bf16)


def small_grads(small, chosen, d_ckv, attn, d_cq, catt, d_low, h_low, d_cross, dgs):
    groups, width, cols = small.shape
    count, _, c_tokens = chosen.shape
    feat2 = d_ckv.shape[2]
    feat = feat2 // 2
    tokens = d_low.shape[1]
    rows = attn.shape[0]
    piece = pl.BlockSpec((1, feat, tokens), lambda g: (g, 0, 0))
    return pl.pallas_call(
        small_grads_kernel,
        grid=(groups,),
        in_specs=[
            pl.BlockSpec((1, width, 2 * 128), lambda g: (g, 0, 0)),
            whole(chosen),
            pl.BlockSpec((count, 1, feat2, c_tokens), lambda g: (0, g, 0, 0)),
            pl.BlockSpec((1, 1, feat, tokens), lambda g: (g % rows, g // rows, 0, 0)),
            piece,
            piece,
            whole(d_low),
            whole(h_low),
            whole(d_cross),
        ]
        + [whole(v) for v in dgs],
        out_specs=[pl.BlockSpec((1, width, cols), lambda g: (g, 0, 0)), whole(chosen)],
        out_shape=[
            jax.ShapeDtypeStruct(small.shape, bf16),
            jax.ShapeDtypeStruct(chosen.shape, bf16),
        ],
        scratch_shapes=[
            pltpu.VMEM(chosen.shape, f32),
            pltpu.VMEM((width, cols - 5 * feat), bf16),
        ],
        compiler_params=kernel_params(),
        name="small_grads",
    )(small, chosen, d_ckv, attn, d_cq, catt, d_low, h_low, d_cross, *dgs)


def mm(spec, left, right):
    return jnp.einsum(spec, left, right, preferred_element_type=f32)


def per_device(
    x_in, prefix, enc_bank, bank_rows, w_qkv, w_out, w_cross_q, w_cross_kv, w_cross_out,
    w_up, w_down, ln_gains, out_grad,
):
    dp, rows, cols = lax.axis_size("dp"), lax.axis_size("row"), lax.axis_size("col")
    d_pos, r_pos, c_pos = lax.axis_index("dp"), lax.axis_index("row"), lax.axis_index("col")
    own_seqs, part_width, row_len = x_in.shape
    seqs = own_seqs * dp
    sub = cols // seqs
    parts = dp * sub
    width = part_width * cols
    tokens = row_len // parts
    heads = w_qkv.shape[2]
    feat = heads * HALF
    units = w_up.shape[1]
    odd = (r_pos % 2) == 1
    seq_pos = c_pos // sub
    part_pos = d_pos * sub + c_pos % sub
    groups = [[s * sub + k for k in range(sub)] for s in range(seqs)]
    everywhere = ("dp", "row", "col")
    swap = [(0, 1), (1, 0)]
    first_core = d_pos == 0

    def flip(value):
        return jnp.where(odd, value[:, :, ::-1], value)

    def to_tokens(value):
        take = value.shape[-1] // parts
        if parts == 2:
            low, high = value[..., :take], value[..., take:]
            upper = first_core == odd
            got = lax.ppermute(jnp.where(upper, low, high), "dp", swap)
            kept = jnp.where(upper, high, low)
            value = jnp.concatenate(
                [jnp.where(first_core, kept, got), jnp.where(first_core, got, kept)], axis=0
            )
        else:
            value = flip(value.reshape(own_seqs, part_width, parts, take))
            value = value.reshape(own_seqs, part_width, dp, sub, take)
            value = lax.all_to_all(value, "dp", 2, 0, tiled=True)
            value = value.reshape(seqs, part_width, sub, take).transpose(0, 2, 1, 3)
        value = lax.all_to_all(value.reshape(cols, part_width, take), "col", 0, 0, tiled=True)
        return value.reshape(width, take)

    def to_home(value):
        take = value.shape[-1]
        value = lax.all_to_all(value.reshape(cols, part_width, take), "col", 0, 0, tiled=True)
        if parts == 2:
            early, late = value[:own_seqs], value[own_seqs:]
            got = lax.ppermute(jnp.where(first_core, late, early), "dp", swap)
            kept = jnp.where(first_core, early, late)
            upper = first_core == odd
            return jnp.concatenate(
                [jnp.where(upper, got, kept), jnp.where(upper, kept, got)], axis=-1
            )
        value = value.reshape(seqs, sub, part_width, take).transpose(0, 2, 1, 3)
        value = value.reshape(seqs, part_width, 1, sub, take)
        value = lax.all_to_all(value, "dp", 0, 2, tiled=True)
        value = flip(value.reshape(own_seqs, part_width, parts, take))
        return value.reshape(own_seqs, part_width, parts * take)

    near = lax.all_gather(w_qkv.reshape(part_width, 3 * feat), ("dp", "col"), axis=0)
    near = near.reshape(dp, width, 3 * feat)
    x_own = to_tokens(x_in)
    x_rows = lax.all_gather(x_own, "row", axis=0)
    spare = 512 - 5 * feat
    small = jnp.concatenate(
        [
            w_cross_kv.reshape(part_width, 2 * feat),
            w_out.reshape(feat, part_width).T,
            w_cross_q.reshape(part_width, feat),
            w_cross_out.reshape(feat, part_width).T,
            jnp.zeros((part_width, spare), bf16),
        ],
        axis=1,
    )
    blocks = dp * rows

    def gather_all(value):
        value = lax.all_gather(value, everywhere, axis=0)
        return value.reshape(blocks, width, value.shape[-1])

    small_all = gather_all(small)
    up_all = gather_all(w_up)
    down_all = gather_all(w_down.T)
    gains = lax.all_gather(ln_gains.astype(f32).T, "col", axis=0, tiled=True)

    query, kv_own = project(near, x_rows)
    query = query.reshape(rows, dp, heads, HALF, tokens)
    kv_own = kv_own.reshape(rows, dp, 2, heads, HALF, tokens)

    def index_of(row, part):
        return jnp.where(row % 2 == 1, parts - 1 - part, part) + row * parts

    row_ids = jnp.arange(rows, dtype=jnp.int32)
    if sub == 1:
        kv_list = [kv_own, lax.ppermute(kv_own, "dp", swap)]
        owners = [part_pos, 1 - part_pos]
    else:
        kv_all = lax.all_gather(kv_own, "col", axis=0, axis_index_groups=groups)
        kv_all = lax.all_gather(kv_all, "dp", axis=0).reshape((parts,) + kv_own.shape)
        kv_list = [kv_all[j] for j in range(parts)]
        owners = list(range(parts))
    q_start = index_of(row_ids, part_pos) * tokens
    places = [index_of(row_ids, owner) for owner in owners]
    seq_prefix = lax.all_gather(prefix, "dp", axis=0, tiled=True)[seq_pos]
    meta = jnp.concatenate([seq_prefix[None], q_start] + places).astype(jnp.int32)
    mixed, lse = attend(meta, query, kv_list, True, "self_attention")
    attn = lax.all_to_all(mixed, "row", 0, 0, tiled=True).reshape(rows, dp, feat, tokens)
    normed_one, inv_one, h_low, cross_q = after_self(x_own, attn, small_all, gains, feat)
    cross_q = cross_q.reshape(1, dp, rows, heads, HALF, tokens)

    picked = bank_rows.shape[1] // rows
    row_pick = lax.dynamic_slice_in_dim(bank_rows, r_pos * picked, picked, 1)
    bank_ids = jnp.arange(enc_bank.shape[2], dtype=jnp.int32)
    hot = (bank_ids[None, :, None] == row_pick[:, None, :]).astype(bf16)
    chosen = to_tokens(mm("swn,snp->swp", enc_bank, hot).astype(bf16))
    c_tokens = chosen.shape[1]
    if sub > 1:
        chosen = lax.all_gather(chosen, "col", axis=0, axis_index_groups=groups)
    chosen = lax.all_gather(chosen, ("dp", "row"), axis=0)
    chosen = chosen.reshape(blocks * sub, width, c_tokens)
    ckv = cross_kv(small_all, chosen, feat)
    ckv = ckv.reshape(blocks * sub, dp, rows, 2, heads, HALF, c_tokens)
    catt, lse_cross = attend(meta, cross_q, [ckv], False, "cross_attention")
    catt_flat = catt.reshape(blocks, feat, tokens)

    cot = to_tokens(out_grad)
    block_out, d_catt, dy_two, d_cross, g_up, g_down, dg_two, dg_three = middle(
        normed_one, catt_flat, small_all, up_all, down_all, cot, gains
    )
    block_out = to_home(block_out)
    d_cq, d_ckv = attend_back(
        meta, cross_q, [ckv], d_catt.reshape(catt.shape), catt, lse_cross, False, [bf16],
        "cross_attention_back",
    )
    d_cq = d_cq.reshape(blocks, feat, tokens)
    d_ckv = d_ckv.reshape(blocks * sub, blocks, 2 * feat, c_tokens)
    d_attn, d_low, dy_one, dg_one = before_self(
        d_cq, small_all, dy_two, normed_one, inv_one, gains, attn.shape
    )
    d_mixed = lax.all_to_all(d_attn, "row", 0, 0, tiled=True).reshape(mixed.shape)
    rest, d_chosen = small_grads(
        small_all, chosen, d_ckv, attn, d_cq, catt_flat, d_low, h_low, d_cross,
        (dg_one, dg_two, dg_three),
    )

    d_chosen = d_chosen.reshape(dp, rows, sub, width, c_tokens)
    d_chosen = lax.psum_scatter(d_chosen, "dp", scatter_dimension=0, tiled=False)
    d_chosen = lax.psum_scatter(d_chosen, "row", scatter_dimension=0, tiled=False)
    if sub > 1:
        d_chosen = lax.psum_scatter(
            d_chosen, "col", scatter_dimension=0, tiled=True, axis_index_groups=groups
        )
    d_chosen = d_chosen.reshape(width, c_tokens)
    d_chosen = lax.all_gather(to_home(d_chosen), "row", axis=2, tiled=True)
    hot_all = (bank_rows[:, :, None] == bank_ids[None, None, :]).astype(bf16)
    bank_grad = mm("swp,spn->swn", d_chosen, hot_all)

    types = [f32] + [bf16] * (len(kv_list) - 1) if sub == 1 else [bf16] * len(kv_list)
    d_query, *d_kv = attend_back(
        meta, query, kv_list, d_mixed, mixed, lse, True, types, "self_attention_back"
    )
    if sub == 1:
        d_kv = [d_kv[0], lax.ppermute(d_kv[1], "dp", swap)]
    else:
        d_kv = jnp.stack(d_kv).reshape((dp, sub) + kv_own.shape)
        d_kv = lax.psum_scatter(d_kv, "dp", scatter_dimension=0, tiled=True)
        d_kv = lax.psum_scatter(
            d_kv, "col", scatter_dimension=1, tiled=True, axis_index_groups=groups
        )
        d_kv = [d_kv]
    kv_shape = (rows, dp, 2, feat, tokens)
    d_kv = [value.reshape(kv_shape) for value in d_kv]
    dx_part, g_qkv = project_back(near, x_rows, d_query.reshape(rows, dp, feat, tokens), d_kv)
    dx_part = lax.all_to_all(dx_part, "row", 0, 0, tiled=True)
    dx = dy_one + jnp.sum(dx_part.astype(f32), axis=0)
    x_grad = to_home(dx.astype(bf16)).astype(f32)

    def scatter(value):
        value = value.reshape(dp, rows, cols, part_width, value.shape[-1])
        for name in everywhere:
            value = lax.psum_scatter(value, name, scatter_dimension=0, tiled=False)
        return value.astype(f32)

    up_grad = scatter(g_up)
    down_grad = scatter(g_down).T
    rest = scatter(rest)
    qkv_grad = g_qkv.reshape(dp, cols, part_width, 3 * feat)
    qkv_grad = lax.psum_scatter(qkv_grad, "dp", scatter_dimension=0, tiled=False)
    qkv_grad = lax.psum_scatter(qkv_grad, "col", scatter_dimension=0, tiled=False).astype(f32)

    return (
        block_out,
        x_grad,
        bank_grad,
        qkv_grad.reshape(w_qkv.shape),
        rest[:, 2 * feat : 3 * feat].T.reshape(w_out.shape),
        rest[:, 3 * feat : 4 * feat].reshape(w_cross_q.shape),
        rest[:, : 2 * feat].reshape(w_cross_kv.shape),
        rest[:, 4 * feat : 5 * feat].T.reshape(w_cross_out.shape),
        up_grad,
        down_grad,
        rest[:, 5 * feat : 5 * feat + 3].T,
    )


def solution(mesh):
    placed = (
        P("dp", "col", "row"),
        P("dp"),
        P("dp", "col", None),
        P("dp", None),
        P("col", None, "row", "dp"),
        P("row", "dp", "col"),
        P("col", "row", "dp"),
        P("col", None, "row", "dp"),
        P("row", "dp", "col"),
        P("col", ("dp", "row")),
        P(("dp", "row"), "col"),
        P(None, "col"),
        P("dp", "col", "row"),
    )
    return jax.shard_map(
        per_device,
        mesh=mesh,
        in_specs=placed,
        out_specs=(
            P("dp", "col", "row"),
            P("dp", "col", "row"),
            P("dp", "col", None),
            P("col", None, "row", "dp"),
            P("row", "dp", "col"),
            P("col", "row", "dp"),
            P("col", None, "row", "dp"),
            P("row", "dp", "col"),
            P("col", ("dp", "row")),
            P(("dp", "row"), "col"),
            P(None, "col"),
        ),
        check_vma=False,
    )
```

```python
import functools

import jax
import jax.numpy as jnp
from jax import lax
from jax.experimental import pallas as pl
from jax.experimental.pallas import tpu as pltpu
from jax.sharding import PartitionSpec as P

bf16 = jnp.bfloat16
f32 = jnp.float32
HD = 64
HALF = 32
NORM_EPS = 1e-05
NEG = -1e30
LIMIT = 90.0
LN2 = 0.6931471805599453
LOG2E = 1.4426950408889634
KB = 512


def dot(left, right, left_dim, right_dim):
    return lax.dot_general(
        left, right, (((left_dim,), (right_dim,)), ((), ())), preferred_element_type=f32
    )


def ones_rows(count, shape, dim):
    return jnp.where(lax.broadcasted_iota(jnp.int32, shape, dim) < count, 1.0, 0.0).astype(bf16)


def allowed_block(meta, i, start, width, cols):
    k_pos = start + lax.broadcasted_iota(jnp.int32, (width, cols), 0)
    q_pos = meta[1 + i] + lax.broadcasted_iota(jnp.int32, (1, cols), 1)
    return k_pos <= jnp.maximum(q_pos, meta[0] - 1)


def block_range(meta, i, cols):
    full = jnp.maximum(meta[1 + i], meta[0]) // KB
    total = (jnp.maximum(meta[1 + i] + cols, meta[0]) + KB - 1) // KB
    return full, total


def over_keys(meta, i, cols, keys, masked, step, carry):
    if not masked:
        for start in range(0, keys, KB):
            carry = step(start, carry, False, KB)
        return carry
    full, total = block_range(meta, i, cols)
    pairs = full // 2
    carry = lax.fori_loop(0, pairs, lambda j, c: step(j * 2 * KB, c, False, 2 * KB), carry)
    carry = lax.fori_loop(2 * pairs, full, lambda j, c: step(j * KB, c, False, KB), carry)
    return lax.fori_loop(full, total, lambda j, c: step(j * KB, c, True, KB), carry)


def pieces(kv_refs, masked):
    out = []
    for ref in kv_refs:
        count = ref.shape[0]
        for b in range(count):
            out.append((ref, b))
    return out


def piece_start(meta, n_query, index, length, masked):
    if masked:
        return pl.multiple_of(meta[1 + n_query + index] * length, length)
    return index * length


def attend_kernel(*refs, sources, n_query, masked):
    meta, q_ref = refs[:2]
    kv_refs = refs[2 : 2 + sources]
    o_ref, l_ref, key_rows, val_cols = refs[2 + sources :]
    i = pl.program_id(1)
    cols = q_ref.shape[-1]
    keys = val_cols.shape[-1]

    @pl.when(i == 0)
    def _():
        key_rows[:, HD:] = ones_rows(1, (keys, 16), 1)
        val_cols[HD:, :] = ones_rows(1, (16, keys), 0)
        for index, (ref, b) in enumerate(pieces(kv_refs, masked)):
            length = ref.shape[-1]
            at = pl.ds(piece_start(meta, n_query, index, length, masked), length)
            key_rows[at, :HD] = ref[b, :, 0, 0].reshape(HD, length).T
            val_cols[:HD, at] = ref[b, :, 1, 0].reshape(HD, length)

    query = q_ref[0, :, 0].reshape(HD, cols)
    first = dot(key_rows[0:128, :HD], query, 1, 0)
    shift = jnp.max(first, axis=0, keepdims=True).astype(bf16).astype(f32)
    row = lax.broadcasted_iota(jnp.int32, (16, cols), 0)
    query_more = jnp.concatenate([query, jnp.where(row == 0, -shift, 0.0).astype(bf16)], axis=0)

    def step(start, carry, mask, width):
        top, acc = carry
        at = pl.ds(pl.multiple_of(start, KB), width)
        scores = dot(key_rows[at, :], query_more, 1, 0)
        if mask:
            scores = jnp.where(allowed_block(meta, i, start, width, cols), scores, NEG)
        top = jnp.maximum(top, jnp.max(scores, axis=0, keepdims=True))
        acc = acc + dot(val_cols[:, at], jnp.exp2(scores).astype(bf16), 1, 0)
        return top, acc

    def put(shift, acc):
        total = acc[HD : HD + 1, :]
        mixed = (acc[:HD] * (1.0 / total)).astype(bf16)
        o_ref[0, :, 0] = mixed.reshape(2, HALF, cols)
        l_ref[0, 0] = shift + jnp.log2(total)

    start = (jnp.full((1, cols), NEG, f32), jnp.zeros((HD + 16, cols), f32))
    top, acc = over_keys(meta, i, cols, keys, masked, step, start)
    put(shift, acc)

    @pl.when(jnp.max(top) > LIMIT)
    def _():
        def careful(j, carry):
            high, acc = carry
            at = pl.ds(pl.multiple_of(j * KB, KB), KB)
            scores = dot(key_rows[at, :HD], query, 1, 0)
            if masked:
                scores = jnp.where(allowed_block(meta, i, j * KB, KB, cols), scores, NEG)
            new = jnp.maximum(high, jnp.max(scores, axis=0, keepdims=True))
            part = dot(val_cols[:, at], jnp.exp2(scores - new).astype(bf16), 1, 0)
            return new, acc * jnp.exp2(high - new) + part

        total = block_range(meta, i, cols)[1] if masked else keys // KB
        put(*lax.fori_loop(0, total, careful, start))


def attend_back_kernel(*refs, sources, n_query, masked):
    meta, q_ref = refs[:2]
    kv_refs = refs[2 : 2 + sources]
    g_ref, o_ref, l_ref = refs[2 + sources : 5 + sources]
    dq_ref = refs[5 + sources]
    dkv_refs = refs[6 + sources : 6 + 2 * sources]
    key_rows, val_rows, key_cols, dk_acc, dv_acc = refs[6 + 2 * sources :]
    i = pl.program_id(1)
    cols = q_ref.shape[-1]
    keys = key_cols.shape[-1]

    @pl.when(i == 0)
    def _():
        key_rows[:, HD:] = ones_rows(3, (keys, 16), 1)
        val_rows[:, HD:] = ones_rows(3, (keys, 16), 1)
        for index, (ref, b) in enumerate(pieces(kv_refs, masked)):
            length = ref.shape[-1]
            at = pl.ds(piece_start(meta, n_query, index, length, masked), length)
            k_part = ref[b, :, 0, 0].reshape(HD, length)
            key_cols[:, at] = k_part
            key_rows[at, :HD] = k_part.T
            val_rows[at, :HD] = ref[b, :, 1, 0].reshape(HD, length).T
        dk_acc[...] = jnp.zeros_like(dk_acc)
        dv_acc[...] = jnp.zeros_like(dv_acc)

    query = q_ref[0, :, 0].reshape(HD, cols)
    grad = g_ref[0, :, 0].reshape(HD, cols)
    delta = jnp.sum(
        grad.astype(f32) * o_ref[0, :, 0].reshape(HD, cols).astype(f32), axis=0, keepdims=True
    )

    def with_shift(value, shift):
        high = shift.astype(bf16).astype(f32)
        mid = (shift - high).astype(bf16).astype(f32)
        low = shift - high - mid
        row = lax.broadcasted_iota(jnp.int32, (16, cols), 0)
        more = jnp.where(row == 0, -high, jnp.where(row == 1, -mid, jnp.where(row == 2, -low, 0.0)))
        return jnp.concatenate([value, more.astype(bf16)], axis=0)

    query_more = with_shift(query, l_ref[0, 0])
    grad_more = with_shift(grad, delta)

    def step(start, dq, mask, width):
        at = pl.ds(pl.multiple_of(start, KB), width)
        scores = dot(key_rows[at, :], query_more, 1, 0)
        if mask:
            scores = jnp.where(allowed_block(meta, i, start, width, cols), scores, NEG)
        probs = jnp.exp2(scores)
        grad_scores = (probs * dot(val_rows[at, :], grad_more, 1, 0)).astype(bf16)
        dv_acc[:, at] += dot(grad, probs.astype(bf16), 1, 1)
        dk_acc[:, at] += dot(query, grad_scores, 1, 1)
        return dq + dot(key_cols[:, at], grad_scores, 1, 0)

    dq = over_keys(meta, i, cols, keys, masked, step, jnp.zeros((HD, cols), f32))
    dq_ref[0, :, 0] = (dq * 0.125).astype(bf16).reshape(2, HALF, cols)

    @pl.when(i == n_query - 1)
    def _():
        for index, (ref, b) in enumerate(pieces(dkv_refs, masked)):
            length = ref.shape[-1]
            at = pl.ds(piece_start(meta, n_query, index, length, masked), length)
            ref[b, :, 0, 0] = (dk_acc[:, at] * LN2).astype(ref.dtype).reshape(2, HALF, length)
            ref[b, :, 1, 0] = dv_acc[:, at].astype(ref.dtype).reshape(2, HALF, length)


def attention_specs(query, kv_list, masked):
    cols = query.shape[-1]
    if masked:
        n_query, _, heads = query.shape[:3]
        grid = (heads, n_query)
        q_spec = pl.BlockSpec((1, 2, 1, HALF, cols), lambda h, i, m: (i, 0, h, 0, 0))
        kv_specs = [
            pl.BlockSpec(kv.shape[:3] + (1,) + kv.shape[4:], lambda h, i, m: (0, 0, 0, h, 0, 0))
            for kv in kv_list
        ]
        l_spec = pl.BlockSpec((1, 1, 1, cols), lambda h, i, m: (h, i, 0, 0))
        l_shape = (heads, n_query, 1, cols)
        keys = sum(kv.shape[0] * kv.shape[-1] for kv in kv_list)
    else:
        n_query = 1
        _, _, rows, heads = query.shape[:4]
        grid = (rows * heads, 1)
        q_spec = pl.BlockSpec(
            (1, 2, None, 1, HALF, cols), lambda g, i, m: (0, 0, g // heads, g % heads, 0, 0)
        )
        kv_specs = [
            pl.BlockSpec(
                (kv.shape[0], 2, None, 2, 1) + kv.shape[5:],
                lambda g, i, m: (0, 0, g // heads, 0, g % heads, 0, 0),
            )
            for kv in kv_list
        ]
        l_spec = pl.BlockSpec((1, 1, 1, cols), lambda g, i, m: (g, 0, 0, 0))
        l_shape = (rows * heads, 1, 1, cols)
        keys = sum(kv.shape[0] * kv.shape[-1] for kv in kv_list)
    return n_query, grid, q_spec, kv_specs, l_spec, l_shape, keys


def cost(query, keys, dots):
    pairs = query.size // HD * keys
    return pl.CostEstimate(
        flops=2 * pairs * 256 * dots // 2, bytes_accessed=query.size * 16, transcendentals=pairs
    )


def attend(meta, query, kv_list, masked, name):
    n_query, grid, q_spec, kv_specs, l_spec, l_shape, keys = attention_specs(query, kv_list, masked)
    return pl.pallas_call(
        functools.partial(attend_kernel, sources=len(kv_list), n_query=n_query, masked=masked),
        grid_spec=pltpu.PrefetchScalarGridSpec(
            num_scalar_prefetch=1,
            grid=grid,
            in_specs=[q_spec] + kv_specs,
            out_specs=[q_spec, l_spec],
            scratch_shapes=[pltpu.VMEM((keys, HD + 16), bf16), pltpu.VMEM((HD + 16, keys), bf16)],
        ),
        out_shape=[
            jax.ShapeDtypeStruct(query.shape, bf16),
            jax.ShapeDtypeStruct(l_shape, f32),
        ],
        compiler_params=pltpu.CompilerParams(vmem_limit_bytes=48 << 20),
        cost_estimate=cost(query, keys, 2),
        name=name,
    )(meta, query, *kv_list)


def attend_back(meta, query, kv_list, grad, out, lse, masked, types, name):
    n_query, grid, q_spec, kv_specs, l_spec, l_shape, keys = attention_specs(query, kv_list, masked)
    return pl.pallas_call(
        functools.partial(attend_back_kernel, sources=len(kv_list), n_query=n_query, masked=masked),
        grid_spec=pltpu.PrefetchScalarGridSpec(
            num_scalar_prefetch=1,
            grid=grid,
            in_specs=[q_spec] + kv_specs + [q_spec, q_spec, l_spec],
            out_specs=[q_spec] + kv_specs,
            scratch_shapes=[
                pltpu.VMEM((keys, HD + 16), bf16),
                pltpu.VMEM((keys, HD + 16), bf16),
                pltpu.VMEM((HD, keys), bf16),
                pltpu.VMEM((HD, keys), f32),
                pltpu.VMEM((HD, keys), f32),
            ],
        ),
        out_shape=[jax.ShapeDtypeStruct(query.shape, bf16)]
        + [jax.ShapeDtypeStruct(kv.shape, t) for kv, t in zip(kv_list, types)],
        compiler_params=pltpu.CompilerParams(vmem_limit_bytes=48 << 20),
        cost_estimate=cost(query, keys, 5),
        name=name,
    )(meta, query, *kv_list, grad, out, lse)


def kernel_params():
    return pltpu.CompilerParams(vmem_limit_bytes=60 << 20)


def whole(value):
    return pl.BlockSpec(value.shape, lambda *i: (0,) * value.ndim)


def by_columns(count, body):
    step = min(128, count)

    def one(j, carry):
        body(pl.ds(pl.multiple_of(j * step, step), step))
        return carry

    lax.fori_loop(0, count // step, one, 0)


def norm_stats(resid):
    width = resid.shape[0]
    mean = jnp.sum(resid, 0, keepdims=True) / width
    square = jnp.sum(resid * resid, 0, keepdims=True) / width
    inv_std = lax.rsqrt(square - mean * mean + NORM_EPS)
    return (resid - mean) * inv_std, inv_std


def norm_back(grad, gain, normed, inv_std):
    width = grad.shape[0]
    scaled = grad * gain
    total = jnp.sum(scaled, 0, keepdims=True) / width
    cross = jnp.sum(scaled * normed, 0, keepdims=True) / width
    return inv_std * (scaled - total - normed * cross)


def project_kernel(place_ref, near_ref, *refs, rows):
    x_refs = refs[:rows]
    q_ref, kv_ref, near_t = refs[rows:]
    feat = q_ref.shape[2]
    step = pl.program_id(0)

    @pl.when(step == 0)
    def _():
        for d in range(near_ref.shape[0]):
            near_t[d] = near_ref[d].T

    for k, x_ref in enumerate(x_refs):

        @pl.when(step == k)
        def _():
            for d in range(near_ref.shape[0]):
                proj = dot(near_t[d, : 3 * feat, :], x_ref[...], 1, 0)
                q_ref[0, d] = (proj[:feat] * (0.125 * LOG2E)).astype(bf16)
                kv_ref[0, d, 0] = proj[feat : 2 * feat].astype(bf16)
                kv_ref[0, d, 1] = proj[2 * feat :].astype(bf16)


def project(place, near, x_rows, feat):
    dp, width, cols = near.shape
    rows = len(x_rows)
    tokens = x_rows[0].shape[1]
    return pl.pallas_call(
        functools.partial(project_kernel, rows=rows),
        grid_spec=pltpu.PrefetchScalarGridSpec(
            num_scalar_prefetch=1,
            grid=(rows,),
            in_specs=[whole(near)] + [whole(x) for x in x_rows],
            out_specs=[
                pl.BlockSpec((1, dp, feat, tokens), lambda k, p: (p[0] ^ k, 0, 0, 0)),
                pl.BlockSpec((1, dp, 2, feat, tokens), lambda k, p: (p[0] ^ k, 0, 0, 0, 0)),
            ],
            scratch_shapes=[pltpu.VMEM((dp, cols, width), bf16)],
        ),
        out_shape=[
            jax.ShapeDtypeStruct((rows, dp, feat, tokens), bf16),
            jax.ShapeDtypeStruct((rows, dp, 2, feat, tokens), bf16),
        ],
        compiler_params=kernel_params(),
        name="project",
    )(place, near, *x_rows)


def project_back_kernel(place_ref, near_ref, *refs, rows, sources):
    x_refs, dq_ref = refs[:rows], refs[rows]
    dkv_refs = refs[rows + 1 : rows + 1 + sources]
    dx_ref, g_ref, acc = refs[rows + 1 + sources :]
    step = pl.program_id(0)
    feat = dq_ref.shape[2]

    @pl.when(step == 0)
    def _():
        acc[...] = jnp.zeros_like(acc)

    for k, x_ref in enumerate(x_refs):

        @pl.when(step == k)
        def _():
            total = None
            for d in range(near_ref.shape[0]):
                parts = [dq_ref[0, d]]
                for kind in range(2):
                    value = sum(ref[0, d, kind].astype(f32) for ref in dkv_refs)
                    parts.append(value.astype(bf16))
                grad = jnp.concatenate(parts, axis=0)
                acc[d, :, : 3 * feat] += dot(x_ref[...], grad, 1, 1)
                part = dot(near_ref[d, :, : 3 * feat], grad, 1, 0)
                total = part if total is None else total + part
            dx_ref[0] = total.astype(bf16)

    @pl.when(step == rows - 1)
    def _():
        g_ref[...] = acc[...].astype(bf16)


def project_back(place, near, x_rows, d_query, d_kv):
    dp, width, cols = near.shape
    rows = len(x_rows)
    tokens = x_rows[0].shape[1]
    feat = d_query.shape[2]
    kv_spec = pl.BlockSpec((1, dp, 2, feat, tokens), lambda k, p: (p[0] ^ k, 0, 0, 0, 0))
    return pl.pallas_call(
        functools.partial(project_back_kernel, rows=rows, sources=len(d_kv)),
        grid_spec=pltpu.PrefetchScalarGridSpec(
            num_scalar_prefetch=1,
            grid=(rows,),
            in_specs=[whole(near)]
            + [whole(x) for x in x_rows]
            + [pl.BlockSpec((1, dp, feat, tokens), lambda k, p: (p[0] ^ k, 0, 0, 0))]
            + [kv_spec] * len(d_kv),
            out_specs=[
                pl.BlockSpec((1, width, tokens), lambda k, p: (p[0] ^ k, 0, 0)),
                whole(near),
            ],
            scratch_shapes=[pltpu.VMEM(near.shape, f32)],
        ),
        out_shape=[
            jax.ShapeDtypeStruct((rows, width, tokens), bf16),
            jax.ShapeDtypeStruct(near.shape, bf16),
        ],
        compiler_params=kernel_params(),
        name="project_back",
    )(place, near, *x_rows, d_query, *d_kv)


def side_by_side(chosen_ref, wide):
    count, _, tokens = chosen_ref.shape
    for n in range(count):
        wide[:, n * tokens : (n + 1) * tokens] = chosen_ref[n]


def cross_kv_kernel(w_ref, chosen_ref, o_ref, wide):
    @pl.when(pl.program_id(0) == 0)
    def _():
        side_by_side(chosen_ref, wide)

    weight = w_ref[0][:, : o_ref.shape[1]].T
    o_ref[0] = dot(weight, wide[...], 1, 0).astype(bf16)


def cross_kv(small, chosen, feat):
    groups, width, cols = small.shape
    keys = chosen.shape[0] * chosen.shape[2]
    return pl.pallas_call(
        cross_kv_kernel,
        grid=(groups,),
        in_specs=[pl.BlockSpec((1, width, 2 * 128), lambda g: (g, 0, 0)), whole(chosen)],
        out_specs=pl.BlockSpec((1, 2 * feat, keys), lambda g: (g, 0, 0)),
        out_shape=jax.ShapeDtypeStruct((groups, 2 * feat, keys), bf16),
        scratch_shapes=[pltpu.VMEM((width, keys), bf16)],
        compiler_params=kernel_params(),
        name="cross_kv",
    )(small, chosen)


def attn_place(g, rows):
    return g % rows, g // rows


def after_self_kernel(x_ref, attn_ref, w_ref, gain_ref, normed_ref, inv_ref, low_ref, cq_ref, acc):
    groups, feat, tokens = cq_ref.shape
    rows = attn_ref.shape[0]
    total = x_ref[...].astype(f32)
    for g in range(groups):
        r, d = attn_place(g, rows)
        total = total + dot(w_ref[g, :, 2 * feat : 3 * feat], attn_ref[r, d], 1, 0)
    acc[...] = total

    def body(at):
        normed, inv_std = norm_stats(acc[:, at])
        normed_ref[:, at] = normed
        inv_ref[:, at] = inv_std
        low_ref[:, at] = (normed * gain_ref[:, 0:1]).astype(bf16)

    by_columns(tokens, body)
    low = low_ref[...]
    for g in range(groups):
        query = dot(w_ref[g, :, 3 * feat : 4 * feat], low, 0, 0)
        cq_ref[g] = (query * (0.125 * LOG2E)).astype(bf16)


def after_self(x_own, attn, small, gains, feat):
    width, tokens = x_own.shape
    groups = small.shape[0]
    args = (x_own, attn, small, gains)
    outs = [
        jax.ShapeDtypeStruct((width, tokens), f32),
        jax.ShapeDtypeStruct((1, tokens), f32),
        jax.ShapeDtypeStruct((width, tokens), bf16),
        jax.ShapeDtypeStruct((groups, feat, tokens), bf16),
    ]
    return pl.pallas_call(
        after_self_kernel,
        grid=(1,),
        in_specs=[whole(a) for a in args],
        out_specs=[whole(o) for o in outs],
        out_shape=outs,
        scratch_shapes=[pltpu.VMEM((width, tokens), f32)],
        compiler_params=kernel_params(),
        name="after_self",
    )(*args)


def middle_kernel(
    normed_one_ref, catt_ref, wc_ref, up_ref, down_ref, cot_ref, gain_ref,
    out_ref, dcatt_ref, dy_ref, dcross_ref, glarge_ref, dg_two_ref, dg_three_ref,
    acc, normed_two, inv_two, act, slope, h_fm, h_tm, d_fm, d_tm,
):
    i = pl.program_id(0)
    groups, feat, tokens = catt_ref.shape
    units = up_ref.shape[2]
    step = min(256, tokens)

    @pl.when(i == 0)
    def _():
        total = normed_one_ref[...] * gain_ref[:, 0:1]
        for g in range(groups):
            total = total + dot(wc_ref[g, :, :feat], catt_ref[g], 1, 0)
        acc[...] = total

        def body(at):
            normed, inv_std = norm_stats(acc[:, at])
            normed_two[:, at] = normed
            inv_two[:, at] = inv_std
            value = normed * gain_ref[:, 1:2]
            acc[:, at] = value
            h_fm[:, at] = value.astype(bf16)

        by_columns(tokens, body)
        h_tm[...] = h_fm[...].T

    @pl.when(i < groups)
    def _():
        for t in range(0, tokens, step):
            upper = dot(h_tm[t : t + step, :], up_ref[0], 1, 0)
            cdf = 0.5 * (1.0 + lax.erf(upper * 0.7071067811865476))
            density = jnp.exp(-0.5 * upper * upper) * 0.3989422804014327
            act[i, t : t + step, :] = (upper * cdf).astype(bf16)
            slope[i, t : t + step, :] = (cdf + upper * density).astype(bf16)
        acc[...] += dot(down_ref[0], act[i], 1, 1)

    @pl.when(i == groups - 1)
    def _():
        dg_three_ref[...] = jnp.zeros_like(dg_three_ref)
        dg_two_ref[...] = jnp.zeros_like(dg_two_ref)

        def body(at):
            normed, inv_std = norm_stats(acc[:, at])
            gain = gain_ref[:, 2:3]
            out_ref[:, at] = (normed * gain).astype(bf16)
            grad = cot_ref[:, at].astype(f32)
            dg_three_ref[...] += grad * normed
            value = norm_back(grad, gain, normed, inv_std)
            acc[:, at] = value
            d_fm[:, at] = value.astype(bf16)

        by_columns(tokens, body)
        d_tm[...] = d_fm[...].T

    @pl.when(i >= groups)
    def _():
        g = i - groups
        for t in range(0, tokens, step):
            at = slice(t, t + step)
            back = dot(d_tm[at, :], down_ref[0], 1, 0) * slope[g, at, :].astype(f32)
            slope[g, at, :] = back.astype(bf16)
        glarge_ref[0, :, units:] = dot(d_fm[...], act[g], 1, 0).astype(bf16)
        glarge_ref[0, :, :units] = dot(h_fm[...], slope[g], 1, 0).astype(bf16)
        acc[...] += dot(up_ref[0], slope[g], 1, 1)

    @pl.when(i == 2 * groups - 1)
    def _():
        def body(at):
            grad = acc[:, at]
            normed = normed_two[:, at]
            dg_two_ref[...] += grad * normed
            value = norm_back(grad, gain_ref[:, 1:2], normed, inv_two[:, at])
            dy_ref[:, at] = value
            dcross_ref[:, at] = value.astype(bf16)

        by_columns(tokens, body)
        low = dcross_ref[...]
        for g in range(groups):
            dcatt_ref[g] = dot(wc_ref[g, :, :feat], low, 0, 0).astype(bf16)


def middle(normed_one, catt, small, large, cot, gains):
    width, tokens = normed_one.shape
    groups, feat, _ = catt.shape
    units = large.shape[2] // 2
    lanes = min(128, tokens)

    def weight(kind):
        return pl.BlockSpec((1, width, units), lambda i: (i % groups, 0, kind))

    outs = [
        jax.ShapeDtypeStruct((width, tokens), bf16),
        jax.ShapeDtypeStruct(catt.shape, bf16),
        jax.ShapeDtypeStruct((width, tokens), f32),
        jax.ShapeDtypeStruct((width, tokens), bf16),
        jax.ShapeDtypeStruct(large.shape, bf16),
        jax.ShapeDtypeStruct((width, lanes), f32),
        jax.ShapeDtypeStruct((width, lanes), f32),
    ]
    specs = [whole(o) for o in outs]
    specs[4] = pl.BlockSpec(
        (1, width, 2 * units), lambda i: (jnp.maximum(i - groups, 0), 0, 0)
    )
    return pl.pallas_call(
        middle_kernel,
        grid=(2 * groups,),
        in_specs=[
            whole(normed_one),
            whole(catt),
            pl.BlockSpec((groups, width, 128), lambda i: (0, 0, 3)),
            weight(0),
            weight(1),
            whole(cot),
            whole(gains),
        ],
        out_specs=specs,
        out_shape=outs,
        scratch_shapes=[
            pltpu.VMEM((width, tokens), f32),
            pltpu.VMEM((width, tokens), f32),
            pltpu.VMEM((1, tokens), f32),
            pltpu.VMEM((groups, tokens, units), bf16),
            pltpu.VMEM((groups, tokens, units), bf16),
            pltpu.VMEM((width, tokens), bf16),
            pltpu.VMEM((tokens, width), bf16),
            pltpu.VMEM((width, tokens), bf16),
            pltpu.VMEM((tokens, width), bf16),
        ],
        compiler_params=kernel_params(),
        cost_estimate=pl.CostEstimate(
            flops=12 * groups * width * units * tokens, bytes_accessed=8 * large.size, transcendentals=0
        ),
        name="middle",
    )(normed_one, catt, small, large, large, cot, gains)


def before_self_kernel(
    dcq_ref, w_ref, dy_ref, normed_ref, inv_ref, gain_ref,
    dattn_ref, dlow_ref, dy_one_ref, dg_ref, acc,
):
    groups, feat, tokens = dcq_ref.shape
    rows = dattn_ref.shape[0]
    total = dy_ref[...]
    for g in range(groups):
        total = total + dot(w_ref[g, :, 3 * feat : 4 * feat], dcq_ref[g], 1, 0)
    acc[...] = total
    dg_ref[...] = jnp.zeros_like(dg_ref)

    def body(at):
        grad = acc[:, at]
        normed = normed_ref[:, at]
        dg_ref[...] += grad * normed
        value = norm_back(grad, gain_ref[:, 0:1], normed, inv_ref[:, at])
        dy_one_ref[:, at] = value
        dlow_ref[:, at] = value.astype(bf16)

    by_columns(tokens, body)
    low = dlow_ref[...]
    for g in range(groups):
        r, d = attn_place(g, rows)
        dattn_ref[r, d] = dot(w_ref[g, :, 2 * feat : 3 * feat], low, 0, 0).astype(bf16)


def before_self(d_cq, small, dy_two, normed_one, inv_one, gains, attn_shape):
    width, tokens = dy_two.shape
    args = (d_cq, small, dy_two, normed_one, inv_one, gains)
    outs = [
        jax.ShapeDtypeStruct(attn_shape, bf16),
        jax.ShapeDtypeStruct((width, tokens), bf16),
        jax.ShapeDtypeStruct((width, tokens), f32),
        jax.ShapeDtypeStruct((width, min(128, tokens)), f32),
    ]
    return pl.pallas_call(
        before_self_kernel,
        grid=(1,),
        in_specs=[whole(a) for a in args],
        out_specs=[whole(o) for o in outs],
        out_shape=outs,
        scratch_shapes=[pltpu.VMEM((width, tokens), f32)],
        compiler_params=kernel_params(),
        name="before_self",
    )(*args)


def small_grads_kernel(
    place_ref, w_ref, chosen_ref, dckv_ref, attn_ref, dcq_ref, catt_ref, dlow_ref, h_ref,
    dcross_ref, dg_one_ref, dg_two_ref, dg_three_ref, rest_ref, dchosen_ref, wide, acc, gain_cols,
    *, paired,
):
    g = pl.program_id(0)
    feat2 = dckv_ref.shape[1]
    feat = feat2 // 2
    count, width, tokens = chosen_ref.shape
    rows = count // 2

    @pl.when(g == 0)
    def _():
        side_by_side(chosen_ref, wide)
        col = lax.broadcasted_iota(jnp.int32, gain_cols.shape, 1)
        total = jnp.zeros(gain_cols.shape, f32)
        for k, ref in enumerate((dg_one_ref, dg_two_ref, dg_three_ref)):
            total = jnp.where(col == k, jnp.sum(ref[...], axis=1, keepdims=True), total)
        gain_cols[...] = total.astype(bf16)
        acc[...] = jnp.zeros_like(acc)

    grad = dckv_ref[0]
    acc[...] += dot(w_ref[0][:, :feat2], grad, 1, 0)
    rest_ref[0, :, :feat2] = dot(wide[...], grad, 1, 1).astype(bf16)
    pairs = ((dlow_ref, attn_ref[0, 0]), (h_ref, dcq_ref[0]), (dcross_ref, catt_ref[0]))
    for k, (left, right) in enumerate(pairs):
        at = feat2 + k * feat
        rest_ref[0, :, at : at + feat] = dot(left[...], right, 1, 1).astype(bf16)
    rest_ref[0, :, 5 * feat :] = gain_cols[...]

    @pl.when(g == pl.num_programs(0) - 1)
    def _():
        for n in range(count):
            at = n
            if paired:
                at = (place_ref[1] ^ (n % 2)) * rows + (place_ref[0] ^ (n // 2))
            dchosen_ref[at] = acc[:, n * tokens : (n + 1) * tokens].astype(bf16)


def small_grads(place, small, chosen, d_ckv, attn, d_cq, catt, d_low, h_low, d_cross, dgs, paired):
    groups, width, cols = small.shape
    _, feat2, keys = d_ckv.shape
    feat = feat2 // 2
    tokens = d_low.shape[1]
    rows = attn.shape[0]
    piece = pl.BlockSpec((1, feat, tokens), lambda g, p: (g, 0, 0))
    return pl.pallas_call(
        functools.partial(small_grads_kernel, paired=paired),
        grid_spec=pltpu.PrefetchScalarGridSpec(
            num_scalar_prefetch=1,
            grid=(groups,),
            in_specs=[
                pl.BlockSpec((1, width, 2 * 128), lambda g, p: (g, 0, 0)),
                whole(chosen),
                pl.BlockSpec((1, feat2, keys), lambda g, p: (g, 0, 0)),
                pl.BlockSpec((1, 1, feat, tokens), lambda g, p: (g % rows, g // rows, 0, 0)),
                piece,
                piece,
                whole(d_low),
                whole(h_low),
                whole(d_cross),
            ]
            + [whole(v) for v in dgs],
            out_specs=[pl.BlockSpec((1, width, cols), lambda g, p: (g, 0, 0)), whole(chosen)],
            scratch_shapes=[
                pltpu.VMEM((width, keys), bf16),
                pltpu.VMEM((width, keys), f32),
                pltpu.VMEM((width, cols - 5 * feat), bf16),
            ],
        ),
        out_shape=[
            jax.ShapeDtypeStruct(small.shape, bf16),
            jax.ShapeDtypeStruct(chosen.shape, bf16),
        ],
        compiler_params=kernel_params(),
        name="small_grads",
    )(place, small, chosen, d_ckv, attn, d_cq, catt, d_low, h_low, d_cross, *dgs)


def mm(spec, left, right):
    return jnp.einsum(spec, left, right, preferred_element_type=f32)


def per_device(
    x_in, prefix, enc_bank, bank_rows, w_qkv, w_out, w_cross_q, w_cross_kv, w_cross_out,
    w_up, w_down, ln_gains, out_grad,
):
    dp, rows, cols = lax.axis_size("dp"), lax.axis_size("row"), lax.axis_size("col")
    d_pos, r_pos, c_pos = lax.axis_index("dp"), lax.axis_index("row"), lax.axis_index("col")
    own_seqs, part_width, row_len = x_in.shape
    seqs = own_seqs * dp
    sub = cols // seqs
    parts = dp * sub
    width = part_width * cols
    tokens = row_len // parts
    heads = w_qkv.shape[2]
    feat = heads * HALF
    units = w_up.shape[1]
    odd = (r_pos % 2) == 1
    seq_pos = c_pos // sub
    part_pos = d_pos * sub + c_pos % sub
    groups = [[s * sub + k for k in range(sub)] for s in range(seqs)]
    everywhere = ("dp", "row", "col")
    swap = [(0, 1), (1, 0)]
    first_core = d_pos == 0

    def flip(value):
        return jnp.where(odd, value[:, :, ::-1], value)

    def swap_cores(value):
        take = value.shape[-1] // parts
        if parts == 2:
            low, high = value[..., :take], value[..., take:]
            upper = first_core == odd
            got = lax.ppermute(jnp.where(upper, low, high), "dp", swap)
            kept = jnp.where(upper, high, low)
            value = jnp.concatenate(
                [jnp.where(first_core, kept, got), jnp.where(first_core, got, kept)], axis=0
            )
        else:
            value = flip(value.reshape(own_seqs, part_width, parts, take))
            value = value.reshape(own_seqs, part_width, dp, sub, take)
            value = lax.all_to_all(value, "dp", 2, 0, tiled=True)
            value = value.reshape(seqs, part_width, sub, take).transpose(0, 2, 1, 3)
        return value.reshape(cols, part_width, take)

    def across_cols(value):
        return lax.all_to_all(value, "col", 0, 0, tiled=True).reshape(width, value.shape[-1])

    def to_tokens(value):
        return across_cols(swap_cores(value))

    def row_gather(value):
        if rows != 4:
            every = lax.all_gather(value, "row", axis=0)
            return [lax.dynamic_index_in_dim(every, r_pos ^ k, 0, False) for k in range(rows)]

        def send(v, k):
            return lax.ppermute(v, "row", [(i, i ^ k) for i in range(rows)])

        near_one, near_two = send(value, 1), send(value, 2)
        half = value.shape[0] // 2
        far = jnp.concatenate([send(near_two[:half], 1), send(near_one[half:], 2)], axis=0)
        return [value, near_one, near_two, far]

    def to_home(value):
        take = value.shape[-1]
        value = lax.all_to_all(value.reshape(cols, part_width, take), "col", 0, 0, tiled=True)
        if parts == 2:
            early, late = value[:own_seqs], value[own_seqs:]
            got = lax.ppermute(jnp.where(first_core, late, early), "dp", swap)
            kept = jnp.where(first_core, early, late)
            upper = first_core == odd
            return jnp.concatenate(
                [jnp.where(upper, got, kept), jnp.where(upper, kept, got)], axis=-1
            )
        value = value.reshape(seqs, sub, part_width, take).transpose(0, 2, 1, 3)
        value = value.reshape(seqs, part_width, 1, sub, take)
        value = lax.all_to_all(value, "dp", 0, 2, tiled=True)
        value = flip(value.reshape(own_seqs, part_width, parts, take))
        return value.reshape(own_seqs, part_width, parts * take)

    place = jnp.stack([r_pos, d_pos]).astype(jnp.int32)
    qkv = jnp.pad(w_qkv.reshape(part_width, 3 * feat), ((0, 0), (0, 384 - 3 * feat)))
    near = lax.all_gather(qkv, ("dp", "col"), axis=0).reshape(dp, width, qkv.shape[1])
    x_swapped = swap_cores(x_in)
    x_own = across_cols(x_swapped)
    x_rows = row_gather(x_own)
    spare = 512 - 5 * feat
    small = jnp.concatenate(
        [
            w_cross_kv.reshape(part_width, 2 * feat),
            w_out.reshape(feat, part_width).T,
            w_cross_q.reshape(part_width, feat),
            w_cross_out.reshape(feat, part_width).T,
            jnp.zeros((part_width, spare), bf16),
        ],
        axis=1,
    )
    blocks = dp * rows

    def gather_all(value):
        value = lax.all_gather(value, everywhere, axis=0)
        return value.reshape(blocks, width, value.shape[-1])

    small, _ = lax.optimization_barrier((small, x_swapped))
    small_all = gather_all(small)
    large, _ = lax.optimization_barrier((jnp.concatenate([w_up, w_down.T], axis=1), x_own))
    large_all = gather_all(large)
    gains = lax.all_gather(ln_gains.astype(f32).T, "col", axis=0, tiled=True)

    query, kv_own = project(place, near, x_rows, feat)
    query = query.reshape(rows, dp, heads, HALF, tokens)
    kv_own = kv_own.reshape(rows, dp, 2, heads, HALF, tokens)

    def index_of(row, part):
        return jnp.where(row % 2 == 1, parts - 1 - part, part) + row * parts

    row_ids = jnp.arange(rows, dtype=jnp.int32)
    if sub == 1:
        kv_list = [kv_own, lax.ppermute(kv_own, "dp", swap)]
        owners = [part_pos, 1 - part_pos]
    else:
        kv_all = lax.all_gather(kv_own, "col", axis=0, axis_index_groups=groups)
        kv_all = lax.all_gather(kv_all, "dp", axis=0).reshape((parts,) + kv_own.shape)
        kv_list = [kv_all[j] for j in range(parts)]
        owners = list(range(parts))
    q_start = index_of(row_ids, part_pos) * tokens
    places = [index_of(row_ids, owner) for owner in owners]
    seq_prefix = lax.all_gather(prefix, "dp", axis=0, tiled=True)[seq_pos]
    meta = jnp.concatenate([seq_prefix[None], q_start] + places).astype(jnp.int32)
    mixed, lse = attend(meta, query, kv_list, True, "self_attention")
    attn = lax.all_to_all(mixed, "row", 0, 0, tiled=True).reshape(rows, dp, feat, tokens)
    normed_one, inv_one, h_low, cross_q = after_self(x_own, attn, small_all, gains, feat)
    cross_q = cross_q.reshape(1, dp, rows, heads, HALF, tokens)

    picked = bank_rows.shape[1] // rows
    row_pick = lax.dynamic_slice_in_dim(bank_rows, r_pos * picked, picked, 1)
    bank_ids = jnp.arange(enc_bank.shape[2], dtype=jnp.int32)
    hot = (bank_ids[None, :, None] == row_pick[:, None, :]).astype(bf16)
    chosen = to_tokens(mm("swn,snp->swp", enc_bank, hot).astype(bf16))
    c_tokens = chosen.shape[1]
    if sub > 1:
        chosen = lax.all_gather(chosen, "col", axis=0, axis_index_groups=groups)
        chosen = lax.all_gather(chosen, ("dp", "row"), axis=0)
        chosen = chosen.reshape(blocks * sub, width, c_tokens)
    else:
        pair = jnp.stack([chosen, lax.ppermute(chosen, "dp", swap)])
        chosen = jnp.concatenate(row_gather(pair), axis=0)
    ckv = cross_kv(small_all, chosen, feat)
    ckv = ckv.reshape(1, dp, rows, 2, heads, HALF, ckv.shape[-1])
    catt, lse_cross = attend(meta, cross_q, [ckv], False, "cross_attention")
    catt_flat = catt.reshape(blocks, feat, tokens)

    cot = to_tokens(out_grad)
    block_out, d_catt, dy_two, d_cross, g_large, dg_two, dg_three = middle(
        normed_one, catt_flat, small_all, large_all, cot, gains
    )
    block_out = to_home(block_out)

    def scatter(value):
        value = value.reshape(dp, rows, cols, part_width, value.shape[-1])
        for name in everywhere:
            value = lax.psum_scatter(value, name, scatter_dimension=0, tiled=False)
        return value

    large_grad = scatter(g_large)
    d_cq, d_ckv = attend_back(
        meta, cross_q, [ckv], d_catt.reshape(catt.shape), catt, lse_cross, False, [bf16],
        "cross_attention_back",
    )
    d_cq = d_cq.reshape(blocks, feat, tokens)
    d_ckv = d_ckv.reshape(blocks, 2 * feat, d_ckv.shape[-1])
    d_attn, d_low, dy_one, dg_one = before_self(
        d_cq, small_all, dy_two, normed_one, inv_one, gains, attn.shape
    )
    d_mixed = lax.all_to_all(d_attn, "row", 0, 0, tiled=True).reshape(mixed.shape)
    rest, d_chosen = small_grads(
        place, small_all, chosen, d_ckv, attn, d_cq, catt_flat, d_low, h_low, d_cross,
        (dg_one, dg_two, dg_three), sub == 1,
    )

    types = [f32] + [bf16] * (len(kv_list) - 1) if sub == 1 else [bf16] * len(kv_list)
    d_query, *d_kv = attend_back(
        meta, query, kv_list, d_mixed, mixed, lse, True, types, "self_attention_back"
    )
    d_query, large_grad, d_chosen, rest = lax.optimization_barrier(
        (d_query, large_grad, d_chosen, rest)
    )
    if sub == 1:
        d_kv = [d_kv[0], lax.ppermute(d_kv[1], "dp", swap)]
    else:
        d_kv = jnp.stack(d_kv).reshape((dp, sub) + kv_own.shape)
        d_kv = lax.psum_scatter(d_kv, "dp", scatter_dimension=0, tiled=True)
        d_kv = lax.psum_scatter(
            d_kv, "col", scatter_dimension=1, tiled=True, axis_index_groups=groups
        )
        d_kv = [d_kv]
    kv_shape = (rows, dp, 2, feat, tokens)
    d_kv = [value.reshape(kv_shape) for value in d_kv]
    dx_part, g_qkv = project_back(
        place, near, x_rows, d_query.reshape(rows, dp, feat, tokens), d_kv
    )
    dx_part = lax.all_to_all(dx_part, "row", 0, 0, tiled=True)
    dx = dy_one + jnp.sum(dx_part.astype(f32), axis=0)
    x_grad = to_home(dx.astype(bf16)).astype(f32)

    d_chosen = d_chosen.reshape(dp, rows, sub, width, c_tokens)
    d_chosen = lax.psum_scatter(d_chosen, "dp", scatter_dimension=0, tiled=False)
    d_chosen = lax.psum_scatter(d_chosen, "row", scatter_dimension=0, tiled=False)
    if sub > 1:
        d_chosen = lax.psum_scatter(
            d_chosen, "col", scatter_dimension=0, tiled=True, axis_index_groups=groups
        )
    d_chosen = d_chosen.reshape(width, c_tokens)
    d_chosen = lax.all_gather(to_home(d_chosen), "row", axis=2, tiled=True)
    hot_all = (bank_rows[:, :, None] == bank_ids[None, None, :]).astype(bf16)
    bank_grad = mm("swp,spn->swn", d_chosen, hot_all)

    large_grad = large_grad.astype(f32)
    rest = scatter(rest).astype(f32)
    qkv_grad = g_qkv.reshape(dp, cols, part_width, g_qkv.shape[-1])
    qkv_grad = lax.psum_scatter(qkv_grad, "dp", scatter_dimension=0, tiled=False)
    qkv_grad = lax.psum_scatter(qkv_grad, "col", scatter_dimension=0, tiled=False).astype(f32)

    return (
        block_out,
        x_grad,
        bank_grad,
        qkv_grad[:, : 3 * feat].reshape(w_qkv.shape),
        rest[:, 2 * feat : 3 * feat].T.reshape(w_out.shape),
        rest[:, 3 * feat : 4 * feat].reshape(w_cross_q.shape),
        rest[:, : 2 * feat].reshape(w_cross_kv.shape),
        rest[:, 4 * feat : 5 * feat].T.reshape(w_cross_out.shape),
        large_grad[:, :units],
        large_grad[:, units:].T,
        rest[:, 5 * feat : 5 * feat + 3].T,
    )


def solution(mesh):
    placed = (
        P("dp", "col", "row"),
        P("dp"),
        P("dp", "col", None),
        P("dp", None),
        P("col", None, "row", "dp"),
        P("row", "dp", "col"),
        P("col", "row", "dp"),
        P("col", None, "row", "dp"),
        P("row", "dp", "col"),
        P("col", ("dp", "row")),
        P(("dp", "row"), "col"),
        P(None, "col"),
        P("dp", "col", "row"),
    )
    return jax.shard_map(
        per_device,
        mesh=mesh,
        in_specs=placed,
        out_specs=(
            P("dp", "col", "row"),
            P("dp", "col", "row"),
            P("dp", "col", None),
            P("col", None, "row", "dp"),
            P("row", "dp", "col"),
            P("col", "row", "dp"),
            P("col", None, "row", "dp"),
            P("row", "dp", "col"),
            P("col", ("dp", "row")),
            P(("dp", "row"), "col"),
            P(None, "col"),
        ),
        check_vma=False,
    )
```

```python
import functools

import jax
import jax.numpy as jnp
from jax import lax
from jax.experimental import pallas as pl
from jax.experimental.pallas import tpu as pltpu
from jax.sharding import PartitionSpec as P

bf16 = jnp.bfloat16
f32 = jnp.float32
HD = 64
HALF = 32
NORM_EPS = 1e-05
NEG = -1e30
LIMIT = 90.0
LN2 = 0.6931471805599453
LOG2E = 1.4426950408889634
KB = 512


def dot(left, right, left_dim, right_dim):
    return lax.dot_general(
        left, right, (((left_dim,), (right_dim,)), ((), ())), preferred_element_type=f32
    )


def ones_rows(count, shape, dim):
    return jnp.where(lax.broadcasted_iota(jnp.int32, shape, dim) < count, 1.0, 0.0).astype(bf16)


def allowed_block(meta, i, start, width, cols):
    k_pos = start + lax.broadcasted_iota(jnp.int32, (width, cols), 0)
    q_pos = meta[1 + i] + lax.broadcasted_iota(jnp.int32, (1, cols), 1)
    return k_pos <= jnp.maximum(q_pos, meta[0] - 1)


def block_range(meta, i, cols):
    full = jnp.maximum(meta[1 + i], meta[0]) // KB
    total = (jnp.maximum(meta[1 + i] + cols, meta[0]) + KB - 1) // KB
    return full, total


def over_keys(meta, i, cols, keys, masked, step, carry):
    if not masked:
        for start in range(0, keys, KB):
            carry = step(start, carry, False, KB)
        return carry
    full, total = block_range(meta, i, cols)
    pairs = full // 2
    carry = lax.fori_loop(0, pairs, lambda j, c: step(j * 2 * KB, c, False, 2 * KB), carry)
    carry = lax.fori_loop(2 * pairs, full, lambda j, c: step(j * KB, c, False, KB), carry)
    return lax.fori_loop(full, total, lambda j, c: step(j * KB, c, True, KB), carry)


def pieces(kv_refs, masked):
    out = []
    for ref in kv_refs:
        count = ref.shape[0]
        for b in range(count):
            out.append((ref, b))
    return out


def piece_start(meta, n_query, index, length, masked):
    if masked:
        return pl.multiple_of(meta[1 + n_query + index] * length, length)
    return index * length


def attend_kernel(*refs, sources, n_query, masked):
    meta, q_ref = refs[:2]
    kv_refs = refs[2 : 2 + sources]
    o_ref, l_ref, key_rows, val_cols = refs[2 + sources :]
    i = pl.program_id(1)
    cols = q_ref.shape[-1]
    keys = val_cols.shape[-1]

    @pl.when(i == 0)
    def _():
        key_rows[:, HD:] = ones_rows(1, (keys, 16), 1)
        val_cols[HD:, :] = ones_rows(1, (16, keys), 0)
        for index, (ref, b) in enumerate(pieces(kv_refs, masked)):
            length = ref.shape[-1]
            at = pl.ds(piece_start(meta, n_query, index, length, masked), length)
            key_rows[at, :HD] = ref[b, :, 0, 0].reshape(HD, length).T
            val_cols[:HD, at] = ref[b, :, 1, 0].reshape(HD, length)

    query = q_ref[0, :, 0].reshape(HD, cols)
    first = dot(key_rows[0:128, :HD], query, 1, 0)
    shift = jnp.max(first, axis=0, keepdims=True).astype(bf16).astype(f32)
    row = lax.broadcasted_iota(jnp.int32, (16, cols), 0)
    query_more = jnp.concatenate([query, jnp.where(row == 0, -shift, 0.0).astype(bf16)], axis=0)

    def step(start, carry, mask, width):
        top, acc = carry
        at = pl.ds(pl.multiple_of(start, KB), width)
        scores = dot(key_rows[at, :], query_more, 1, 0)
        if mask:
            scores = jnp.where(allowed_block(meta, i, start, width, cols), scores, NEG)
        top = jnp.maximum(top, jnp.max(scores, axis=0, keepdims=True))
        acc = acc + dot(val_cols[:, at], jnp.exp2(scores).astype(bf16), 1, 0)
        return top, acc

    def put(shift, acc):
        total = acc[HD : HD + 1, :]
        mixed = (acc[:HD] * (1.0 / total)).astype(bf16)
        o_ref[0, :, 0] = mixed.reshape(2, HALF, cols)
        l_ref[0, 0] = shift + jnp.log2(total)

    start = (jnp.full((1, cols), NEG, f32), jnp.zeros((HD + 16, cols), f32))
    top, acc = over_keys(meta, i, cols, keys, masked, step, start)
    put(shift, acc)

    @pl.when(jnp.max(top) > LIMIT)
    def _():
        def careful(j, carry):
            high, acc = carry
            at = pl.ds(pl.multiple_of(j * KB, KB), KB)
            scores = dot(key_rows[at, :HD], query, 1, 0)
            if masked:
                scores = jnp.where(allowed_block(meta, i, j * KB, KB, cols), scores, NEG)
            new = jnp.maximum(high, jnp.max(scores, axis=0, keepdims=True))
            part = dot(val_cols[:, at], jnp.exp2(scores - new).astype(bf16), 1, 0)
            return new, acc * jnp.exp2(high - new) + part

        total = block_range(meta, i, cols)[1] if masked else keys // KB
        put(*lax.fori_loop(0, total, careful, start))


def attend_back_kernel(*refs, sources, n_query, masked):
    meta, q_ref = refs[:2]
    kv_refs = refs[2 : 2 + sources]
    g_ref, o_ref, l_ref = refs[2 + sources : 5 + sources]
    dq_ref = refs[5 + sources]
    dkv_refs = refs[6 + sources : 6 + 2 * sources]
    key_rows, val_rows, key_cols, dk_acc, dv_acc = refs[6 + 2 * sources :]
    i = pl.program_id(1)
    cols = q_ref.shape[-1]
    keys = key_cols.shape[-1]

    @pl.when(i == 0)
    def _():
        key_rows[:, HD:] = ones_rows(3, (keys, 16), 1)
        val_rows[:, HD:] = ones_rows(3, (keys, 16), 1)
        for index, (ref, b) in enumerate(pieces(kv_refs, masked)):
            length = ref.shape[-1]
            at = pl.ds(piece_start(meta, n_query, index, length, masked), length)
            k_part = ref[b, :, 0, 0].reshape(HD, length)
            key_cols[:, at] = k_part
            key_rows[at, :HD] = k_part.T
            val_rows[at, :HD] = ref[b, :, 1, 0].reshape(HD, length).T
        dk_acc[...] = jnp.zeros_like(dk_acc)
        dv_acc[...] = jnp.zeros_like(dv_acc)

    query = q_ref[0, :, 0].reshape(HD, cols)
    grad = g_ref[0, :, 0].reshape(HD, cols)
    delta = jnp.sum(
        grad.astype(f32) * o_ref[0, :, 0].reshape(HD, cols).astype(f32), axis=0, keepdims=True
    )

    def with_shift(value, shift):
        high = shift.astype(bf16).astype(f32)
        mid = (shift - high).astype(bf16).astype(f32)
        low = shift - high - mid
        row = lax.broadcasted_iota(jnp.int32, (16, cols), 0)
        more = jnp.where(row == 0, -high, jnp.where(row == 1, -mid, jnp.where(row == 2, -low, 0.0)))
        return jnp.concatenate([value, more.astype(bf16)], axis=0)

    query_more = with_shift(query, l_ref[0, 0])
    grad_more = with_shift(grad, delta)

    def step(start, dq, mask, width):
        at = pl.ds(pl.multiple_of(start, KB), width)
        scores = dot(key_rows[at, :], query_more, 1, 0)
        if mask:
            scores = jnp.where(allowed_block(meta, i, start, width, cols), scores, NEG)
        probs = jnp.exp2(scores)
        grad_scores = (probs * dot(val_rows[at, :], grad_more, 1, 0)).astype(bf16)
        dv_acc[:, at] += dot(grad, probs.astype(bf16), 1, 1)
        dk_acc[:, at] += dot(query, grad_scores, 1, 1)
        return dq + dot(key_cols[:, at], grad_scores, 1, 0)

    dq = over_keys(meta, i, cols, keys, masked, step, jnp.zeros((HD, cols), f32))
    dq_ref[0, :, 0] = (dq * 0.125).astype(bf16).reshape(2, HALF, cols)

    @pl.when(i == n_query - 1)
    def _():
        for index, (ref, b) in enumerate(pieces(dkv_refs, masked)):
            length = ref.shape[-1]
            at = pl.ds(piece_start(meta, n_query, index, length, masked), length)
            ref[b, :, 0, 0] = (dk_acc[:, at] * LN2).astype(ref.dtype).reshape(2, HALF, length)
            ref[b, :, 1, 0] = dv_acc[:, at].astype(ref.dtype).reshape(2, HALF, length)


def attention_specs(query, kv_list, masked):
    cols = query.shape[-1]
    if masked:
        n_query, _, heads = query.shape[:3]
        grid = (heads, n_query)
        q_spec = pl.BlockSpec((1, 2, 1, HALF, cols), lambda h, i, m: (i, 0, h, 0, 0))
        kv_specs = [
            pl.BlockSpec(kv.shape[:3] + (1,) + kv.shape[4:], lambda h, i, m: (0, 0, 0, h, 0, 0))
            for kv in kv_list
        ]
        l_spec = pl.BlockSpec((1, 1, 1, cols), lambda h, i, m: (h, i, 0, 0))
        l_shape = (heads, n_query, 1, cols)
        keys = sum(kv.shape[0] * kv.shape[-1] for kv in kv_list)
    else:
        n_query = 1
        _, _, rows, heads = query.shape[:4]
        grid = (rows * heads, 1)
        q_spec = pl.BlockSpec(
            (1, 2, None, 1, HALF, cols), lambda g, i, m: (0, 0, g // heads, g % heads, 0, 0)
        )
        kv_specs = [
            pl.BlockSpec(
                (kv.shape[0], 2, None, 2, 1) + kv.shape[5:],
                lambda g, i, m: (0, 0, g // heads, 0, g % heads, 0, 0),
            )
            for kv in kv_list
        ]
        l_spec = pl.BlockSpec((1, 1, 1, cols), lambda g, i, m: (g, 0, 0, 0))
        l_shape = (rows * heads, 1, 1, cols)
        keys = sum(kv.shape[0] * kv.shape[-1] for kv in kv_list)
    return n_query, grid, q_spec, kv_specs, l_spec, l_shape, keys


def cost(query, keys, dots):
    pairs = query.size // HD * keys
    return pl.CostEstimate(
        flops=2 * pairs * 256 * dots // 2, bytes_accessed=query.size * 16, transcendentals=pairs
    )


def attend(meta, query, kv_list, masked, name):
    n_query, grid, q_spec, kv_specs, l_spec, l_shape, keys = attention_specs(query, kv_list, masked)
    return pl.pallas_call(
        functools.partial(attend_kernel, sources=len(kv_list), n_query=n_query, masked=masked),
        grid_spec=pltpu.PrefetchScalarGridSpec(
            num_scalar_prefetch=1,
            grid=grid,
            in_specs=[q_spec] + kv_specs,
            out_specs=[q_spec, l_spec],
            scratch_shapes=[pltpu.VMEM((keys, HD + 16), bf16), pltpu.VMEM((HD + 16, keys), bf16)],
        ),
        out_shape=[
            jax.ShapeDtypeStruct(query.shape, bf16),
            jax.ShapeDtypeStruct(l_shape, f32),
        ],
        compiler_params=pltpu.CompilerParams(vmem_limit_bytes=48 << 20),
        cost_estimate=cost(query, keys, 2),
        name=name,
    )(meta, query, *kv_list)


def attend_back(meta, query, kv_list, grad, out, lse, masked, types, name):
    n_query, grid, q_spec, kv_specs, l_spec, l_shape, keys = attention_specs(query, kv_list, masked)
    return pl.pallas_call(
        functools.partial(attend_back_kernel, sources=len(kv_list), n_query=n_query, masked=masked),
        grid_spec=pltpu.PrefetchScalarGridSpec(
            num_scalar_prefetch=1,
            grid=grid,
            in_specs=[q_spec] + kv_specs + [q_spec, q_spec, l_spec],
            out_specs=[q_spec] + kv_specs,
            scratch_shapes=[
                pltpu.VMEM((keys, HD + 16), bf16),
                pltpu.VMEM((keys, HD + 16), bf16),
                pltpu.VMEM((HD, keys), bf16),
                pltpu.VMEM((HD, keys), f32),
                pltpu.VMEM((HD, keys), f32),
            ],
        ),
        out_shape=[jax.ShapeDtypeStruct(query.shape, bf16)]
        + [jax.ShapeDtypeStruct(kv.shape, t) for kv, t in zip(kv_list, types)],
        compiler_params=pltpu.CompilerParams(vmem_limit_bytes=48 << 20),
        cost_estimate=cost(query, keys, 5),
        name=name,
    )(meta, query, *kv_list, grad, out, lse)


def gain_of(w_ref, first, k):
    return w_ref[0, :, first + k : first + k + 1].astype(f32)


def other_first(i, place, half):
    return jnp.where(i < half, (1 - place[1]) * half + i, place[1] * half + i - half)


def kernel_params():
    return pltpu.CompilerParams(vmem_limit_bytes=60 << 20)


def whole(value):
    return pl.BlockSpec(value.shape, lambda *i: (0,) * value.ndim)


def by_columns(count, body):
    step = min(128, count)

    def one(j, carry):
        body(pl.ds(pl.multiple_of(j * step, step), step))
        return carry

    lax.fori_loop(0, count // step, one, 0)


def norm_stats(resid):
    width = resid.shape[0]
    mean = jnp.sum(resid, 0, keepdims=True) / width
    square = jnp.sum(resid * resid, 0, keepdims=True) / width
    inv_std = lax.rsqrt(square - mean * mean + NORM_EPS)
    return (resid - mean) * inv_std, inv_std


def norm_back(grad, gain, normed, inv_std):
    width = grad.shape[0]
    scaled = grad * gain
    total = jnp.sum(scaled, 0, keepdims=True) / width
    cross = jnp.sum(scaled * normed, 0, keepdims=True) / width
    return inv_std * (scaled - total - normed * cross)


def project_kernel(place_ref, near_ref, *refs, rows):
    x_refs = refs[:rows]
    q_ref, kv_ref, near_t = refs[rows:]
    feat = q_ref.shape[2]
    step = pl.program_id(0)

    @pl.when(step == 0)
    def _():
        for d in range(near_ref.shape[0]):
            near_t[d] = near_ref[d].T

    for k, x_ref in enumerate(x_refs):

        @pl.when(step == k)
        def _():
            for d in range(near_ref.shape[0]):
                proj = dot(near_t[d, : 3 * feat, :], x_ref[...], 1, 0)
                q_ref[0, d] = (proj[:feat] * (0.125 * LOG2E)).astype(bf16)
                kv_ref[0, d, 0] = proj[feat : 2 * feat].astype(bf16)
                kv_ref[0, d, 1] = proj[2 * feat :].astype(bf16)


def project(place, near, x_rows, feat):
    dp, width, cols = near.shape
    rows = len(x_rows)
    tokens = x_rows[0].shape[1]
    return pl.pallas_call(
        functools.partial(project_kernel, rows=rows),
        grid_spec=pltpu.PrefetchScalarGridSpec(
            num_scalar_prefetch=1,
            grid=(rows,),
            in_specs=[whole(near)] + [whole(x) for x in x_rows],
            out_specs=[
                pl.BlockSpec((1, dp, feat, tokens), lambda k, p: (p[0] ^ k, 0, 0, 0)),
                pl.BlockSpec((1, dp, 2, feat, tokens), lambda k, p: (p[0] ^ k, 0, 0, 0, 0)),
            ],
            scratch_shapes=[pltpu.VMEM((dp, cols, width), bf16)],
        ),
        out_shape=[
            jax.ShapeDtypeStruct((rows, dp, feat, tokens), bf16),
            jax.ShapeDtypeStruct((rows, dp, 2, feat, tokens), bf16),
        ],
        compiler_params=kernel_params(),
        name="project",
    )(place, near, *x_rows)


def project_back_kernel(place_ref, near_ref, *refs, rows, sources):
    x_refs, dq_ref = refs[:rows], refs[rows]
    dkv_refs = refs[rows + 1 : rows + 1 + sources]
    dx_ref, gother_ref, gown_ref, acc = refs[rows + 1 + sources :]
    step = pl.program_id(0)
    feat = dq_ref.shape[2]

    @pl.when(step == 0)
    def _():
        acc[...] = jnp.zeros_like(acc)

    for k, x_ref in enumerate(x_refs):

        @pl.when(step == k)
        def _():
            total = None
            for d in range(near_ref.shape[0]):
                parts = [dq_ref[0, d]]
                for kind in range(2):
                    value = sum(ref[0, d, kind].astype(f32) for ref in dkv_refs)
                    parts.append(value.astype(bf16))
                grad = jnp.concatenate(parts, axis=0)
                acc[d, :, : 3 * feat] += dot(x_ref[...], grad, 1, 1)
                part = dot(near_ref[d, :, : 3 * feat], grad, 1, 0)
                total = part if total is None else total + part
            dx_ref[0] = total.astype(bf16)

    @pl.when(step == rows - 1)
    def _():
        gown_ref[...] = acc[place_ref[1]].astype(bf16)
        gother_ref[...] = acc[1 - place_ref[1]].astype(bf16)


def project_back(place, near, x_rows, d_query, d_kv):
    dp, width, cols = near.shape
    rows = len(x_rows)
    tokens = x_rows[0].shape[1]
    feat = d_query.shape[2]
    kv_spec = pl.BlockSpec((1, dp, 2, feat, tokens), lambda k, p: (p[0] ^ k, 0, 0, 0, 0))
    half = jax.ShapeDtypeStruct((width, cols), bf16)
    return pl.pallas_call(
        functools.partial(project_back_kernel, rows=rows, sources=len(d_kv)),
        grid_spec=pltpu.PrefetchScalarGridSpec(
            num_scalar_prefetch=1,
            grid=(rows,),
            in_specs=[whole(near)]
            + [whole(x) for x in x_rows]
            + [pl.BlockSpec((1, dp, feat, tokens), lambda k, p: (p[0] ^ k, 0, 0, 0))]
            + [kv_spec] * len(d_kv),
            out_specs=[
                pl.BlockSpec((1, width, tokens), lambda k, p: (p[0] ^ k, 0, 0)),
                whole(half),
                whole(half),
            ],
            scratch_shapes=[pltpu.VMEM(near.shape, f32)],
        ),
        out_shape=[
            jax.ShapeDtypeStruct((rows, width, tokens), bf16),
            half,
            half,
        ],
        compiler_params=kernel_params(),
        name="project_back",
    )(place, near, *x_rows, d_query, *d_kv)


def side_by_side(chosen_ref, wide):
    count, _, tokens = chosen_ref.shape
    for n in range(count):
        wide[:, n * tokens : (n + 1) * tokens] = chosen_ref[n]


def cross_kv_kernel(w_ref, chosen_ref, o_ref, wide):
    @pl.when(pl.program_id(0) == 0)
    def _():
        side_by_side(chosen_ref, wide)

    weight = w_ref[0][:, : o_ref.shape[1]].T
    o_ref[0] = dot(weight, wide[...], 1, 0).astype(bf16)


def cross_kv(small, chosen, feat):
    groups, width, cols = small.shape
    keys = chosen.shape[0] * chosen.shape[2]
    return pl.pallas_call(
        cross_kv_kernel,
        grid=(groups,),
        in_specs=[pl.BlockSpec((1, width, 2 * 128), lambda g: (g, 0, 0)), whole(chosen)],
        out_specs=pl.BlockSpec((1, 2 * feat, keys), lambda g: (g, 0, 0)),
        out_shape=jax.ShapeDtypeStruct((groups, 2 * feat, keys), bf16),
        scratch_shapes=[pltpu.VMEM((width, keys), bf16)],
        compiler_params=kernel_params(),
        name="cross_kv",
    )(small, chosen)


def attn_place(g, rows):
    return g % rows, g // rows


def after_self_kernel(x_ref, attn_ref, w_ref, normed_ref, inv_ref, low_ref, cq_ref, acc):
    groups, feat, tokens = cq_ref.shape
    rows = attn_ref.shape[0]
    total = x_ref[...].astype(f32)
    for g in range(groups):
        r, d = attn_place(g, rows)
        total = total + dot(w_ref[g, :, 2 * feat : 3 * feat], attn_ref[r, d], 1, 0)
    acc[...] = total

    def body(at):
        normed, inv_std = norm_stats(acc[:, at])
        normed_ref[:, at] = normed
        inv_ref[:, at] = inv_std
        low_ref[:, at] = (normed * gain_of(w_ref, 5 * feat, 0)).astype(bf16)

    by_columns(tokens, body)
    low = low_ref[...]
    for g in range(groups):
        query = dot(w_ref[g, :, 3 * feat : 4 * feat], low, 0, 0)
        cq_ref[g] = (query * (0.125 * LOG2E)).astype(bf16)


def after_self(x_own, attn, small, feat):
    width, tokens = x_own.shape
    groups = small.shape[0]
    args = (x_own, attn, small)
    outs = [
        jax.ShapeDtypeStruct((width, tokens), f32),
        jax.ShapeDtypeStruct((1, tokens), f32),
        jax.ShapeDtypeStruct((width, tokens), bf16),
        jax.ShapeDtypeStruct((groups, feat, tokens), bf16),
    ]
    return pl.pallas_call(
        after_self_kernel,
        grid=(1,),
        in_specs=[whole(a) for a in args],
        out_specs=[whole(o) for o in outs],
        out_shape=outs,
        scratch_shapes=[pltpu.VMEM((width, tokens), f32)],
        compiler_params=kernel_params(),
        name="after_self",
    )(*args)


def middle_kernel(
    place_ref, normed_one_ref, catt_ref, wc_ref, up_ref, down_ref, cot_ref,
    out_ref, dcatt_ref, dy_ref, dcross_ref, gother_ref, gown_ref, dg_two_ref, dg_three_ref,
    acc, normed_two, inv_two, act, slope, h_fm, h_tm, d_fm, d_tm,
):
    i = pl.program_id(0)
    groups, feat, tokens = catt_ref.shape
    half = groups // 2
    units = up_ref.shape[2]
    step = min(256, tokens)

    @pl.when(i == 0)
    def _():
        total = normed_one_ref[...] * gain_of(wc_ref, feat, 0)
        for g in range(groups):
            total = total + dot(wc_ref[g, :, :feat], catt_ref[g], 1, 0)
        acc[...] = total

        def body(at):
            normed, inv_std = norm_stats(acc[:, at])
            normed_two[:, at] = normed
            inv_two[:, at] = inv_std
            value = normed * gain_of(wc_ref, feat, 1)
            acc[:, at] = value
            h_fm[:, at] = value.astype(bf16)

        by_columns(tokens, body)
        h_tm[...] = h_fm[...].T

    @pl.when(i < groups)
    def _():
        for t in range(0, tokens, step):
            upper = dot(h_tm[t : t + step, :], up_ref[0], 1, 0)
            cdf = 0.5 * (1.0 + lax.erf(upper * 0.7071067811865476))
            density = jnp.exp(-0.5 * upper * upper) * 0.3989422804014327
            act[i, t : t + step, :] = (upper * cdf).astype(bf16)
            slope[i, t : t + step, :] = (cdf + upper * density).astype(bf16)
        acc[...] += dot(down_ref[0], act[i], 1, 1)

    @pl.when(i == groups - 1)
    def _():
        dg_three_ref[...] = jnp.zeros_like(dg_three_ref)
        dg_two_ref[...] = jnp.zeros_like(dg_two_ref)

        def body(at):
            normed, inv_std = norm_stats(acc[:, at])
            gain = gain_of(wc_ref, feat, 2)
            out_ref[:, at] = (normed * gain).astype(bf16)
            grad = cot_ref[:, at].astype(f32)
            dg_three_ref[...] += grad * normed
            value = norm_back(grad, gain, normed, inv_std)
            acc[:, at] = value
            d_fm[:, at] = value.astype(bf16)

        by_columns(tokens, body)
        d_tm[...] = d_fm[...].T

    @pl.when(i >= groups)
    def _():
        g = other_first(i - groups, place_ref, half)
        for t in range(0, tokens, step):
            at = slice(t, t + step)
            back = dot(d_tm[at, :], down_ref[0], 1, 0) * slope[g, at, :].astype(f32)
            slope[g, at, :] = back.astype(bf16)
        g_down = dot(d_fm[...], act[g], 1, 0).astype(bf16)
        g_up = dot(h_fm[...], slope[g], 1, 0).astype(bf16)

        @pl.when(i < groups + half)
        def _():
            gother_ref[0, :, units:] = g_down
            gother_ref[0, :, :units] = g_up

        @pl.when(i >= groups + half)
        def _():
            gown_ref[0, :, units:] = g_down
            gown_ref[0, :, :units] = g_up

        acc[...] += dot(up_ref[0], slope[g], 1, 1)

    @pl.when(i == 2 * groups - 1)
    def _():
        def body(at):
            grad = acc[:, at]
            normed = normed_two[:, at]
            dg_two_ref[...] += grad * normed
            value = norm_back(grad, gain_of(wc_ref, feat, 1), normed, inv_two[:, at])
            dy_ref[:, at] = value
            dcross_ref[:, at] = value.astype(bf16)

        by_columns(tokens, body)
        low = dcross_ref[...]
        for g in range(groups):
            dcatt_ref[g] = dot(wc_ref[g, :, :feat], low, 0, 0).astype(bf16)


def middle(place, normed_one, catt, small, large, cot):
    width, tokens = normed_one.shape
    groups, feat, _ = catt.shape
    half = groups // 2
    units = large.shape[2] // 2
    lanes = min(128, tokens)

    def weight(kind):
        def index(i, p):
            return jnp.where(i < groups, i, other_first(i - groups, p, half)), 0, kind

        return pl.BlockSpec((1, width, units), index)

    def grad_out(first):
        return pl.BlockSpec(
            (1, width, 2 * units), lambda i, p: (jnp.clip(i - first, 0, half - 1), 0, 0)
        )

    outs = [
        jax.ShapeDtypeStruct((width, tokens), bf16),
        jax.ShapeDtypeStruct(catt.shape, bf16),
        jax.ShapeDtypeStruct((width, tokens), f32),
        jax.ShapeDtypeStruct((width, tokens), bf16),
        jax.ShapeDtypeStruct((half, width, 2 * units), bf16),
        jax.ShapeDtypeStruct((half, width, 2 * units), bf16),
        jax.ShapeDtypeStruct((width, lanes), f32),
        jax.ShapeDtypeStruct((width, lanes), f32),
    ]
    specs = [whole(o) for o in outs]
    specs[4], specs[5] = grad_out(groups), grad_out(groups + half)
    return pl.pallas_call(
        middle_kernel,
        grid_spec=pltpu.PrefetchScalarGridSpec(
            num_scalar_prefetch=1,
            grid=(2 * groups,),
            in_specs=[
                whole(normed_one),
                whole(catt),
                pl.BlockSpec((groups, width, 128), lambda i, p: (0, 0, 3)),
                weight(0),
                weight(1),
                whole(cot),
            ],
            out_specs=specs,
            scratch_shapes=[
                pltpu.VMEM((width, tokens), f32),
                pltpu.VMEM((width, tokens), f32),
                pltpu.VMEM((1, tokens), f32),
                pltpu.VMEM((groups, tokens, units), bf16),
                pltpu.VMEM((groups, tokens, units), bf16),
                pltpu.VMEM((width, tokens), bf16),
                pltpu.VMEM((tokens, width), bf16),
                pltpu.VMEM((width, tokens), bf16),
                pltpu.VMEM((tokens, width), bf16),
            ],
        ),
        out_shape=outs,
        compiler_params=kernel_params(),
        cost_estimate=pl.CostEstimate(
            flops=12 * groups * width * units * tokens, bytes_accessed=8 * large.size, transcendentals=0
        ),
        name="middle",
    )(place, normed_one, catt, small, large, large, cot)


def before_self_kernel(
    dcq_ref, w_ref, dy_ref, normed_ref, inv_ref,
    dattn_ref, dlow_ref, dy_one_ref, dg_ref, acc,
):
    groups, feat, tokens = dcq_ref.shape
    rows = dattn_ref.shape[0]
    total = dy_ref[...]
    for g in range(groups):
        total = total + dot(w_ref[g, :, 3 * feat : 4 * feat], dcq_ref[g], 1, 0)
    acc[...] = total
    dg_ref[...] = jnp.zeros_like(dg_ref)

    def body(at):
        grad = acc[:, at]
        normed = normed_ref[:, at]
        dg_ref[...] += grad * normed
        value = norm_back(grad, gain_of(w_ref, 5 * feat, 0), normed, inv_ref[:, at])
        dy_one_ref[:, at] = value
        dlow_ref[:, at] = value.astype(bf16)

    by_columns(tokens, body)
    low = dlow_ref[...]
    for g in range(groups):
        r, d = attn_place(g, rows)
        dattn_ref[r, d] = dot(w_ref[g, :, 2 * feat : 3 * feat], low, 0, 0).astype(bf16)


def before_self(d_cq, small, dy_two, normed_one, inv_one, attn_shape):
    width, tokens = dy_two.shape
    args = (d_cq, small, dy_two, normed_one, inv_one)
    outs = [
        jax.ShapeDtypeStruct(attn_shape, bf16),
        jax.ShapeDtypeStruct((width, tokens), bf16),
        jax.ShapeDtypeStruct((width, tokens), f32),
        jax.ShapeDtypeStruct((width, min(128, tokens)), f32),
    ]
    return pl.pallas_call(
        before_self_kernel,
        grid=(1,),
        in_specs=[whole(a) for a in args],
        out_specs=[whole(o) for o in outs],
        out_shape=outs,
        scratch_shapes=[pltpu.VMEM((width, tokens), f32)],
        compiler_params=kernel_params(),
        name="before_self",
    )(*args)


def small_grads_kernel(
    place_ref, w_ref, chosen_ref, dckv_ref, attn_ref, dcq_ref, catt_ref, dlow_ref, h_ref,
    dcross_ref, dg_one_ref, dg_two_ref, dg_three_ref, rother_ref, rown_ref, cother_ref, cown_ref,
    wide, acc, gain_cols, *, paired,
):
    g = pl.program_id(0)
    feat2 = dckv_ref.shape[1]
    feat = feat2 // 2
    count, width, tokens = chosen_ref.shape
    share = count // 2
    half = pl.num_programs(0) // 2

    @pl.when(g == 0)
    def _():
        side_by_side(chosen_ref, wide)
        col = lax.broadcasted_iota(jnp.int32, gain_cols.shape, 1)
        total = jnp.zeros(gain_cols.shape, f32)
        for k, ref in enumerate((dg_one_ref, dg_two_ref, dg_three_ref)):
            total = jnp.where(col == k, jnp.sum(ref[...], axis=1, keepdims=True), total)
        gain_cols[...] = total.astype(bf16)
        acc[...] = jnp.zeros_like(acc)

    grad = dckv_ref[0]
    acc[...] += dot(w_ref[0][:, :feat2], grad, 1, 0)
    parts = [dot(wide[...], grad, 1, 1).astype(bf16)]
    pairs = ((dlow_ref, attn_ref[0, 0]), (h_ref, dcq_ref[0]), (dcross_ref, catt_ref[0]))
    for left, right in pairs:
        parts.append(dot(left[...], right, 1, 1).astype(bf16))
    parts.append(gain_cols[...])

    def put(ref):
        at = 0
        for part in parts:
            ref[0, :, at : at + part.shape[1]] = part
            at += part.shape[1]

    @pl.when(g < half)
    def _():
        put(rother_ref)

    @pl.when(g >= half)
    def _():
        put(rown_ref)

    @pl.when(g == pl.num_programs(0) - 1)
    def _():
        for n in range(count):
            piece = acc[:, n * tokens : (n + 1) * tokens].astype(bf16)
            if paired:
                ref = cother_ref if n % 2 else cown_ref
                ref[place_ref[0] ^ (n // 2)] = piece
                continue
            mine = place_ref[1] == n // share

            @pl.when(mine)
            def _():
                cown_ref[n % share] = piece

            @pl.when(jnp.logical_not(mine))
            def _():
                cother_ref[n % share] = piece


def small_grads(place, small, chosen, d_ckv, attn, d_cq, catt, d_low, h_low, d_cross, dgs, paired):
    groups, width, cols = small.shape
    _, feat2, keys = d_ckv.shape
    feat = feat2 // 2
    tokens = d_low.shape[1]
    rows = attn.shape[0]
    half = groups // 2

    def order(g, p):
        return other_first(g, p, half)

    def rest_out(first):
        return pl.BlockSpec((1, width, cols), lambda g, p: (jnp.clip(g - first, 0, half - 1), 0, 0))

    piece = pl.BlockSpec((1, feat, tokens), lambda g, p: (order(g, p), 0, 0))
    share = jax.ShapeDtypeStruct((chosen.shape[0] // 2,) + chosen.shape[1:], bf16)
    rest_shape = jax.ShapeDtypeStruct((half, width, cols), bf16)
    return pl.pallas_call(
        functools.partial(small_grads_kernel, paired=paired),
        grid_spec=pltpu.PrefetchScalarGridSpec(
            num_scalar_prefetch=1,
            grid=(groups,),
            in_specs=[
                pl.BlockSpec((1, width, 2 * 128), lambda g, p: (order(g, p), 0, 0)),
                whole(chosen),
                pl.BlockSpec((1, feat2, keys), lambda g, p: (order(g, p), 0, 0)),
                pl.BlockSpec(
                    (1, 1, feat, tokens),
                    lambda g, p: (order(g, p) % rows, order(g, p) // rows, 0, 0),
                ),
                piece,
                piece,
                whole(d_low),
                whole(h_low),
                whole(d_cross),
            ]
            + [whole(v) for v in dgs],
            out_specs=[rest_out(0), rest_out(half), whole(share), whole(share)],
            scratch_shapes=[
                pltpu.VMEM((width, keys), bf16),
                pltpu.VMEM((width, keys), f32),
                pltpu.VMEM((width, cols - 5 * feat), bf16),
            ],
        ),
        out_shape=[rest_shape, rest_shape, share, share],
        compiler_params=kernel_params(),
        name="small_grads",
    )(place, small, chosen, d_ckv, attn, d_cq, catt, d_low, h_low, d_cross, *dgs)


def mm(spec, left, right):
    return jnp.einsum(spec, left, right, preferred_element_type=f32)


def per_device(
    x_in, prefix, enc_bank, bank_rows, w_qkv, w_out, w_cross_q, w_cross_kv, w_cross_out,
    w_up, w_down, ln_gains, out_grad,
):
    dp, rows, cols = lax.axis_size("dp"), lax.axis_size("row"), lax.axis_size("col")
    d_pos, r_pos, c_pos = lax.axis_index("dp"), lax.axis_index("row"), lax.axis_index("col")
    own_seqs, part_width, row_len = x_in.shape
    seqs = own_seqs * dp
    sub = cols // seqs
    parts = dp * sub
    width = part_width * cols
    tokens = row_len // parts
    heads = w_qkv.shape[2]
    feat = heads * HALF
    units = w_up.shape[1]
    odd = (r_pos % 2) == 1
    seq_pos = c_pos // sub
    part_pos = d_pos * sub + c_pos % sub
    groups = [[s * sub + k for k in range(sub)] for s in range(seqs)]
    everywhere = ("dp", "row", "col")
    swap = [(0, 1), (1, 0)]
    first_core = d_pos == 0

    def flip(value):
        return jnp.where(odd, value[:, :, ::-1], value)

    def swap_cores(value):
        take = value.shape[-1] // parts
        if parts == 2:
            low, high = value[..., :take], value[..., take:]
            upper = first_core == odd
            got = lax.ppermute(jnp.where(upper, low, high), "dp", swap)
            kept = jnp.where(upper, high, low)
            value = jnp.concatenate(
                [jnp.where(first_core, kept, got), jnp.where(first_core, got, kept)], axis=0
            )
        else:
            value = flip(value.reshape(own_seqs, part_width, parts, take))
            value = value.reshape(own_seqs, part_width, dp, sub, take)
            value = lax.all_to_all(value, "dp", 2, 0, tiled=True)
            value = value.reshape(seqs, part_width, sub, take).transpose(0, 2, 1, 3)
        return value.reshape(cols, part_width, take)

    def across_cols(value):
        return lax.all_to_all(value, "col", 0, 0, tiled=True).reshape(width, value.shape[-1])

    def to_tokens(value):
        return across_cols(swap_cores(value))

    def row_gather(value):
        if rows != 4:
            every = lax.all_gather(value, "row", axis=0)
            return [lax.dynamic_index_in_dim(every, r_pos ^ k, 0, False) for k in range(rows)]

        def send(v, k):
            return lax.ppermute(v, "row", [(i, i ^ k) for i in range(rows)])

        near_one, near_two = send(value, 1), send(value, 2)
        half = value.shape[0] // 2
        far = jnp.concatenate([send(near_two[:half], 1), send(near_one[half:], 2)], axis=0)
        return [value, near_one, near_two, far]

    def to_home(value):
        take = value.shape[-1]
        value = lax.all_to_all(value.reshape(cols, part_width, take), "col", 0, 0, tiled=True)
        if parts == 2:
            early, late = value[:own_seqs], value[own_seqs:]
            got = lax.ppermute(jnp.where(first_core, late, early), "dp", swap)
            kept = jnp.where(first_core, early, late)
            upper = first_core == odd
            return jnp.concatenate(
                [jnp.where(upper, got, kept), jnp.where(upper, kept, got)], axis=-1
            )
        value = value.reshape(seqs, sub, part_width, take).transpose(0, 2, 1, 3)
        value = value.reshape(seqs, part_width, 1, sub, take)
        value = lax.all_to_all(value, "dp", 0, 2, tiled=True)
        value = flip(value.reshape(own_seqs, part_width, parts, take))
        return value.reshape(own_seqs, part_width, parts * take)

    place = jnp.stack([r_pos, d_pos]).astype(jnp.int32)
    qkv = jnp.pad(w_qkv.reshape(part_width, 3 * feat), ((0, 0), (0, 384 - 3 * feat)))
    near = lax.all_gather(qkv, ("dp", "col"), axis=0).reshape(dp, width, qkv.shape[1])
    x_swapped = swap_cores(x_in)
    x_own = across_cols(x_swapped)
    x_rows = row_gather(x_own)
    tied, _ = lax.optimization_barrier(
        ((w_cross_kv, w_out, w_cross_q, w_cross_out, w_up, w_down, ln_gains), x_swapped)
    )
    small = jnp.concatenate(
        [
            tied[0].reshape(part_width, 2 * feat),
            tied[1].reshape(feat, part_width).T,
            tied[2].reshape(part_width, feat),
            tied[3].reshape(feat, part_width).T,
            tied[6].T,
            jnp.zeros((part_width, 512 - 5 * feat - 3), bf16),
        ],
        axis=1,
    )
    blocks = dp * rows

    def gather_all(value):
        value = lax.all_gather(value, everywhere, axis=0)
        return value.reshape(blocks, width, value.shape[-1])

    small_all = gather_all(small)
    large, _ = lax.optimization_barrier((jnp.concatenate([tied[4], tied[5].T], axis=1), x_own))
    large_all = gather_all(large)

    query, kv_own = project(place, near, x_rows, feat)
    query = query.reshape(rows, dp, heads, HALF, tokens)
    kv_own = kv_own.reshape(rows, dp, 2, heads, HALF, tokens)

    def index_of(row, part):
        return jnp.where(row % 2 == 1, parts - 1 - part, part) + row * parts

    row_ids = jnp.arange(rows, dtype=jnp.int32)
    if sub == 1:
        kv_list = [kv_own, lax.ppermute(kv_own, "dp", swap)]
        owners = [part_pos, 1 - part_pos]
    else:
        kv_all = lax.all_gather(kv_own, "col", axis=0, axis_index_groups=groups)
        kv_all = lax.all_gather(kv_all, "dp", axis=0).reshape((parts,) + kv_own.shape)
        kv_list = [kv_all[j] for j in range(parts)]
        owners = list(range(parts))
    q_start = index_of(row_ids, part_pos) * tokens
    places = [index_of(row_ids, owner) for owner in owners]
    seq_prefix = lax.all_gather(prefix, "dp", axis=0, tiled=True)[seq_pos]
    meta = jnp.concatenate([seq_prefix[None], q_start] + places).astype(jnp.int32)
    mixed, lse = attend(meta, query, kv_list, True, "self_attention")
    attn = lax.all_to_all(mixed, "row", 0, 0, tiled=True).reshape(rows, dp, feat, tokens)
    normed_one, inv_one, h_low, cross_q = after_self(x_own, attn, small_all, feat)
    cross_q = cross_q.reshape(1, dp, rows, heads, HALF, tokens)

    picked = bank_rows.shape[1] // rows
    row_pick = lax.dynamic_slice_in_dim(bank_rows, r_pos * picked, picked, 1)
    bank_ids = jnp.arange(enc_bank.shape[2], dtype=jnp.int32)
    hot = (bank_ids[None, :, None] == row_pick[:, None, :]).astype(bf16)
    chosen = to_tokens(mm("swn,snp->swp", enc_bank, hot).astype(bf16))
    c_tokens = chosen.shape[1]
    if sub > 1:
        chosen = lax.all_gather(chosen, "col", axis=0, axis_index_groups=groups)
        chosen = lax.all_gather(chosen, ("dp", "row"), axis=0)
        chosen = chosen.reshape(blocks * sub, width, c_tokens)
    else:
        pair = jnp.stack([chosen, lax.ppermute(chosen, "dp", swap)])
        chosen = jnp.concatenate(row_gather(pair), axis=0)
    ckv = cross_kv(small_all, chosen, feat)
    ckv = ckv.reshape(1, dp, rows, 2, heads, HALF, ckv.shape[-1])
    catt, lse_cross = attend(meta, cross_q, [ckv], False, "cross_attention")
    catt_flat = catt.reshape(blocks, feat, tokens)

    cot = to_tokens(out_grad)
    block_out, d_catt, dy_two, d_cross, g_other, g_own, dg_two, dg_three = middle(
        place, normed_one, catt_flat, small_all, large_all, cot
    )
    block_out = to_home(block_out)


    def with_core(own, got):
        return (own.astype(f32) + got.astype(f32)).astype(bf16)

    g_other = lax.ppermute(g_other, "dp", swap)
    d_cq, d_ckv = attend_back(
        meta, cross_q, [ckv], d_catt.reshape(catt.shape), catt, lse_cross, False, [bf16],
        "cross_attention_back",
    )
    g_other, d_cq = lax.optimization_barrier((g_other, d_cq))
    large_grad = with_core(g_own, g_other).reshape(rows * cols, part_width, 2 * units)
    large_grad = lax.psum_scatter(large_grad, ("row", "col"), scatter_dimension=0, tiled=False)
    d_cq = d_cq.reshape(blocks, feat, tokens)
    d_ckv = d_ckv.reshape(blocks, 2 * feat, d_ckv.shape[-1])
    d_attn, d_low, dy_one, dg_one = before_self(
        d_cq, small_all, dy_two, normed_one, inv_one, attn.shape
    )
    d_mixed = lax.all_to_all(d_attn, "row", 0, 0, tiled=True).reshape(mixed.shape)
    rest_other, rest, chosen_other, d_chosen = small_grads(
        place, small_all, chosen, d_ckv, attn, d_cq, catt_flat, d_low, h_low, d_cross,
        (dg_one, dg_two, dg_three), sub == 1,
    )
    rest_other = lax.ppermute(rest_other, "dp", swap)
    d_chosen = with_core(d_chosen, lax.ppermute(chosen_other, "dp", swap))
    d_chosen = d_chosen.reshape(rows, sub * width, c_tokens)
    d_chosen = lax.all_to_all(d_chosen, "row", 0, 0, tiled=True)

    types = [f32] + [bf16] * (len(kv_list) - 1) if sub == 1 else [bf16] * len(kv_list)
    d_query, *d_kv = attend_back(
        meta, query, kv_list, d_mixed, mixed, lse, True, types, "self_attention_back"
    )
    d_query, d_chosen, rest_other, block_out = lax.optimization_barrier(
        (d_query, d_chosen, rest_other, block_out)
    )
    rest = with_core(rest, rest_other).reshape(rows, cols, part_width, -1)
    rest = lax.psum_scatter(rest, "row", scatter_dimension=0, tiled=False)
    if sub == 1:
        d_kv = [d_kv[0], lax.ppermute(d_kv[1], "dp", swap)]
    else:
        d_kv = jnp.stack(d_kv).reshape((dp, sub) + kv_own.shape)
        d_kv = lax.psum_scatter(d_kv, "dp", scatter_dimension=0, tiled=True)
        d_kv = lax.psum_scatter(
            d_kv, "col", scatter_dimension=1, tiled=True, axis_index_groups=groups
        )
        d_kv = [d_kv]
    kv_shape = (rows, dp, 2, feat, tokens)
    d_kv = [value.reshape(kv_shape) for value in d_kv]
    dx_part, qkv_other, g_qkv = project_back(
        place, near, x_rows, d_query.reshape(rows, dp, feat, tokens), d_kv
    )
    dx_part = lax.all_to_all(dx_part, "row", 0, 0, tiled=True)
    dx = dy_one + jnp.sum(dx_part.astype(f32), axis=0)
    x_grad = to_home(dx.astype(bf16)).astype(f32)

    d_chosen = jnp.sum(d_chosen.astype(f32), axis=0).astype(bf16)
    if sub > 1:
        d_chosen = lax.psum_scatter(
            d_chosen.reshape(sub, width, c_tokens), "col", scatter_dimension=0, tiled=True,
            axis_index_groups=groups,
        )
    d_chosen = d_chosen.reshape(width, c_tokens)
    d_chosen = jnp.concatenate(row_gather(to_home(d_chosen)), axis=2)
    pick_rows = jnp.concatenate(
        [
            lax.dynamic_slice_in_dim(bank_rows, (r_pos ^ k) * picked, picked, 1)
            for k in range(rows)
        ],
        axis=1,
    )
    hot_all = (pick_rows[:, :, None] == bank_ids[None, None, :]).astype(bf16)
    bank_grad = mm("swp,spn->swn", d_chosen, hot_all)

    qkv = with_core(g_qkv, lax.ppermute(qkv_other, "dp", swap))
    last = jnp.concatenate([rest, qkv.reshape(cols, part_width, -1)], axis=2)
    last = lax.psum_scatter(last, "col", scatter_dimension=0, tiled=False).astype(f32)
    rest, qkv_grad = last[:, :512], last[:, 512:]
    large_grad = large_grad.astype(f32)

    return (
        block_out,
        x_grad,
        bank_grad,
        qkv_grad[:, : 3 * feat].reshape(w_qkv.shape),
        rest[:, 2 * feat : 3 * feat].T.reshape(w_out.shape),
        rest[:, 3 * feat : 4 * feat].reshape(w_cross_q.shape),
        rest[:, : 2 * feat].reshape(w_cross_kv.shape),
        rest[:, 4 * feat : 5 * feat].T.reshape(w_cross_out.shape),
        large_grad[:, :units],
        large_grad[:, units:].T,
        rest[:, 5 * feat : 5 * feat + 3].T,
    )


def solution(mesh):
    placed = (
        P("dp", "col", "row"),
        P("dp"),
        P("dp", "col", None),
        P("dp", None),
        P("col", None, "row", "dp"),
        P("row", "dp", "col"),
        P("col", "row", "dp"),
        P("col", None, "row", "dp"),
        P("row", "dp", "col"),
        P("col", ("dp", "row")),
        P(("dp", "row"), "col"),
        P(None, "col"),
        P("dp", "col", "row"),
    )
    return jax.shard_map(
        per_device,
        mesh=mesh,
        in_specs=placed,
        out_specs=(
            P("dp", "col", "row"),
            P("dp", "col", "row"),
            P("dp", "col", None),
            P("col", None, "row", "dp"),
            P("row", "dp", "col"),
            P("col", "row", "dp"),
            P("col", None, "row", "dp"),
            P("row", "dp", "col"),
            P("col", ("dp", "row")),
            P(("dp", "row"), "col"),
            P(None, "col"),
        ),
        check_vma=False,
    )
```

```python
import functools

import jax
import jax.numpy as jnp
from jax import lax
from jax.experimental import pallas as pl
from jax.experimental.pallas import tpu as pltpu
from jax.sharding import PartitionSpec as P

bf16 = jnp.bfloat16
f32 = jnp.float32
HD = 64
HALF = 32
NORM_EPS = 1e-05
NEG = -1e30
LIMIT = 90.0
LN2 = 0.6931471805599453
LOG2E = 1.4426950408889634
KB = 512


def dot(left, right, left_dim, right_dim):
    return lax.dot_general(
        left, right, (((left_dim,), (right_dim,)), ((), ())), preferred_element_type=f32
    )


def ones_rows(count, shape, dim):
    return jnp.where(lax.broadcasted_iota(jnp.int32, shape, dim) < count, 1.0, 0.0).astype(bf16)


def allowed_block(meta, i, start, width, cols):
    k_pos = start + lax.broadcasted_iota(jnp.int32, (width, cols), 0)
    q_pos = meta[1 + i] + lax.broadcasted_iota(jnp.int32, (1, cols), 1)
    return k_pos <= jnp.maximum(q_pos, meta[0] - 1)


def block_range(meta, i, cols):
    full = jnp.maximum(meta[1 + i], meta[0]) // KB
    total = (jnp.maximum(meta[1 + i] + cols, meta[0]) + KB - 1) // KB
    return full, total


def over_keys(meta, i, cols, keys, masked, step, carry):
    if not masked:
        for start in range(0, keys, KB):
            carry = step(start, carry, False, KB)
        return carry
    full, total = block_range(meta, i, cols)
    pairs = full // 2
    carry = lax.fori_loop(0, pairs, lambda j, c: step(j * 2 * KB, c, False, 2 * KB), carry)
    carry = lax.fori_loop(2 * pairs, full, lambda j, c: step(j * KB, c, False, KB), carry)
    return lax.fori_loop(full, total, lambda j, c: step(j * KB, c, True, KB), carry)


def pieces(kv_refs, masked):
    out = []
    for ref in kv_refs:
        count = ref.shape[0]
        for b in range(count):
            out.append((ref, b))
    return out


def piece_start(meta, n_query, index, length, masked):
    if masked:
        return pl.multiple_of(meta[1 + n_query + index] * length, length)
    return index * length


def attend_kernel(*refs, sources, n_query, masked):
    meta, q_ref = refs[:2]
    kv_refs = refs[2 : 2 + sources]
    o_ref, l_ref, key_rows, val_cols = refs[2 + sources :]
    i = pl.program_id(1)
    cols = q_ref.shape[-1]
    keys = val_cols.shape[-1]

    @pl.when(i == 0)
    def _():
        key_rows[:, HD:] = ones_rows(1, (keys, 16), 1)
        val_cols[HD:, :] = ones_rows(1, (16, keys), 0)
        for index, (ref, b) in enumerate(pieces(kv_refs, masked)):
            length = ref.shape[-1]
            at = pl.ds(piece_start(meta, n_query, index, length, masked), length)
            key_rows[at, :HD] = ref[b, :, 0, 0].reshape(HD, length).T
            val_cols[:HD, at] = ref[b, :, 1, 0].reshape(HD, length)

    query = q_ref[0, :, 0].reshape(HD, cols)
    first = dot(key_rows[0:128, :HD], query, 1, 0)
    shift = jnp.max(first, axis=0, keepdims=True).astype(bf16).astype(f32)
    row = lax.broadcasted_iota(jnp.int32, (16, cols), 0)
    query_more = jnp.concatenate([query, jnp.where(row == 0, -shift, 0.0).astype(bf16)], axis=0)

    def step(start, carry, mask, width):
        top, acc = carry
        at = pl.ds(pl.multiple_of(start, KB), width)
        scores = dot(key_rows[at, :], query_more, 1, 0)
        if mask:
            scores = jnp.where(allowed_block(meta, i, start, width, cols), scores, NEG)
        top = jnp.maximum(top, jnp.max(scores, axis=0, keepdims=True))
        acc = acc + dot(val_cols[:, at], jnp.exp2(scores).astype(bf16), 1, 0)
        return top, acc

    def put(shift, acc):
        total = acc[HD : HD + 1, :]
        mixed = (acc[:HD] * (1.0 / total)).astype(bf16)
        o_ref[0, :, 0] = mixed.reshape(2, HALF, cols)
        l_ref[0, 0] = shift + jnp.log2(total)

    start = (jnp.full((1, cols), NEG, f32), jnp.zeros((HD + 16, cols), f32))
    top, acc = over_keys(meta, i, cols, keys, masked, step, start)
    put(shift, acc)

    @pl.when(jnp.max(top) > LIMIT)
    def _():
        def careful(j, carry):
            high, acc = carry
            at = pl.ds(pl.multiple_of(j * KB, KB), KB)
            scores = dot(key_rows[at, :HD], query, 1, 0)
            if masked:
                scores = jnp.where(allowed_block(meta, i, j * KB, KB, cols), scores, NEG)
            new = jnp.maximum(high, jnp.max(scores, axis=0, keepdims=True))
            part = dot(val_cols[:, at], jnp.exp2(scores - new).astype(bf16), 1, 0)
            return new, acc * jnp.exp2(high - new) + part

        total = block_range(meta, i, cols)[1] if masked else keys // KB
        put(*lax.fori_loop(0, total, careful, start))


def attend_back_kernel(*refs, sources, n_query, masked):
    meta, q_ref = refs[:2]
    kv_refs = refs[2 : 2 + sources]
    g_ref, o_ref, l_ref = refs[2 + sources : 5 + sources]
    dq_ref = refs[5 + sources]
    dkv_refs = refs[6 + sources : 6 + 2 * sources]
    key_rows, val_rows, key_cols, dk_acc, dv_acc = refs[6 + 2 * sources :]
    i = pl.program_id(1)
    cols = q_ref.shape[-1]
    keys = key_cols.shape[-1]

    @pl.when(i == 0)
    def _():
        key_rows[:, HD:] = ones_rows(3, (keys, 16), 1)
        val_rows[:, HD:] = ones_rows(3, (keys, 16), 1)
        for index, (ref, b) in enumerate(pieces(kv_refs, masked)):
            length = ref.shape[-1]
            at = pl.ds(piece_start(meta, n_query, index, length, masked), length)
            k_part = ref[b, :, 0, 0].reshape(HD, length)
            key_cols[:, at] = k_part
            key_rows[at, :HD] = k_part.T
            val_rows[at, :HD] = ref[b, :, 1, 0].reshape(HD, length).T
        dk_acc[...] = jnp.zeros_like(dk_acc)
        dv_acc[...] = jnp.zeros_like(dv_acc)

    query = q_ref[0, :, 0].reshape(HD, cols)
    grad = g_ref[0, :, 0].reshape(HD, cols)
    delta = jnp.sum(
        grad.astype(f32) * o_ref[0, :, 0].reshape(HD, cols).astype(f32), axis=0, keepdims=True
    )

    def with_shift(value, shift):
        high = shift.astype(bf16).astype(f32)
        mid = (shift - high).astype(bf16).astype(f32)
        low = shift - high - mid
        row = lax.broadcasted_iota(jnp.int32, (16, cols), 0)
        more = jnp.where(row == 0, -high, jnp.where(row == 1, -mid, jnp.where(row == 2, -low, 0.0)))
        return jnp.concatenate([value, more.astype(bf16)], axis=0)

    query_more = with_shift(query, l_ref[0, 0])
    grad_more = with_shift(grad, delta)

    def step(start, dq, mask, width):
        at = pl.ds(pl.multiple_of(start, KB), width)
        scores = dot(key_rows[at, :], query_more, 1, 0)
        if mask:
            scores = jnp.where(allowed_block(meta, i, start, width, cols), scores, NEG)
        probs = jnp.exp2(scores)
        grad_scores = (probs * dot(val_rows[at, :], grad_more, 1, 0)).astype(bf16)
        dv_acc[:, at] += dot(grad, probs.astype(bf16), 1, 1)
        dk_acc[:, at] += dot(query, grad_scores, 1, 1)
        return dq + dot(key_cols[:, at], grad_scores, 1, 0)

    dq = over_keys(meta, i, cols, keys, masked, step, jnp.zeros((HD, cols), f32))
    dq_ref[0, :, 0] = (dq * 0.125).astype(bf16).reshape(2, HALF, cols)

    @pl.when(i == n_query - 1)
    def _():
        for index, (ref, b) in enumerate(pieces(dkv_refs, masked)):
            length = ref.shape[-1]
            at = pl.ds(piece_start(meta, n_query, index, length, masked), length)
            ref[b, :, 0, 0] = (dk_acc[:, at] * LN2).astype(ref.dtype).reshape(2, HALF, length)
            ref[b, :, 1, 0] = dv_acc[:, at].astype(ref.dtype).reshape(2, HALF, length)


def attention_specs(query, kv_list, masked):
    cols = query.shape[-1]
    if masked:
        n_query, _, heads = query.shape[:3]
        grid = (heads, n_query)
        q_spec = pl.BlockSpec((1, 2, 1, HALF, cols), lambda h, i, m: (i, 0, h, 0, 0))
        kv_specs = [
            pl.BlockSpec(kv.shape[:3] + (1,) + kv.shape[4:], lambda h, i, m: (0, 0, 0, h, 0, 0))
            for kv in kv_list
        ]
        l_spec = pl.BlockSpec((1, 1, 1, cols), lambda h, i, m: (h, i, 0, 0))
        l_shape = (heads, n_query, 1, cols)
        keys = sum(kv.shape[0] * kv.shape[-1] for kv in kv_list)
    else:
        n_query = 1
        _, _, rows, heads = query.shape[:4]
        grid = (rows * heads, 1)
        q_spec = pl.BlockSpec(
            (1, 2, None, 1, HALF, cols), lambda g, i, m: (0, 0, g // heads, g % heads, 0, 0)
        )
        kv_specs = [
            pl.BlockSpec(
                (kv.shape[0], 2, None, 2, 1) + kv.shape[5:],
                lambda g, i, m: (0, 0, g // heads, 0, g % heads, 0, 0),
            )
            for kv in kv_list
        ]
        l_spec = pl.BlockSpec((1, 1, 1, cols), lambda g, i, m: (g, 0, 0, 0))
        l_shape = (rows * heads, 1, 1, cols)
        keys = sum(kv.shape[0] * kv.shape[-1] for kv in kv_list)
    return n_query, grid, q_spec, kv_specs, l_spec, l_shape, keys


def cost(query, keys, dots):
    pairs = query.size // HD * keys
    return pl.CostEstimate(
        flops=2 * pairs * 256 * dots // 2, bytes_accessed=query.size * 16, transcendentals=pairs
    )


def attend(meta, query, kv_list, masked, name):
    n_query, grid, q_spec, kv_specs, l_spec, l_shape, keys = attention_specs(query, kv_list, masked)
    return pl.pallas_call(
        functools.partial(attend_kernel, sources=len(kv_list), n_query=n_query, masked=masked),
        grid_spec=pltpu.PrefetchScalarGridSpec(
            num_scalar_prefetch=1,
            grid=grid,
            in_specs=[q_spec] + kv_specs,
            out_specs=[q_spec, l_spec],
            scratch_shapes=[pltpu.VMEM((keys, HD + 16), bf16), pltpu.VMEM((HD + 16, keys), bf16)],
        ),
        out_shape=[
            jax.ShapeDtypeStruct(query.shape, bf16),
            jax.ShapeDtypeStruct(l_shape, f32),
        ],
        compiler_params=pltpu.CompilerParams(vmem_limit_bytes=48 << 20),
        cost_estimate=cost(query, keys, 2),
        name=name,
    )(meta, query, *kv_list)


def attend_back(meta, query, kv_list, grad, out, lse, masked, types, name):
    n_query, grid, q_spec, kv_specs, l_spec, l_shape, keys = attention_specs(query, kv_list, masked)
    return pl.pallas_call(
        functools.partial(attend_back_kernel, sources=len(kv_list), n_query=n_query, masked=masked),
        grid_spec=pltpu.PrefetchScalarGridSpec(
            num_scalar_prefetch=1,
            grid=grid,
            in_specs=[q_spec] + kv_specs + [q_spec, q_spec, l_spec],
            out_specs=[q_spec] + kv_specs,
            scratch_shapes=[
                pltpu.VMEM((keys, HD + 16), bf16),
                pltpu.VMEM((keys, HD + 16), bf16),
                pltpu.VMEM((HD, keys), bf16),
                pltpu.VMEM((HD, keys), f32),
                pltpu.VMEM((HD, keys), f32),
            ],
        ),
        out_shape=[jax.ShapeDtypeStruct(query.shape, bf16)]
        + [jax.ShapeDtypeStruct(kv.shape, t) for kv, t in zip(kv_list, types)],
        compiler_params=pltpu.CompilerParams(vmem_limit_bytes=48 << 20),
        cost_estimate=cost(query, keys, 5),
        name=name,
    )(meta, query, *kv_list, grad, out, lse)


def gain_of(w_ref, first, k):
    return w_ref[0, :, first + k : first + k + 1].astype(f32)


def other_first(i, place, half):
    return jnp.where(i < half, (1 - place[1]) * half + i, place[1] * half + i - half)


def kernel_params():
    return pltpu.CompilerParams(vmem_limit_bytes=60 << 20)


def whole(value):
    return pl.BlockSpec(value.shape, lambda *i: (0,) * value.ndim)


def by_columns(count, body):
    step = min(128, count)

    def one(j, carry):
        body(pl.ds(pl.multiple_of(j * step, step), step))
        return carry

    lax.fori_loop(0, count // step, one, 0)


def norm_stats(resid):
    width = resid.shape[0]
    mean = jnp.sum(resid, 0, keepdims=True) / width
    square = jnp.sum(resid * resid, 0, keepdims=True) / width
    inv_std = lax.rsqrt(square - mean * mean + NORM_EPS)
    return (resid - mean) * inv_std, inv_std


def norm_back(grad, gain, normed, inv_std):
    width = grad.shape[0]
    scaled = grad * gain
    total = jnp.sum(scaled, 0, keepdims=True) / width
    cross = jnp.sum(scaled * normed, 0, keepdims=True) / width
    return inv_std * (scaled - total - normed * cross)


def project_kernel(place_ref, near_ref, *refs, rows):
    x_refs = refs[:rows]
    q_ref, kv_ref, near_t = refs[rows:]
    feat = q_ref.shape[2]
    step = pl.program_id(0)

    @pl.when(step == 0)
    def _():
        for d in range(near_ref.shape[0]):
            near_t[d] = near_ref[d].T

    for k, x_ref in enumerate(x_refs):

        @pl.when(step == k)
        def _():
            for d in range(near_ref.shape[0]):
                proj = dot(near_t[d, : 3 * feat, :], x_ref[...], 1, 0)
                q_ref[0, d] = (proj[:feat] * (0.125 * LOG2E)).astype(bf16)
                kv_ref[0, d, 0] = proj[feat : 2 * feat].astype(bf16)
                kv_ref[0, d, 1] = proj[2 * feat :].astype(bf16)


def project(place, near, x_rows, feat):
    dp, width, cols = near.shape
    rows = len(x_rows)
    tokens = x_rows[0].shape[1]
    return pl.pallas_call(
        functools.partial(project_kernel, rows=rows),
        grid_spec=pltpu.PrefetchScalarGridSpec(
            num_scalar_prefetch=1,
            grid=(rows,),
            in_specs=[whole(near)] + [whole(x) for x in x_rows],
            out_specs=[
                pl.BlockSpec((1, dp, feat, tokens), lambda k, p: (p[0] ^ k, 0, 0, 0)),
                pl.BlockSpec((1, dp, 2, feat, tokens), lambda k, p: (p[0] ^ k, 0, 0, 0, 0)),
            ],
            scratch_shapes=[pltpu.VMEM((dp, cols, width), bf16)],
        ),
        out_shape=[
            jax.ShapeDtypeStruct((rows, dp, feat, tokens), bf16),
            jax.ShapeDtypeStruct((rows, dp, 2, feat, tokens), bf16),
        ],
        compiler_params=kernel_params(),
        name="project",
    )(place, near, *x_rows)


def project_back_kernel(place_ref, near_ref, *refs, rows, sources):
    x_refs, dq_ref = refs[:rows], refs[rows]
    dkv_refs = refs[rows + 1 : rows + 1 + sources]
    dx_ref, gother_ref, gown_ref, acc = refs[rows + 1 + sources :]
    step = pl.program_id(0)
    feat = dq_ref.shape[2]

    @pl.when(step == 0)
    def _():
        acc[...] = jnp.zeros_like(acc)

    for k, x_ref in enumerate(x_refs):

        @pl.when(step == k)
        def _():
            total = None
            for d in range(near_ref.shape[0]):
                parts = [dq_ref[0, d]]
                for kind in range(2):
                    value = sum(ref[0, d, kind].astype(f32) for ref in dkv_refs)
                    parts.append(value.astype(bf16))
                grad = jnp.concatenate(parts, axis=0)
                acc[d, :, : 3 * feat] += dot(x_ref[...], grad, 1, 1)
                part = dot(near_ref[d, :, : 3 * feat], grad, 1, 0)
                total = part if total is None else total + part
            dx_ref[0] = total.astype(bf16)

    @pl.when(step == rows - 1)
    def _():
        gown_ref[...] = acc[place_ref[1]].astype(bf16)
        gother_ref[...] = acc[1 - place_ref[1]].astype(bf16)


def project_back(place, near, x_rows, d_query, d_kv):
    dp, width, cols = near.shape
    rows = len(x_rows)
    tokens = x_rows[0].shape[1]
    feat = d_query.shape[2]
    kv_spec = pl.BlockSpec((1, dp, 2, feat, tokens), lambda k, p: (p[0] ^ k, 0, 0, 0, 0))
    half = jax.ShapeDtypeStruct((width, cols), bf16)
    return pl.pallas_call(
        functools.partial(project_back_kernel, rows=rows, sources=len(d_kv)),
        grid_spec=pltpu.PrefetchScalarGridSpec(
            num_scalar_prefetch=1,
            grid=(rows,),
            in_specs=[whole(near)]
            + [whole(x) for x in x_rows]
            + [pl.BlockSpec((1, dp, feat, tokens), lambda k, p: (p[0] ^ k, 0, 0, 0))]
            + [kv_spec] * len(d_kv),
            out_specs=[
                pl.BlockSpec((1, width, tokens), lambda k, p: (p[0] ^ k, 0, 0)),
                whole(half),
                whole(half),
            ],
            scratch_shapes=[pltpu.VMEM(near.shape, f32)],
        ),
        out_shape=[
            jax.ShapeDtypeStruct((rows, width, tokens), bf16),
            half,
            half,
        ],
        compiler_params=kernel_params(),
        name="project_back",
    )(place, near, *x_rows, d_query, *d_kv)


def side_by_side(chosen_ref, wide):
    count, _, tokens = chosen_ref.shape
    for n in range(count):
        wide[:, n * tokens : (n + 1) * tokens] = chosen_ref[n]


def cross_kv_kernel(w_ref, chosen_ref, o_ref, wide):
    @pl.when(pl.program_id(0) == 0)
    def _():
        side_by_side(chosen_ref, wide)

    weight = w_ref[0][:, : o_ref.shape[1]].T
    o_ref[0] = dot(weight, wide[...], 1, 0).astype(bf16)


def cross_kv(small, chosen, feat):
    groups, width, cols = small.shape
    keys = chosen.shape[0] * chosen.shape[2]
    return pl.pallas_call(
        cross_kv_kernel,
        grid=(groups,),
        in_specs=[pl.BlockSpec((1, width, 2 * 128), lambda g: (g, 0, 0)), whole(chosen)],
        out_specs=pl.BlockSpec((1, 2 * feat, keys), lambda g: (g, 0, 0)),
        out_shape=jax.ShapeDtypeStruct((groups, 2 * feat, keys), bf16),
        scratch_shapes=[pltpu.VMEM((width, keys), bf16)],
        compiler_params=kernel_params(),
        name="cross_kv",
    )(small, chosen)


def attn_place(g, rows):
    return g % rows, g // rows


def after_self_kernel(x_ref, attn_ref, w_ref, normed_ref, inv_ref, low_ref, cq_ref, acc):
    groups, feat, tokens = cq_ref.shape
    rows = attn_ref.shape[0]
    total = x_ref[...].astype(f32)
    for g in range(groups):
        r, d = attn_place(g, rows)
        total = total + dot(w_ref[g, :, 2 * feat : 3 * feat], attn_ref[r, d], 1, 0)
    acc[...] = total

    def body(at):
        normed, inv_std = norm_stats(acc[:, at])
        normed_ref[:, at] = normed
        inv_ref[:, at] = inv_std
        low_ref[:, at] = (normed * gain_of(w_ref, 5 * feat, 0)).astype(bf16)

    by_columns(tokens, body)
    low = low_ref[...]
    for g in range(groups):
        query = dot(w_ref[g, :, 3 * feat : 4 * feat], low, 0, 0)
        cq_ref[g] = (query * (0.125 * LOG2E)).astype(bf16)


def after_self(x_own, attn, small, feat):
    width, tokens = x_own.shape
    groups = small.shape[0]
    args = (x_own, attn, small)
    outs = [
        jax.ShapeDtypeStruct((width, tokens), f32),
        jax.ShapeDtypeStruct((1, tokens), f32),
        jax.ShapeDtypeStruct((width, tokens), bf16),
        jax.ShapeDtypeStruct((groups, feat, tokens), bf16),
    ]
    return pl.pallas_call(
        after_self_kernel,
        grid=(1,),
        in_specs=[whole(a) for a in args],
        out_specs=[whole(o) for o in outs],
        out_shape=outs,
        scratch_shapes=[pltpu.VMEM((width, tokens), f32)],
        compiler_params=kernel_params(),
        name="after_self",
    )(*args)


def middle_kernel(
    place_ref, normed_one_ref, catt_ref, wc_ref, up_ref, down_ref, cot_ref,
    out_ref, dcatt_ref, dy_ref, dcross_ref, gother_ref, gown_ref, dg_two_ref, dg_three_ref,
    acc, normed_two, inv_two, act, slope, h_fm, h_tm, d_fm, d_tm,
):
    i = pl.program_id(0)
    groups, feat, tokens = catt_ref.shape
    half = groups // 2
    units = up_ref.shape[2]
    step = min(256, tokens)

    @pl.when(i == 0)
    def _():
        total = normed_one_ref[...] * gain_of(wc_ref, feat, 0)
        for g in range(groups):
            total = total + dot(wc_ref[g, :, :feat], catt_ref[g], 1, 0)
        acc[...] = total

        def body(at):
            normed, inv_std = norm_stats(acc[:, at])
            normed_two[:, at] = normed
            inv_two[:, at] = inv_std
            value = normed * gain_of(wc_ref, feat, 1)
            acc[:, at] = value
            h_fm[:, at] = value.astype(bf16)

        by_columns(tokens, body)
        h_tm[...] = h_fm[...].T

    @pl.when(i < groups)
    def _():
        for t in range(0, tokens, step):
            upper = dot(h_tm[t : t + step, :], up_ref[0], 1, 0)
            cdf = 0.5 * (1.0 + lax.erf(upper * 0.7071067811865476))
            density = jnp.exp(-0.5 * upper * upper) * 0.3989422804014327
            act[i, t : t + step, :] = (upper * cdf).astype(bf16)
            slope[i, t : t + step, :] = (cdf + upper * density).astype(bf16)
        acc[...] += dot(down_ref[0], act[i], 1, 1)

    @pl.when(i == groups - 1)
    def _():
        dg_three_ref[...] = jnp.zeros_like(dg_three_ref)
        dg_two_ref[...] = jnp.zeros_like(dg_two_ref)

        def body(at):
            normed, inv_std = norm_stats(acc[:, at])
            gain = gain_of(wc_ref, feat, 2)
            out_ref[:, at] = (normed * gain).astype(bf16)
            grad = cot_ref[:, at].astype(f32)
            dg_three_ref[...] += grad * normed
            value = norm_back(grad, gain, normed, inv_std)
            acc[:, at] = value
            d_fm[:, at] = value.astype(bf16)

        by_columns(tokens, body)
        d_tm[...] = d_fm[...].T

    @pl.when(i >= groups)
    def _():
        g = other_first(i - groups, place_ref, half)
        for t in range(0, tokens, step):
            at = slice(t, t + step)
            back = dot(d_tm[at, :], down_ref[0], 1, 0) * slope[g, at, :].astype(f32)
            slope[g, at, :] = back.astype(bf16)
        g_down = dot(d_fm[...], act[g], 1, 0).astype(bf16)
        g_up = dot(h_fm[...], slope[g], 1, 0).astype(bf16)

        @pl.when(i < groups + half)
        def _():
            gother_ref[0, :, units:] = g_down
            gother_ref[0, :, :units] = g_up

        @pl.when(i >= groups + half)
        def _():
            gown_ref[0, :, units:] = g_down
            gown_ref[0, :, :units] = g_up

        acc[...] += dot(up_ref[0], slope[g], 1, 1)

    @pl.when(i == 2 * groups - 1)
    def _():
        def body(at):
            grad = acc[:, at]
            normed = normed_two[:, at]
            dg_two_ref[...] += grad * normed
            value = norm_back(grad, gain_of(wc_ref, feat, 1), normed, inv_two[:, at])
            dy_ref[:, at] = value
            dcross_ref[:, at] = value.astype(bf16)

        by_columns(tokens, body)
        low = dcross_ref[...]
        for g in range(groups):
            dcatt_ref[g] = dot(wc_ref[g, :, :feat], low, 0, 0).astype(bf16)


def middle(place, normed_one, catt, small, large, cot):
    width, tokens = normed_one.shape
    groups, feat, _ = catt.shape
    half = groups // 2
    units = large.shape[2] // 2
    lanes = min(128, tokens)

    def weight(kind):
        def index(i, p):
            return jnp.where(i < groups, i, other_first(i - groups, p, half)), 0, kind

        return pl.BlockSpec((1, width, units), index)

    def grad_out(first):
        return pl.BlockSpec(
            (1, width, 2 * units), lambda i, p: (jnp.clip(i - first, 0, half - 1), 0, 0)
        )

    outs = [
        jax.ShapeDtypeStruct((width, tokens), bf16),
        jax.ShapeDtypeStruct(catt.shape, bf16),
        jax.ShapeDtypeStruct((width, tokens), f32),
        jax.ShapeDtypeStruct((width, tokens), bf16),
        jax.ShapeDtypeStruct((half, width, 2 * units), bf16),
        jax.ShapeDtypeStruct((half, width, 2 * units), bf16),
        jax.ShapeDtypeStruct((width, lanes), f32),
        jax.ShapeDtypeStruct((width, lanes), f32),
    ]
    specs = [whole(o) for o in outs]
    specs[4], specs[5] = grad_out(groups), grad_out(groups + half)
    return pl.pallas_call(
        middle_kernel,
        grid_spec=pltpu.PrefetchScalarGridSpec(
            num_scalar_prefetch=1,
            grid=(2 * groups,),
            in_specs=[
                whole(normed_one),
                whole(catt),
                pl.BlockSpec((groups, width, 128), lambda i, p: (0, 0, 3)),
                weight(0),
                weight(1),
                whole(cot),
            ],
            out_specs=specs,
            scratch_shapes=[
                pltpu.VMEM((width, tokens), f32),
                pltpu.VMEM((width, tokens), f32),
                pltpu.VMEM((1, tokens), f32),
                pltpu.VMEM((groups, tokens, units), bf16),
                pltpu.VMEM((groups, tokens, units), bf16),
                pltpu.VMEM((width, tokens), bf16),
                pltpu.VMEM((tokens, width), bf16),
                pltpu.VMEM((width, tokens), bf16),
                pltpu.VMEM((tokens, width), bf16),
            ],
        ),
        out_shape=outs,
        compiler_params=kernel_params(),
        cost_estimate=pl.CostEstimate(
            flops=12 * groups * width * units * tokens, bytes_accessed=8 * large.size, transcendentals=0
        ),
        name="middle",
    )(place, normed_one, catt, small, large, large, cot)


def before_self_kernel(
    dcq_ref, w_ref, dy_ref, normed_ref, inv_ref,
    dattn_ref, dlow_ref, dy_one_ref, dg_ref, acc,
):
    groups, feat, tokens = dcq_ref.shape
    rows = dattn_ref.shape[0]
    total = dy_ref[...]
    for g in range(groups):
        total = total + dot(w_ref[g, :, 3 * feat : 4 * feat], dcq_ref[g], 1, 0)
    acc[...] = total
    dg_ref[...] = jnp.zeros_like(dg_ref)

    def body(at):
        grad = acc[:, at]
        normed = normed_ref[:, at]
        dg_ref[...] += grad * normed
        value = norm_back(grad, gain_of(w_ref, 5 * feat, 0), normed, inv_ref[:, at])
        dy_one_ref[:, at] = value
        dlow_ref[:, at] = value.astype(bf16)

    by_columns(tokens, body)
    low = dlow_ref[...]
    for g in range(groups):
        r, d = attn_place(g, rows)
        dattn_ref[r, d] = dot(w_ref[g, :, 2 * feat : 3 * feat], low, 0, 0).astype(bf16)


def before_self(d_cq, small, dy_two, normed_one, inv_one, attn_shape):
    width, tokens = dy_two.shape
    args = (d_cq, small, dy_two, normed_one, inv_one)
    outs = [
        jax.ShapeDtypeStruct(attn_shape, bf16),
        jax.ShapeDtypeStruct((width, tokens), bf16),
        jax.ShapeDtypeStruct((width, tokens), f32),
        jax.ShapeDtypeStruct((width, min(128, tokens)), f32),
    ]
    return pl.pallas_call(
        before_self_kernel,
        grid=(1,),
        in_specs=[whole(a) for a in args],
        out_specs=[whole(o) for o in outs],
        out_shape=outs,
        scratch_shapes=[pltpu.VMEM((width, tokens), f32)],
        compiler_params=kernel_params(),
        name="before_self",
    )(*args)


def small_grads_kernel(
    place_ref, w_ref, chosen_ref, dckv_ref, attn_ref, dcq_ref, catt_ref, dlow_ref, h_ref,
    dcross_ref, dg_one_ref, dg_two_ref, dg_three_ref, rother_ref, rown_ref, cother_ref, cown_ref,
    wide, acc, gain_cols, *, paired,
):
    g = pl.program_id(0)
    feat2 = dckv_ref.shape[1]
    feat = feat2 // 2
    count, width, tokens = chosen_ref.shape
    share = count // 2
    half = pl.num_programs(0) // 2

    @pl.when(g == 0)
    def _():
        side_by_side(chosen_ref, wide)
        col = lax.broadcasted_iota(jnp.int32, gain_cols.shape, 1)
        total = jnp.zeros(gain_cols.shape, f32)
        for k, ref in enumerate((dg_one_ref, dg_two_ref, dg_three_ref)):
            total = jnp.where(col == k, jnp.sum(ref[...], axis=1, keepdims=True), total)
        gain_cols[...] = total.astype(bf16)
        acc[...] = jnp.zeros_like(acc)

    grad = dckv_ref[0]
    acc[...] += dot(w_ref[0][:, :feat2], grad, 1, 0)
    parts = [dot(wide[...], grad, 1, 1).astype(bf16)]
    pairs = ((dlow_ref, attn_ref[0, 0]), (h_ref, dcq_ref[0]), (dcross_ref, catt_ref[0]))
    for left, right in pairs:
        parts.append(dot(left[...], right, 1, 1).astype(bf16))
    parts.append(gain_cols[...])

    def put(ref):
        at = 0
        for part in parts:
            ref[0, :, at : at + part.shape[1]] = part
            at += part.shape[1]

    @pl.when(g < half)
    def _():
        put(rother_ref)

    @pl.when(g >= half)
    def _():
        put(rown_ref)

    @pl.when(g == pl.num_programs(0) - 1)
    def _():
        for n in range(count):
            piece = acc[:, n * tokens : (n + 1) * tokens].astype(bf16)
            if paired:
                ref = cother_ref if n % 2 else cown_ref
                ref[place_ref[0] ^ (n // 2)] = piece
                continue
            mine = place_ref[1] == n // share

            @pl.when(mine)
            def _():
                cown_ref[n % share] = piece

            @pl.when(jnp.logical_not(mine))
            def _():
                cother_ref[n % share] = piece


def small_grads(place, small, chosen, d_ckv, attn, d_cq, catt, d_low, h_low, d_cross, dgs, paired):
    groups, width, cols = small.shape
    _, feat2, keys = d_ckv.shape
    feat = feat2 // 2
    tokens = d_low.shape[1]
    rows = attn.shape[0]
    half = groups // 2

    def order(g, p):
        return other_first(g, p, half)

    def rest_out(first):
        return pl.BlockSpec((1, width, cols), lambda g, p: (jnp.clip(g - first, 0, half - 1), 0, 0))

    piece = pl.BlockSpec((1, feat, tokens), lambda g, p: (order(g, p), 0, 0))
    share = jax.ShapeDtypeStruct((chosen.shape[0] // 2,) + chosen.shape[1:], bf16)
    rest_shape = jax.ShapeDtypeStruct((half, width, cols), bf16)
    return pl.pallas_call(
        functools.partial(small_grads_kernel, paired=paired),
        grid_spec=pltpu.PrefetchScalarGridSpec(
            num_scalar_prefetch=1,
            grid=(groups,),
            in_specs=[
                pl.BlockSpec((1, width, 2 * 128), lambda g, p: (order(g, p), 0, 0)),
                whole(chosen),
                pl.BlockSpec((1, feat2, keys), lambda g, p: (order(g, p), 0, 0)),
                pl.BlockSpec(
                    (1, 1, feat, tokens),
                    lambda g, p: (order(g, p) % rows, order(g, p) // rows, 0, 0),
                ),
                piece,
                piece,
                whole(d_low),
                whole(h_low),
                whole(d_cross),
            ]
            + [whole(v) for v in dgs],
            out_specs=[rest_out(0), rest_out(half), whole(share), whole(share)],
            scratch_shapes=[
                pltpu.VMEM((width, keys), bf16),
                pltpu.VMEM((width, keys), f32),
                pltpu.VMEM((width, cols - 5 * feat), bf16),
            ],
        ),
        out_shape=[rest_shape, rest_shape, share, share],
        compiler_params=kernel_params(),
        cost_estimate=pl.CostEstimate(
            flops=groups * width * (4 * feat2 * keys + 6 * feat * tokens),
            bytes_accessed=4 * small.size,
            transcendentals=0,
        ),
        name="small_grads",
    )(place, small, chosen, d_ckv, attn, d_cq, catt, d_low, h_low, d_cross, *dgs)


def mm(spec, left, right):
    return jnp.einsum(spec, left, right, preferred_element_type=f32)


def per_device(
    x_in, prefix, enc_bank, bank_rows, w_qkv, w_out, w_cross_q, w_cross_kv, w_cross_out,
    w_up, w_down, ln_gains, out_grad,
):
    dp, rows, cols = lax.axis_size("dp"), lax.axis_size("row"), lax.axis_size("col")
    d_pos, r_pos, c_pos = lax.axis_index("dp"), lax.axis_index("row"), lax.axis_index("col")
    own_seqs, part_width, row_len = x_in.shape
    seqs = own_seqs * dp
    sub = cols // seqs
    parts = dp * sub
    width = part_width * cols
    tokens = row_len // parts
    heads = w_qkv.shape[2]
    feat = heads * HALF
    units = w_up.shape[1]
    odd = (r_pos % 2) == 1
    seq_pos = c_pos // sub
    part_pos = d_pos * sub + c_pos % sub
    groups = [[s * sub + k for k in range(sub)] for s in range(seqs)]
    everywhere = ("dp", "row", "col")
    swap = [(0, 1), (1, 0)]
    first_core = d_pos == 0

    def flip(value):
        return jnp.where(odd, value[:, :, ::-1], value)

    def swap_cores(value):
        take = value.shape[-1] // parts
        if parts == 2:
            low, high = value[..., :take], value[..., take:]
            upper = first_core == odd
            got = lax.ppermute(jnp.where(upper, low, high), "dp", swap)
            kept = jnp.where(upper, high, low)
            value = jnp.concatenate(
                [jnp.where(first_core, kept, got), jnp.where(first_core, got, kept)], axis=0
            )
        else:
            value = flip(value.reshape(own_seqs, part_width, parts, take))
            value = value.reshape(own_seqs, part_width, dp, sub, take)
            value = lax.all_to_all(value, "dp", 2, 0, tiled=True)
            value = value.reshape(seqs, part_width, sub, take).transpose(0, 2, 1, 3)
        return value.reshape(cols, part_width, take)

    def across_cols(value):
        return lax.all_to_all(value, "col", 0, 0, tiled=True).reshape(width, value.shape[-1])

    def to_tokens(value):
        return across_cols(swap_cores(value))

    def row_gather(value):
        if rows != 4:
            every = lax.all_gather(value, "row", axis=0)
            return [lax.dynamic_index_in_dim(every, r_pos ^ k, 0, False) for k in range(rows)]

        def send(v, k):
            return lax.ppermute(v, "row", [(i, i ^ k) for i in range(rows)])

        near_one, near_two = send(value, 1), send(value, 2)
        half = value.shape[0] // 2
        far = jnp.concatenate([send(near_two[:half], 1), send(near_one[half:], 2)], axis=0)
        return [value, near_one, near_two, far]

    def home_cols(value):
        value = value.reshape(cols, part_width, value.shape[-1])
        return lax.all_to_all(value, "col", 0, 0, tiled=True)

    def to_home(value):
        return home_cores(home_cols(value))

    def home_cores(value):
        take = value.shape[-1]
        if parts == 2:
            early, late = value[:own_seqs], value[own_seqs:]
            got = lax.ppermute(jnp.where(first_core, late, early), "dp", swap)
            kept = jnp.where(first_core, early, late)
            upper = first_core == odd
            return jnp.concatenate(
                [jnp.where(upper, got, kept), jnp.where(upper, kept, got)], axis=-1
            )
        value = value.reshape(seqs, sub, part_width, take).transpose(0, 2, 1, 3)
        value = value.reshape(seqs, part_width, 1, sub, take)
        value = lax.all_to_all(value, "dp", 0, 2, tiled=True)
        value = flip(value.reshape(own_seqs, part_width, parts, take))
        return value.reshape(own_seqs, part_width, parts * take)

    place = jnp.stack([r_pos, d_pos]).astype(jnp.int32)
    qkv = jnp.pad(w_qkv.reshape(part_width, 3 * feat), ((0, 0), (0, 384 - 3 * feat)))
    near = lax.all_gather(qkv, ("dp", "col"), axis=0).reshape(dp, width, qkv.shape[1])
    x_swapped = swap_cores(x_in)
    x_own = across_cols(x_swapped)
    x_rows = row_gather(x_own)
    tied, _ = lax.optimization_barrier(
        ((w_cross_kv, w_out, w_cross_q, w_cross_out, w_up, w_down, ln_gains), x_swapped)
    )
    small = jnp.concatenate(
        [
            tied[0].reshape(part_width, 2 * feat),
            tied[1].reshape(feat, part_width).T,
            tied[2].reshape(part_width, feat),
            tied[3].reshape(feat, part_width).T,
            tied[6].T,
            jnp.zeros((part_width, 512 - 5 * feat - 3), bf16),
        ],
        axis=1,
    )
    blocks = dp * rows

    def gather_all(value):
        value = lax.all_gather(value, everywhere, axis=0)
        return value.reshape(blocks, width, value.shape[-1])

    small_all = gather_all(small)
    large, _ = lax.optimization_barrier((jnp.concatenate([tied[4], tied[5].T], axis=1), x_own))
    large_all = gather_all(large)

    query, kv_own = project(place, near, x_rows, feat)
    query = query.reshape(rows, dp, heads, HALF, tokens)
    kv_own = kv_own.reshape(rows, dp, 2, heads, HALF, tokens)

    def index_of(row, part):
        return jnp.where(row % 2 == 1, parts - 1 - part, part) + row * parts

    row_ids = jnp.arange(rows, dtype=jnp.int32)
    if sub == 1:
        kv_list = [kv_own, lax.ppermute(kv_own, "dp", swap)]
        owners = [part_pos, 1 - part_pos]
    else:
        kv_all = lax.all_gather(kv_own, "col", axis=0, axis_index_groups=groups)
        kv_all = lax.all_gather(kv_all, "dp", axis=0).reshape((parts,) + kv_own.shape)
        kv_list = [kv_all[j] for j in range(parts)]
        owners = list(range(parts))
    q_start = index_of(row_ids, part_pos) * tokens
    places = [index_of(row_ids, owner) for owner in owners]
    seq_prefix = lax.all_gather(prefix, "dp", axis=0, tiled=True)[seq_pos]
    meta = jnp.concatenate([seq_prefix[None], q_start] + places).astype(jnp.int32)
    mixed, lse = attend(meta, query, kv_list, True, "self_attention")
    attn = lax.all_to_all(mixed, "row", 0, 0, tiled=True).reshape(rows, dp, feat, tokens)
    normed_one, inv_one, h_low, cross_q = after_self(x_own, attn, small_all, feat)
    cross_q = cross_q.reshape(1, dp, rows, heads, HALF, tokens)

    picked = bank_rows.shape[1] // rows
    row_pick = lax.dynamic_slice_in_dim(bank_rows, r_pos * picked, picked, 1)
    bank_ids = jnp.arange(enc_bank.shape[2], dtype=jnp.int32)
    hot = (bank_ids[None, :, None] == row_pick[:, None, :]).astype(bf16)
    chosen = to_tokens(mm("swn,snp->swp", enc_bank, hot).astype(bf16))
    c_tokens = chosen.shape[1]
    if sub > 1:
        chosen = lax.all_gather(chosen, "col", axis=0, axis_index_groups=groups)
        chosen = lax.all_gather(chosen, ("dp", "row"), axis=0)
        chosen = chosen.reshape(blocks * sub, width, c_tokens)
    else:
        pair = jnp.stack([chosen, lax.ppermute(chosen, "dp", swap)])
        chosen = jnp.concatenate(row_gather(pair), axis=0)
    ckv = cross_kv(small_all, chosen, feat)
    ckv = ckv.reshape(1, dp, rows, 2, heads, HALF, ckv.shape[-1])
    catt, lse_cross = attend(meta, cross_q, [ckv], False, "cross_attention")
    catt_flat = catt.reshape(blocks, feat, tokens)

    cot = to_tokens(out_grad)
    block_out, d_catt, dy_two, d_cross, g_other, g_own, dg_two, dg_three = middle(
        place, normed_one, catt_flat, small_all, large_all, cot
    )
    block_out = home_cols(block_out)


    def with_core(own, got):
        return (own.astype(f32) + got.astype(f32)).astype(bf16)

    g_other = lax.ppermute(g_other, "dp", swap)
    d_cq, d_ckv = attend_back(
        meta, cross_q, [ckv], d_catt.reshape(catt.shape), catt, lse_cross, False, [bf16],
        "cross_attention_back",
    )
    g_other, d_cq, block_out = lax.optimization_barrier((g_other, d_cq, block_out))
    large_grad, d_cq = lax.optimization_barrier((with_core(g_own, g_other), d_cq))
    large_grad = large_grad.reshape(rows * cols, part_width, 2 * units)
    large_grad = lax.psum_scatter(large_grad, ("row", "col"), scatter_dimension=0, tiled=False)
    d_cq = d_cq.reshape(blocks, feat, tokens)
    d_ckv = d_ckv.reshape(blocks, 2 * feat, d_ckv.shape[-1])
    d_attn, d_low, dy_one, dg_one = before_self(
        d_cq, small_all, dy_two, normed_one, inv_one, attn.shape
    )
    d_mixed = lax.all_to_all(d_attn, "row", 0, 0, tiled=True).reshape(mixed.shape)
    rest_other, rest, chosen_other, d_chosen = small_grads(
        place, small_all, chosen, d_ckv, attn, d_cq, catt_flat, d_low, h_low, d_cross,
        (dg_one, dg_two, dg_three), sub == 1,
    )
    d_mixed, rest_other, rest, chosen_other, d_chosen = lax.optimization_barrier(
        (d_mixed, rest_other, rest, chosen_other, d_chosen)
    )
    rest_other = lax.ppermute(rest_other, "dp", swap)
    d_chosen = with_core(d_chosen, lax.ppermute(chosen_other, "dp", swap))
    d_chosen = d_chosen.reshape(rows, sub * width, c_tokens)
    d_chosen = lax.all_to_all(d_chosen, "row", 0, 0, tiled=True)

    types = [f32] + [bf16] * (len(kv_list) - 1) if sub == 1 else [bf16] * len(kv_list)
    d_query, *d_kv = attend_back(
        meta, query, kv_list, d_mixed, mixed, lse, True, types, "self_attention_back"
    )
    d_query, d_chosen, rest_other, large_grad = lax.optimization_barrier(
        (d_query, d_chosen, rest_other, large_grad)
    )
    rest = with_core(rest, rest_other).reshape(rows, cols, part_width, -1)
    rest = lax.psum_scatter(rest, "row", scatter_dimension=0, tiled=False)
    if sub == 1:
        d_kv = [d_kv[0], lax.ppermute(d_kv[1], "dp", swap)]
    else:
        d_kv = jnp.stack(d_kv).reshape((dp, sub) + kv_own.shape)
        d_kv = lax.psum_scatter(d_kv, "dp", scatter_dimension=0, tiled=True)
        d_kv = lax.psum_scatter(
            d_kv, "col", scatter_dimension=1, tiled=True, axis_index_groups=groups
        )
        d_kv = [d_kv]
    kv_shape = (rows, dp, 2, feat, tokens)
    d_kv = [value.reshape(kv_shape) for value in d_kv]
    dx_part, qkv_other, g_qkv = project_back(
        place, near, x_rows, d_query.reshape(rows, dp, feat, tokens), d_kv
    )
    dx_part = lax.all_to_all(dx_part, "row", 0, 0, tiled=True)
    dx = dy_one + jnp.sum(dx_part.astype(f32), axis=0)
    x_grad = to_home(dx.astype(bf16)).astype(f32)

    d_chosen = jnp.sum(d_chosen.astype(f32), axis=0).astype(bf16)
    if sub > 1:
        d_chosen = lax.psum_scatter(
            d_chosen.reshape(sub, width, c_tokens), "col", scatter_dimension=0, tiled=True,
            axis_index_groups=groups,
        )
    d_chosen = d_chosen.reshape(width, c_tokens)
    d_chosen = jnp.concatenate(row_gather(to_home(d_chosen)), axis=2)
    pick_rows = jnp.concatenate(
        [
            lax.dynamic_slice_in_dim(bank_rows, (r_pos ^ k) * picked, picked, 1)
            for k in range(rows)
        ],
        axis=1,
    )
    hot_all = (pick_rows[:, :, None] == bank_ids[None, None, :]).astype(bf16)
    bank_grad = mm("swp,spn->swn", d_chosen, hot_all)

    qkv = with_core(g_qkv, lax.ppermute(qkv_other, "dp", swap))
    last = jnp.concatenate([rest, qkv.reshape(cols, part_width, -1)], axis=2)
    last = lax.psum_scatter(last, "col", scatter_dimension=0, tiled=False).astype(f32)
    rest, qkv_grad = last[:, :512], last[:, 512:]
    large_grad = large_grad.astype(f32)

    return (
        home_cores(block_out),
        x_grad,
        bank_grad,
        qkv_grad[:, : 3 * feat].reshape(w_qkv.shape),
        rest[:, 2 * feat : 3 * feat].T.reshape(w_out.shape),
        rest[:, 3 * feat : 4 * feat].reshape(w_cross_q.shape),
        rest[:, : 2 * feat].reshape(w_cross_kv.shape),
        rest[:, 4 * feat : 5 * feat].T.reshape(w_cross_out.shape),
        large_grad[:, :units],
        large_grad[:, units:].T,
        rest[:, 5 * feat : 5 * feat + 3].T,
    )


def solution(mesh):
    placed = (
        P("dp", "col", "row"),
        P("dp"),
        P("dp", "col", None),
        P("dp", None),
        P("col", None, "row", "dp"),
        P("row", "dp", "col"),
        P("col", "row", "dp"),
        P("col", None, "row", "dp"),
        P("row", "dp", "col"),
        P("col", ("dp", "row")),
        P(("dp", "row"), "col"),
        P(None, "col"),
        P("dp", "col", "row"),
    )
    return jax.shard_map(
        per_device,
        mesh=mesh,
        in_specs=placed,
        out_specs=(
            P("dp", "col", "row"),
            P("dp", "col", "row"),
            P("dp", "col", None),
            P("col", None, "row", "dp"),
            P("row", "dp", "col"),
            P("col", "row", "dp"),
            P("col", None, "row", "dp"),
            P("row", "dp", "col"),
            P("col", ("dp", "row")),
            P(("dp", "row"), "col"),
            P(None, "col"),
        ),
        check_vma=False,
    )
```

```python
import functools

import jax
import jax.numpy as jnp
from jax import lax
from jax.experimental import pallas as pl
from jax.experimental.pallas import tpu as pltpu
from jax.sharding import PartitionSpec as P

bf16 = jnp.bfloat16
f32 = jnp.float32
HD = 64
HALF = 32
NORM_EPS = 1e-05
NEG = -1e30
LIMIT = 90.0
LN2 = 0.6931471805599453
LOG2E = 1.4426950408889634
KB = 512


def dot(left, right, left_dim, right_dim):
    return lax.dot_general(
        left, right, (((left_dim,), (right_dim,)), ((), ())), preferred_element_type=f32
    )


def ones_rows(count, shape, dim):
    return jnp.where(lax.broadcasted_iota(jnp.int32, shape, dim) < count, 1.0, 0.0).astype(bf16)


def allowed_block(meta, i, start, width, cols):
    k_pos = start + lax.broadcasted_iota(jnp.int32, (width, cols), 0)
    q_pos = meta[1 + i] + lax.broadcasted_iota(jnp.int32, (1, cols), 1)
    return k_pos <= jnp.maximum(q_pos, meta[0] - 1)


def block_range(meta, i, cols):
    full = jnp.maximum(meta[1 + i], meta[0]) // KB
    total = (jnp.maximum(meta[1 + i] + cols, meta[0]) + KB - 1) // KB
    return full, total


def over_keys(meta, i, cols, keys, masked, step, carry):
    if not masked:
        for start in range(0, keys, KB):
            carry = step(start, carry, False, KB)
        return carry
    full, total = block_range(meta, i, cols)
    pairs = full // 2
    carry = lax.fori_loop(0, pairs, lambda j, c: step(j * 2 * KB, c, False, 2 * KB), carry)
    carry = lax.fori_loop(2 * pairs, full, lambda j, c: step(j * KB, c, False, KB), carry)
    return lax.fori_loop(full, total, lambda j, c: step(j * KB, c, True, KB), carry)


def pieces(kv_refs, masked):
    out = []
    for ref in kv_refs:
        count = ref.shape[0]
        for b in range(count):
            out.append((ref, b))
    return out


def piece_start(meta, n_query, index, length, masked):
    if masked:
        return pl.multiple_of(meta[1 + n_query + index] * length, length)
    return index * length


def attend_kernel(*refs, sources, n_query, masked):
    meta, q_ref = refs[:2]
    kv_refs = refs[2 : 2 + sources]
    o_ref, l_ref, key_rows, val_cols = refs[2 + sources :]
    i = pl.program_id(1)
    cols = q_ref.shape[-1]
    keys = val_cols.shape[-1]

    @pl.when(i == 0)
    def _():
        key_rows[:, HD:] = ones_rows(1, (keys, 16), 1)
        val_cols[HD:, :] = ones_rows(1, (16, keys), 0)
        for index, (ref, b) in enumerate(pieces(kv_refs, masked)):
            length = ref.shape[-1]
            at = pl.ds(piece_start(meta, n_query, index, length, masked), length)
            key_rows[at, :HD] = ref[b, :, 0, 0].reshape(HD, length).T
            val_cols[:HD, at] = ref[b, :, 1, 0].reshape(HD, length)

    query = q_ref[0, :, 0].reshape(HD, cols)
    first = dot(key_rows[0:128, :HD], query, 1, 0)
    shift = jnp.max(first, axis=0, keepdims=True).astype(bf16).astype(f32)
    row = lax.broadcasted_iota(jnp.int32, (16, cols), 0)
    query_more = jnp.concatenate([query, jnp.where(row == 0, -shift, 0.0).astype(bf16)], axis=0)

    def step(start, carry, mask, width):
        top, acc = carry
        at = pl.ds(pl.multiple_of(start, KB), width)
        scores = dot(key_rows[at, :], query_more, 1, 0)
        if mask:
            scores = jnp.where(allowed_block(meta, i, start, width, cols), scores, NEG)
        top = jnp.maximum(top, jnp.max(scores, axis=0, keepdims=True))
        acc = acc + dot(val_cols[:, at], jnp.exp2(scores).astype(bf16), 1, 0)
        return top, acc

    def put(shift, acc):
        total = acc[HD : HD + 1, :]
        mixed = (acc[:HD] * (1.0 / total)).astype(bf16)
        o_ref[0, :, 0] = mixed.reshape(2, HALF, cols)
        l_ref[0, 0] = shift + jnp.log2(total)

    start = (jnp.full((1, cols), NEG, f32), jnp.zeros((HD + 16, cols), f32))
    top, acc = over_keys(meta, i, cols, keys, masked, step, start)
    put(shift, acc)

    @pl.when(jnp.max(top) > LIMIT)
    def _():
        def careful(j, carry):
            high, acc = carry
            at = pl.ds(pl.multiple_of(j * KB, KB), KB)
            scores = dot(key_rows[at, :HD], query, 1, 0)
            if masked:
                scores = jnp.where(allowed_block(meta, i, j * KB, KB, cols), scores, NEG)
            new = jnp.maximum(high, jnp.max(scores, axis=0, keepdims=True))
            part = dot(val_cols[:, at], jnp.exp2(scores - new).astype(bf16), 1, 0)
            return new, acc * jnp.exp2(high - new) + part

        total = block_range(meta, i, cols)[1] if masked else keys // KB
        put(*lax.fori_loop(0, total, careful, start))


def attend_back_kernel(*refs, sources, n_query, masked):
    meta, q_ref = refs[:2]
    kv_refs = refs[2 : 2 + sources]
    g_ref, o_ref, l_ref = refs[2 + sources : 5 + sources]
    dq_ref = refs[5 + sources]
    dkv_refs = refs[6 + sources : 6 + 2 * sources]
    key_rows, val_rows, key_cols, dk_acc, dv_acc = refs[6 + 2 * sources :]
    i = pl.program_id(1)
    cols = q_ref.shape[-1]
    keys = key_cols.shape[-1]

    @pl.when(i == 0)
    def _():
        key_rows[:, HD:] = ones_rows(3, (keys, 16), 1)
        val_rows[:, HD:] = ones_rows(3, (keys, 16), 1)
        for index, (ref, b) in enumerate(pieces(kv_refs, masked)):
            length = ref.shape[-1]
            at = pl.ds(piece_start(meta, n_query, index, length, masked), length)
            k_part = ref[b, :, 0, 0].reshape(HD, length)
            key_cols[:, at] = k_part
            key_rows[at, :HD] = k_part.T
            val_rows[at, :HD] = ref[b, :, 1, 0].reshape(HD, length).T
        dk_acc[...] = jnp.zeros_like(dk_acc)
        dv_acc[...] = jnp.zeros_like(dv_acc)

    query = q_ref[0, :, 0].reshape(HD, cols)
    grad = g_ref[0, :, 0].reshape(HD, cols)
    delta = jnp.sum(
        grad.astype(f32) * o_ref[0, :, 0].reshape(HD, cols).astype(f32), axis=0, keepdims=True
    )

    def with_shift(value, shift):
        high = shift.astype(bf16).astype(f32)
        mid = (shift - high).astype(bf16).astype(f32)
        low = shift - high - mid
        row = lax.broadcasted_iota(jnp.int32, (16, cols), 0)
        more = jnp.where(row == 0, -high, jnp.where(row == 1, -mid, jnp.where(row == 2, -low, 0.0)))
        return jnp.concatenate([value, more.astype(bf16)], axis=0)

    query_more = with_shift(query, l_ref[0, 0])
    grad_more = with_shift(grad, delta)

    def step(start, dq, mask, width):
        at = pl.ds(pl.multiple_of(start, KB), width)
        scores = dot(key_rows[at, :], query_more, 1, 0)
        if mask:
            scores = jnp.where(allowed_block(meta, i, start, width, cols), scores, NEG)
        probs = jnp.exp2(scores)
        grad_scores = (probs * dot(val_rows[at, :], grad_more, 1, 0)).astype(bf16)
        dv_acc[:, at] += dot(grad, probs.astype(bf16), 1, 1)
        dk_acc[:, at] += dot(query, grad_scores, 1, 1)
        return dq + dot(key_cols[:, at], grad_scores, 1, 0)

    dq = over_keys(meta, i, cols, keys, masked, step, jnp.zeros((HD, cols), f32))
    dq_ref[0, :, 0] = (dq * 0.125).astype(bf16).reshape(2, HALF, cols)

    @pl.when(i == n_query - 1)
    def _():
        for index, (ref, b) in enumerate(pieces(dkv_refs, masked)):
            length = ref.shape[-1]
            at = pl.ds(piece_start(meta, n_query, index, length, masked), length)
            ref[b, :, 0, 0] = (dk_acc[:, at] * LN2).astype(ref.dtype).reshape(2, HALF, length)
            ref[b, :, 1, 0] = dv_acc[:, at].astype(ref.dtype).reshape(2, HALF, length)


def attention_specs(query, kv_list, masked):
    cols = query.shape[-1]
    if masked:
        n_query, _, heads = query.shape[:3]
        grid = (heads, n_query)
        q_spec = pl.BlockSpec((1, 2, 1, HALF, cols), lambda h, i, m: (i, 0, h, 0, 0))
        kv_specs = [
            pl.BlockSpec(kv.shape[:3] + (1,) + kv.shape[4:], lambda h, i, m: (0, 0, 0, h, 0, 0))
            for kv in kv_list
        ]
        l_spec = pl.BlockSpec((1, 1, 1, cols), lambda h, i, m: (h, i, 0, 0))
        l_shape = (heads, n_query, 1, cols)
        keys = sum(kv.shape[0] * kv.shape[-1] for kv in kv_list)
    else:
        n_query = 1
        _, _, rows, heads = query.shape[:4]
        grid = (rows * heads, 1)
        q_spec = pl.BlockSpec(
            (1, 2, None, 1, HALF, cols), lambda g, i, m: (0, 0, g // heads, g % heads, 0, 0)
        )
        kv_specs = [
            pl.BlockSpec(
                (kv.shape[0], 2, None, 2, 1) + kv.shape[5:],
                lambda g, i, m: (0, 0, g // heads, 0, g % heads, 0, 0),
            )
            for kv in kv_list
        ]
        l_spec = pl.BlockSpec((1, 1, 1, cols), lambda g, i, m: (g, 0, 0, 0))
        l_shape = (rows * heads, 1, 1, cols)
        keys = sum(kv.shape[0] * kv.shape[-1] for kv in kv_list)
    return n_query, grid, q_spec, kv_specs, l_spec, l_shape, keys


def cost(query, keys, dots):
    pairs = query.size // HD * keys
    return pl.CostEstimate(
        flops=2 * pairs * 256 * dots // 2, bytes_accessed=query.size * 16, transcendentals=pairs
    )


def attend(meta, query, kv_list, masked, name):
    n_query, grid, q_spec, kv_specs, l_spec, l_shape, keys = attention_specs(query, kv_list, masked)
    return pl.pallas_call(
        functools.partial(attend_kernel, sources=len(kv_list), n_query=n_query, masked=masked),
        grid_spec=pltpu.PrefetchScalarGridSpec(
            num_scalar_prefetch=1,
            grid=grid,
            in_specs=[q_spec] + kv_specs,
            out_specs=[q_spec, l_spec],
            scratch_shapes=[pltpu.VMEM((keys, HD + 16), bf16), pltpu.VMEM((HD + 16, keys), bf16)],
        ),
        out_shape=[
            jax.ShapeDtypeStruct(query.shape, bf16),
            jax.ShapeDtypeStruct(l_shape, f32),
        ],
        compiler_params=pltpu.CompilerParams(vmem_limit_bytes=48 << 20),
        cost_estimate=cost(query, keys, 2),
        name=name,
    )(meta, query, *kv_list)


def attend_back(meta, query, kv_list, grad, out, lse, masked, types, name):
    n_query, grid, q_spec, kv_specs, l_spec, l_shape, keys = attention_specs(query, kv_list, masked)
    return pl.pallas_call(
        functools.partial(attend_back_kernel, sources=len(kv_list), n_query=n_query, masked=masked),
        grid_spec=pltpu.PrefetchScalarGridSpec(
            num_scalar_prefetch=1,
            grid=grid,
            in_specs=[q_spec] + kv_specs + [q_spec, q_spec, l_spec],
            out_specs=[q_spec] + kv_specs,
            scratch_shapes=[
                pltpu.VMEM((keys, HD + 16), bf16),
                pltpu.VMEM((keys, HD + 16), bf16),
                pltpu.VMEM((HD, keys), bf16),
                pltpu.VMEM((HD, keys), f32),
                pltpu.VMEM((HD, keys), f32),
            ],
        ),
        out_shape=[jax.ShapeDtypeStruct(query.shape, bf16)]
        + [jax.ShapeDtypeStruct(kv.shape, t) for kv, t in zip(kv_list, types)],
        compiler_params=pltpu.CompilerParams(vmem_limit_bytes=48 << 20),
        cost_estimate=cost(query, keys, 5),
        name=name,
    )(meta, query, *kv_list, grad, out, lse)


def gain_of(w_ref, first, k):
    return w_ref[0, :, first + k : first + k + 1].astype(f32)


def other_first(i, place, half):
    return jnp.where(i < half, (1 - place[1]) * half + i, place[1] * half + i - half)


def kernel_params():
    return pltpu.CompilerParams(vmem_limit_bytes=60 << 20)


def whole(value):
    return pl.BlockSpec(value.shape, lambda *i: (0,) * value.ndim)


def by_columns(count, body):
    step = min(128, count)

    def one(j, carry):
        body(pl.ds(pl.multiple_of(j * step, step), step))
        return carry

    lax.fori_loop(0, count // step, one, 0)


def norm_stats(resid):
    width = resid.shape[0]
    mean = jnp.sum(resid, 0, keepdims=True) / width
    square = jnp.sum(resid * resid, 0, keepdims=True) / width
    inv_std = lax.rsqrt(square - mean * mean + NORM_EPS)
    return (resid - mean) * inv_std, inv_std


def norm_back(grad, gain, normed, inv_std):
    width = grad.shape[0]
    scaled = grad * gain
    total = jnp.sum(scaled, 0, keepdims=True) / width
    cross = jnp.sum(scaled * normed, 0, keepdims=True) / width
    return inv_std * (scaled - total - normed * cross)


def project_kernel(place_ref, near_ref, *refs, rows):
    x_refs = refs[:rows]
    q_ref, kv_ref, near_t = refs[rows:]
    feat = q_ref.shape[2]
    step = pl.program_id(0)

    @pl.when(step == 0)
    def _():
        for d in range(near_ref.shape[0]):
            near_t[d] = near_ref[d].T

    for k, x_ref in enumerate(x_refs):

        @pl.when(step == k)
        def _():
            for d in range(near_ref.shape[0]):
                proj = dot(near_t[d, : 3 * feat, :], x_ref[...], 1, 0)
                q_ref[0, d] = (proj[:feat] * (0.125 * LOG2E)).astype(bf16)
                kv_ref[0, d, 0] = proj[feat : 2 * feat].astype(bf16)
                kv_ref[0, d, 1] = proj[2 * feat :].astype(bf16)


def project(place, near, x_rows, feat):
    dp, width, cols = near.shape
    rows = len(x_rows)
    tokens = x_rows[0].shape[1]
    return pl.pallas_call(
        functools.partial(project_kernel, rows=rows),
        grid_spec=pltpu.PrefetchScalarGridSpec(
            num_scalar_prefetch=1,
            grid=(rows,),
            in_specs=[whole(near)] + [whole(x) for x in x_rows],
            out_specs=[
                pl.BlockSpec((1, dp, feat, tokens), lambda k, p: (p[0] ^ k, 0, 0, 0)),
                pl.BlockSpec((1, dp, 2, feat, tokens), lambda k, p: (p[0] ^ k, 0, 0, 0, 0)),
            ],
            scratch_shapes=[pltpu.VMEM((dp, cols, width), bf16)],
        ),
        out_shape=[
            jax.ShapeDtypeStruct((rows, dp, feat, tokens), bf16),
            jax.ShapeDtypeStruct((rows, dp, 2, feat, tokens), bf16),
        ],
        compiler_params=kernel_params(),
        name="project",
    )(place, near, *x_rows)


def project_back_kernel(place_ref, near_ref, *refs, rows, sources):
    x_refs, dq_ref = refs[:rows], refs[rows]
    dkv_refs = refs[rows + 1 : rows + 1 + sources]
    dx_ref, gother_ref, gown_ref, acc = refs[rows + 1 + sources :]
    step = pl.program_id(0)
    feat = dq_ref.shape[2]

    @pl.when(step == 0)
    def _():
        acc[...] = jnp.zeros_like(acc)

    for k, x_ref in enumerate(x_refs):

        @pl.when(step == k)
        def _():
            total = None
            for d in range(near_ref.shape[0]):
                parts = [dq_ref[0, d]]
                for kind in range(2):
                    value = sum(ref[0, d, kind].astype(f32) for ref in dkv_refs)
                    parts.append(value.astype(bf16))
                grad = jnp.concatenate(parts, axis=0)
                acc[d, :, : 3 * feat] += dot(x_ref[...], grad, 1, 1)
                part = dot(near_ref[d, :, : 3 * feat], grad, 1, 0)
                total = part if total is None else total + part
            dx_ref[0] = total.astype(bf16)

    @pl.when(step == rows - 1)
    def _():
        gown_ref[...] = acc[place_ref[1]].astype(bf16)
        gother_ref[...] = acc[1 - place_ref[1]].astype(bf16)


def project_back(place, near, x_rows, d_query, d_kv):
    dp, width, cols = near.shape
    rows = len(x_rows)
    tokens = x_rows[0].shape[1]
    feat = d_query.shape[2]
    kv_spec = pl.BlockSpec((1, dp, 2, feat, tokens), lambda k, p: (p[0] ^ k, 0, 0, 0, 0))
    half = jax.ShapeDtypeStruct((width, cols), bf16)
    return pl.pallas_call(
        functools.partial(project_back_kernel, rows=rows, sources=len(d_kv)),
        grid_spec=pltpu.PrefetchScalarGridSpec(
            num_scalar_prefetch=1,
            grid=(rows,),
            in_specs=[whole(near)]
            + [whole(x) for x in x_rows]
            + [pl.BlockSpec((1, dp, feat, tokens), lambda k, p: (p[0] ^ k, 0, 0, 0))]
            + [kv_spec] * len(d_kv),
            out_specs=[
                pl.BlockSpec((1, width, tokens), lambda k, p: (p[0] ^ k, 0, 0)),
                whole(half),
                whole(half),
            ],
            scratch_shapes=[pltpu.VMEM(near.shape, f32)],
        ),
        out_shape=[
            jax.ShapeDtypeStruct((rows, width, tokens), bf16),
            half,
            half,
        ],
        compiler_params=kernel_params(),
        cost_estimate=pl.CostEstimate(
            flops=12 * rows * dp * width * feat * tokens, bytes_accessed=16 << 20, transcendentals=0
        ),
        name="project_back",
    )(place, near, *x_rows, d_query, *d_kv)


def side_by_side(chosen_ref, wide):
    count, _, tokens = chosen_ref.shape
    for n in range(count):
        wide[:, n * tokens : (n + 1) * tokens] = chosen_ref[n]


def cross_kv_kernel(w_ref, chosen_ref, o_ref, wide):
    @pl.when(pl.program_id(0) == 0)
    def _():
        side_by_side(chosen_ref, wide)

    weight = w_ref[0][:, : o_ref.shape[1]].T
    o_ref[0] = dot(weight, wide[...], 1, 0).astype(bf16)


def cross_kv(small, chosen, feat):
    groups, width, cols = small.shape
    keys = chosen.shape[0] * chosen.shape[2]
    return pl.pallas_call(
        cross_kv_kernel,
        grid=(groups,),
        in_specs=[pl.BlockSpec((1, width, 2 * 128), lambda g: (g, 0, 0)), whole(chosen)],
        out_specs=pl.BlockSpec((1, 2 * feat, keys), lambda g: (g, 0, 0)),
        out_shape=jax.ShapeDtypeStruct((groups, 2 * feat, keys), bf16),
        scratch_shapes=[pltpu.VMEM((width, keys), bf16)],
        compiler_params=kernel_params(),
        name="cross_kv",
    )(small, chosen)


def attn_place(g, rows):
    return g % rows, g // rows


def after_self_kernel(x_ref, attn_ref, w_ref, normed_ref, inv_ref, low_ref, cq_ref, acc):
    groups, feat, tokens = cq_ref.shape
    rows = attn_ref.shape[0]
    total = x_ref[...].astype(f32)
    for g in range(groups):
        r, d = attn_place(g, rows)
        total = total + dot(w_ref[g, :, 2 * feat : 3 * feat], attn_ref[r, d], 1, 0)
    acc[...] = total

    def body(at):
        normed, inv_std = norm_stats(acc[:, at])
        normed_ref[:, at] = normed
        inv_ref[:, at] = inv_std
        low_ref[:, at] = (normed * gain_of(w_ref, 5 * feat, 0)).astype(bf16)

    by_columns(tokens, body)
    low = low_ref[...]
    for g in range(groups):
        query = dot(w_ref[g, :, 3 * feat : 4 * feat], low, 0, 0)
        cq_ref[g] = (query * (0.125 * LOG2E)).astype(bf16)


def after_self(x_own, attn, small, feat):
    width, tokens = x_own.shape
    groups = small.shape[0]
    args = (x_own, attn, small)
    outs = [
        jax.ShapeDtypeStruct((width, tokens), f32),
        jax.ShapeDtypeStruct((1, tokens), f32),
        jax.ShapeDtypeStruct((width, tokens), bf16),
        jax.ShapeDtypeStruct((groups, feat, tokens), bf16),
    ]
    return pl.pallas_call(
        after_self_kernel,
        grid=(1,),
        in_specs=[whole(a) for a in args],
        out_specs=[whole(o) for o in outs],
        out_shape=outs,
        scratch_shapes=[pltpu.VMEM((width, tokens), f32)],
        compiler_params=kernel_params(),
        name="after_self",
    )(*args)


def middle_kernel(
    place_ref, normed_one_ref, catt_ref, wc_ref, up_ref, down_ref, cot_ref,
    out_ref, dcatt_ref, dy_ref, dcross_ref, gother_ref, gown_ref, dg_two_ref, dg_three_ref,
    acc, normed_two, inv_two, act, slope, h_fm, h_tm, d_fm, d_tm,
):
    i = pl.program_id(0)
    groups, feat, tokens = catt_ref.shape
    half = groups // 2
    units = up_ref.shape[2]
    step = min(256, tokens)

    @pl.when(i == 0)
    def _():
        total = normed_one_ref[...] * gain_of(wc_ref, feat, 0)
        for g in range(groups):
            total = total + dot(wc_ref[g, :, :feat], catt_ref[g], 1, 0)
        acc[...] = total

        def body(at):
            normed, inv_std = norm_stats(acc[:, at])
            normed_two[:, at] = normed
            inv_two[:, at] = inv_std
            value = normed * gain_of(wc_ref, feat, 1)
            acc[:, at] = value
            h_fm[:, at] = value.astype(bf16)

        by_columns(tokens, body)
        h_tm[...] = h_fm[...].T

    @pl.when(i < groups)
    def _():
        for t in range(0, tokens, step):
            upper = dot(h_tm[t : t + step, :], up_ref[0], 1, 0)
            cdf = 0.5 * (1.0 + lax.erf(upper * 0.7071067811865476))
            density = jnp.exp(-0.5 * upper * upper) * 0.3989422804014327
            act[i, t : t + step, :] = (upper * cdf).astype(bf16)
            slope[i, t : t + step, :] = (cdf + upper * density).astype(bf16)
        acc[...] += dot(down_ref[0], act[i], 1, 1)

    @pl.when(i == groups - 1)
    def _():
        dg_three_ref[...] = jnp.zeros_like(dg_three_ref)
        dg_two_ref[...] = jnp.zeros_like(dg_two_ref)

        def body(at):
            normed, inv_std = norm_stats(acc[:, at])
            gain = gain_of(wc_ref, feat, 2)
            out_ref[:, at] = (normed * gain).astype(bf16)
            grad = cot_ref[:, at].astype(f32)
            dg_three_ref[...] += grad * normed
            value = norm_back(grad, gain, normed, inv_std)
            acc[:, at] = value
            d_fm[:, at] = value.astype(bf16)

        by_columns(tokens, body)
        d_tm[...] = d_fm[...].T

    @pl.when(i >= groups)
    def _():
        g = other_first(i - groups, place_ref, half)
        for t in range(0, tokens, step):
            at = slice(t, t + step)
            back = dot(d_tm[at, :], down_ref[0], 1, 0) * slope[g, at, :].astype(f32)
            slope[g, at, :] = back.astype(bf16)
        g_down = dot(d_fm[...], act[g], 1, 0).astype(bf16)
        g_up = dot(h_fm[...], slope[g], 1, 0).astype(bf16)

        @pl.when(i < groups + half)
        def _():
            gother_ref[0, :, units:] = g_down
            gother_ref[0, :, :units] = g_up

        @pl.when(i >= groups + half)
        def _():
            gown_ref[0, :, units:] = g_down
            gown_ref[0, :, :units] = g_up

        acc[...] += dot(up_ref[0], slope[g], 1, 1)

    @pl.when(i == 2 * groups - 1)
    def _():
        def body(at):
            grad = acc[:, at]
            normed = normed_two[:, at]
            dg_two_ref[...] += grad * normed
            value = norm_back(grad, gain_of(wc_ref, feat, 1), normed, inv_two[:, at])
            dy_ref[:, at] = value
            dcross_ref[:, at] = value.astype(bf16)

        by_columns(tokens, body)
        low = dcross_ref[...]
        for g in range(groups):
            dcatt_ref[g] = dot(wc_ref[g, :, :feat], low, 0, 0).astype(bf16)


def middle(place, normed_one, catt, small, large, cot):
    width, tokens = normed_one.shape
    groups, feat, _ = catt.shape
    half = groups // 2
    units = large.shape[2] // 2
    lanes = min(128, tokens)

    def weight(kind):
        def index(i, p):
            return jnp.where(i < groups, i, other_first(i - groups, p, half)), 0, kind

        return pl.BlockSpec((1, width, units), index)

    def grad_out(first):
        return pl.BlockSpec(
            (1, width, 2 * units), lambda i, p: (jnp.clip(i - first, 0, half - 1), 0, 0)
        )

    outs = [
        jax.ShapeDtypeStruct((width, tokens), bf16),
        jax.ShapeDtypeStruct(catt.shape, bf16),
        jax.ShapeDtypeStruct((width, tokens), f32),
        jax.ShapeDtypeStruct((width, tokens), bf16),
        jax.ShapeDtypeStruct((half, width, 2 * units), bf16),
        jax.ShapeDtypeStruct((half, width, 2 * units), bf16),
        jax.ShapeDtypeStruct((width, lanes), f32),
        jax.ShapeDtypeStruct((width, lanes), f32),
    ]
    specs = [whole(o) for o in outs]
    specs[4], specs[5] = grad_out(groups), grad_out(groups + half)
    return pl.pallas_call(
        middle_kernel,
        grid_spec=pltpu.PrefetchScalarGridSpec(
            num_scalar_prefetch=1,
            grid=(2 * groups,),
            in_specs=[
                whole(normed_one),
                whole(catt),
                pl.BlockSpec((groups, width, 128), lambda i, p: (0, 0, 3)),
                weight(0),
                weight(1),
                whole(cot),
            ],
            out_specs=specs,
            scratch_shapes=[
                pltpu.VMEM((width, tokens), f32),
                pltpu.VMEM((width, tokens), f32),
                pltpu.VMEM((1, tokens), f32),
                pltpu.VMEM((groups, tokens, units), bf16),
                pltpu.VMEM((groups, tokens, units), bf16),
                pltpu.VMEM((width, tokens), bf16),
                pltpu.VMEM((tokens, width), bf16),
                pltpu.VMEM((width, tokens), bf16),
                pltpu.VMEM((tokens, width), bf16),
            ],
        ),
        out_shape=outs,
        compiler_params=kernel_params(),
        cost_estimate=pl.CostEstimate(
            flops=12 * groups * width * units * tokens, bytes_accessed=8 * large.size, transcendentals=0
        ),
        name="middle",
    )(place, normed_one, catt, small, large, large, cot)


def before_self_kernel(
    dcq_ref, w_ref, dy_ref, normed_ref, inv_ref,
    dattn_ref, dlow_ref, dy_one_ref, dg_ref, acc,
):
    groups, feat, tokens = dcq_ref.shape
    rows = dattn_ref.shape[0]
    total = dy_ref[...]
    for g in range(groups):
        total = total + dot(w_ref[g, :, 3 * feat : 4 * feat], dcq_ref[g], 1, 0)
    acc[...] = total
    dg_ref[...] = jnp.zeros_like(dg_ref)

    def body(at):
        grad = acc[:, at]
        normed = normed_ref[:, at]
        dg_ref[...] += grad * normed
        value = norm_back(grad, gain_of(w_ref, 5 * feat, 0), normed, inv_ref[:, at])
        dy_one_ref[:, at] = value
        dlow_ref[:, at] = value.astype(bf16)

    by_columns(tokens, body)
    low = dlow_ref[...]
    for g in range(groups):
        r, d = attn_place(g, rows)
        dattn_ref[r, d] = dot(w_ref[g, :, 2 * feat : 3 * feat], low, 0, 0).astype(bf16)


def before_self(d_cq, small, dy_two, normed_one, inv_one, attn_shape):
    width, tokens = dy_two.shape
    args = (d_cq, small, dy_two, normed_one, inv_one)
    outs = [
        jax.ShapeDtypeStruct(attn_shape, bf16),
        jax.ShapeDtypeStruct((width, tokens), bf16),
        jax.ShapeDtypeStruct((width, tokens), f32),
        jax.ShapeDtypeStruct((width, min(128, tokens)), f32),
    ]
    return pl.pallas_call(
        before_self_kernel,
        grid=(1,),
        in_specs=[whole(a) for a in args],
        out_specs=[whole(o) for o in outs],
        out_shape=outs,
        scratch_shapes=[pltpu.VMEM((width, tokens), f32)],
        compiler_params=kernel_params(),
        name="before_self",
    )(*args)


def small_grads_kernel(
    place_ref, w_ref, chosen_ref, dckv_ref, attn_ref, dcq_ref, catt_ref, dlow_ref, h_ref,
    dcross_ref, dg_one_ref, dg_two_ref, dg_three_ref, rother_ref, rown_ref, cother_ref, cown_ref,
    wide, acc, gain_cols, *, paired,
):
    g = pl.program_id(0)
    feat2 = dckv_ref.shape[1]
    feat = feat2 // 2
    count, width, tokens = chosen_ref.shape
    share = count // 2
    half = pl.num_programs(0) // 2

    @pl.when(g == 0)
    def _():
        side_by_side(chosen_ref, wide)
        col = lax.broadcasted_iota(jnp.int32, gain_cols.shape, 1)
        total = jnp.zeros(gain_cols.shape, f32)
        for k, ref in enumerate((dg_one_ref, dg_two_ref, dg_three_ref)):
            total = jnp.where(col == k, jnp.sum(ref[...], axis=1, keepdims=True), total)
        gain_cols[...] = total.astype(bf16)
        acc[...] = jnp.zeros_like(acc)

    grad = dckv_ref[0]
    acc[...] += dot(w_ref[0][:, :feat2], grad, 1, 0)
    parts = [dot(wide[...], grad, 1, 1).astype(bf16)]
    pairs = ((dlow_ref, attn_ref[0, 0]), (h_ref, dcq_ref[0]), (dcross_ref, catt_ref[0]))
    for left, right in pairs:
        parts.append(dot(left[...], right, 1, 1).astype(bf16))
    parts.append(gain_cols[...])

    def put(ref):
        at = 0
        for part in parts:
            ref[0, :, at : at + part.shape[1]] = part
            at += part.shape[1]

    @pl.when(g < half)
    def _():
        put(rother_ref)

    @pl.when(g >= half)
    def _():
        put(rown_ref)

    @pl.when(g == pl.num_programs(0) - 1)
    def _():
        for n in range(count):
            piece = acc[:, n * tokens : (n + 1) * tokens].astype(bf16)
            if paired:
                ref = cother_ref if n % 2 else cown_ref
                ref[place_ref[0] ^ (n // 2)] = piece
                continue
            mine = place_ref[1] == n // share

            @pl.when(mine)
            def _():
                cown_ref[n % share] = piece

            @pl.when(jnp.logical_not(mine))
            def _():
                cother_ref[n % share] = piece


def small_grads(place, small, chosen, d_ckv, attn, d_cq, catt, d_low, h_low, d_cross, dgs, paired):
    groups, width, cols = small.shape
    _, feat2, keys = d_ckv.shape
    feat = feat2 // 2
    tokens = d_low.shape[1]
    rows = attn.shape[0]
    half = groups // 2

    def order(g, p):
        return other_first(g, p, half)

    def rest_out(first):
        return pl.BlockSpec((1, width, cols), lambda g, p: (jnp.clip(g - first, 0, half - 1), 0, 0))

    piece = pl.BlockSpec((1, feat, tokens), lambda g, p: (order(g, p), 0, 0))
    share = jax.ShapeDtypeStruct((chosen.shape[0] // 2,) + chosen.shape[1:], bf16)
    rest_shape = jax.ShapeDtypeStruct((half, width, cols), bf16)
    return pl.pallas_call(
        functools.partial(small_grads_kernel, paired=paired),
        grid_spec=pltpu.PrefetchScalarGridSpec(
            num_scalar_prefetch=1,
            grid=(groups,),
            in_specs=[
                pl.BlockSpec((1, width, 2 * 128), lambda g, p: (order(g, p), 0, 0)),
                whole(chosen),
                pl.BlockSpec((1, feat2, keys), lambda g, p: (order(g, p), 0, 0)),
                pl.BlockSpec(
                    (1, 1, feat, tokens),
                    lambda g, p: (order(g, p) % rows, order(g, p) // rows, 0, 0),
                ),
                piece,
                piece,
                whole(d_low),
                whole(h_low),
                whole(d_cross),
            ]
            + [whole(v) for v in dgs],
            out_specs=[rest_out(0), rest_out(half), whole(share), whole(share)],
            scratch_shapes=[
                pltpu.VMEM((width, keys), bf16),
                pltpu.VMEM((width, keys), f32),
                pltpu.VMEM((width, cols - 5 * feat), bf16),
            ],
        ),
        out_shape=[rest_shape, rest_shape, share, share],
        compiler_params=kernel_params(),
        cost_estimate=pl.CostEstimate(
            flops=groups * width * (4 * feat2 * keys + 6 * feat * tokens),
            bytes_accessed=4 * small.size,
            transcendentals=0,
        ),
        name="small_grads",
    )(place, small, chosen, d_ckv, attn, d_cq, catt, d_low, h_low, d_cross, *dgs)


def mm(spec, left, right):
    return jnp.einsum(spec, left, right, preferred_element_type=f32)


def per_device(
    x_in, prefix, enc_bank, bank_rows, w_qkv, w_out, w_cross_q, w_cross_kv, w_cross_out,
    w_up, w_down, ln_gains, out_grad,
):
    dp, rows, cols = lax.axis_size("dp"), lax.axis_size("row"), lax.axis_size("col")
    d_pos, r_pos, c_pos = lax.axis_index("dp"), lax.axis_index("row"), lax.axis_index("col")
    own_seqs, part_width, row_len = x_in.shape
    seqs = own_seqs * dp
    sub = cols // seqs
    parts = dp * sub
    width = part_width * cols
    tokens = row_len // parts
    heads = w_qkv.shape[2]
    feat = heads * HALF
    units = w_up.shape[1]
    odd = (r_pos % 2) == 1
    seq_pos = c_pos // sub
    part_pos = d_pos * sub + c_pos % sub
    groups = [[s * sub + k for k in range(sub)] for s in range(seqs)]
    everywhere = ("dp", "row", "col")
    swap = [(0, 1), (1, 0)]
    first_core = d_pos == 0

    def flip(value):
        return jnp.where(odd, value[:, :, ::-1], value)

    def swap_cores(value):
        take = value.shape[-1] // parts
        if parts == 2:
            low, high = value[..., :take], value[..., take:]
            upper = first_core == odd
            got = lax.ppermute(jnp.where(upper, low, high), "dp", swap)
            kept = jnp.where(upper, high, low)
            value = jnp.concatenate(
                [jnp.where(first_core, kept, got), jnp.where(first_core, got, kept)], axis=0
            )
        else:
            value = flip(value.reshape(own_seqs, part_width, parts, take))
            value = value.reshape(own_seqs, part_width, dp, sub, take)
            value = lax.all_to_all(value, "dp", 2, 0, tiled=True)
            value = value.reshape(seqs, part_width, sub, take).transpose(0, 2, 1, 3)
        return value.reshape(cols, part_width, take)

    def across_cols(value):
        return lax.all_to_all(value, "col", 0, 0, tiled=True).reshape(width, value.shape[-1])

    def to_tokens(value):
        return across_cols(swap_cores(value))

    def row_gather(value):
        if rows != 4:
            every = lax.all_gather(value, "row", axis=0)
            return [lax.dynamic_index_in_dim(every, r_pos ^ k, 0, False) for k in range(rows)]

        def send(v, k):
            return lax.ppermute(v, "row", [(i, i ^ k) for i in range(rows)])

        near_one, near_two = send(value, 1), send(value, 2)
        half = value.shape[0] // 2
        far = jnp.concatenate([send(near_two[:half], 1), send(near_one[half:], 2)], axis=0)
        return [value, near_one, near_two, far]

    def home_cols(value):
        value = value.reshape(cols, part_width, value.shape[-1])
        return lax.all_to_all(value, "col", 0, 0, tiled=True)

    def to_home(value):
        return home_cores(home_cols(value))

    def home_cores(value):
        take = value.shape[-1]
        if parts == 2:
            early, late = value[:own_seqs], value[own_seqs:]
            got = lax.ppermute(jnp.where(first_core, late, early), "dp", swap)
            kept = jnp.where(first_core, early, late)
            upper = first_core == odd
            return jnp.concatenate(
                [jnp.where(upper, got, kept), jnp.where(upper, kept, got)], axis=-1
            )
        value = value.reshape(seqs, sub, part_width, take).transpose(0, 2, 1, 3)
        value = value.reshape(seqs, part_width, 1, sub, take)
        value = lax.all_to_all(value, "dp", 0, 2, tiled=True)
        value = flip(value.reshape(own_seqs, part_width, parts, take))
        return value.reshape(own_seqs, part_width, parts * take)

    place = jnp.stack([r_pos, d_pos]).astype(jnp.int32)
    qkv = jnp.pad(w_qkv.reshape(part_width, 3 * feat), ((0, 0), (0, 384 - 3 * feat)))
    near = lax.all_gather(qkv, ("dp", "col"), axis=0).reshape(dp, width, qkv.shape[1])
    x_swapped = swap_cores(x_in)
    x_own = across_cols(x_swapped)
    x_rows = row_gather(x_own)
    tied, _ = lax.optimization_barrier(
        ((w_cross_kv, w_out, w_cross_q, w_cross_out, w_up, w_down, ln_gains), x_swapped)
    )
    small = jnp.concatenate(
        [
            tied[0].reshape(part_width, 2 * feat),
            tied[1].reshape(feat, part_width).T,
            tied[2].reshape(part_width, feat),
            tied[3].reshape(feat, part_width).T,
            tied[6].T,
            jnp.zeros((part_width, 512 - 5 * feat - 3), bf16),
        ],
        axis=1,
    )
    blocks = dp * rows

    def gather_all(value):
        value = lax.all_gather(value, everywhere, axis=0)
        return value.reshape(blocks, width, value.shape[-1])

    small_all = gather_all(small)
    large, _ = lax.optimization_barrier((jnp.concatenate([tied[4], tied[5].T], axis=1), x_own))
    large_all = gather_all(large)

    query, kv_own = project(place, near, x_rows, feat)
    query = query.reshape(rows, dp, heads, HALF, tokens)
    kv_own = kv_own.reshape(rows, dp, 2, heads, HALF, tokens)

    def index_of(row, part):
        return jnp.where(row % 2 == 1, parts - 1 - part, part) + row * parts

    row_ids = jnp.arange(rows, dtype=jnp.int32)
    if sub == 1:
        kv_list = [kv_own, lax.ppermute(kv_own, "dp", swap)]
        owners = [part_pos, 1 - part_pos]
    else:
        kv_all = lax.all_gather(kv_own, "col", axis=0, axis_index_groups=groups)
        kv_all = lax.all_gather(kv_all, "dp", axis=0).reshape((parts,) + kv_own.shape)
        kv_list = [kv_all[j] for j in range(parts)]
        owners = list(range(parts))
    q_start = index_of(row_ids, part_pos) * tokens
    places = [index_of(row_ids, owner) for owner in owners]
    seq_prefix = lax.all_gather(prefix, "dp", axis=0, tiled=True)[seq_pos]
    meta = jnp.concatenate([seq_prefix[None], q_start] + places).astype(jnp.int32)
    mixed, lse = attend(meta, query, kv_list, True, "self_attention")
    attn = lax.all_to_all(mixed, "row", 0, 0, tiled=True).reshape(rows, dp, feat, tokens)
    normed_one, inv_one, h_low, cross_q = after_self(x_own, attn, small_all, feat)
    cross_q = cross_q.reshape(1, dp, rows, heads, HALF, tokens)

    picked = bank_rows.shape[1] // rows
    row_pick = lax.dynamic_slice_in_dim(bank_rows, r_pos * picked, picked, 1)
    bank_ids = jnp.arange(enc_bank.shape[2], dtype=jnp.int32)
    hot = (bank_ids[None, :, None] == row_pick[:, None, :]).astype(bf16)
    chosen = to_tokens(mm("swn,snp->swp", enc_bank, hot).astype(bf16))
    c_tokens = chosen.shape[1]
    if sub > 1:
        chosen = lax.all_gather(chosen, "col", axis=0, axis_index_groups=groups)
        chosen = lax.all_gather(chosen, ("dp", "row"), axis=0)
        chosen = chosen.reshape(blocks * sub, width, c_tokens)
    else:
        pair = jnp.stack([chosen, lax.ppermute(chosen, "dp", swap)])
        chosen = jnp.concatenate(row_gather(pair), axis=0)
    ckv = cross_kv(small_all, chosen, feat)
    ckv = ckv.reshape(1, dp, rows, 2, heads, HALF, ckv.shape[-1])
    catt, lse_cross = attend(meta, cross_q, [ckv], False, "cross_attention")
    catt_flat = catt.reshape(blocks, feat, tokens)

    cot = to_tokens(out_grad)
    block_out, d_catt, dy_two, d_cross, g_other, g_own, dg_two, dg_three = middle(
        place, normed_one, catt_flat, small_all, large_all, cot
    )
    block_out = home_cols(block_out)


    def with_core(own, got):
        return (own.astype(f32) + got.astype(f32)).astype(bf16)

    g_other = lax.ppermute(g_other, "dp", swap)
    d_cq, d_ckv = attend_back(
        meta, cross_q, [ckv], d_catt.reshape(catt.shape), catt, lse_cross, False, [bf16],
        "cross_attention_back",
    )
    g_other, d_cq, block_out = lax.optimization_barrier((g_other, d_cq, block_out))
    large_grad, d_cq = lax.optimization_barrier((with_core(g_own, g_other), d_cq))
    large_grad = large_grad.reshape(rows, cols, part_width, 2 * units)
    large_grad = lax.psum_scatter(large_grad, "row", scatter_dimension=0, tiled=False)
    d_cq = d_cq.reshape(blocks, feat, tokens)
    d_ckv = d_ckv.reshape(blocks, 2 * feat, d_ckv.shape[-1])
    d_attn, d_low, dy_one, dg_one = before_self(
        d_cq, small_all, dy_two, normed_one, inv_one, attn.shape
    )
    d_mixed = lax.all_to_all(d_attn, "row", 0, 0, tiled=True).reshape(mixed.shape)
    rest_other, rest, chosen_other, d_chosen = small_grads(
        place, small_all, chosen, d_ckv, attn, d_cq, catt_flat, d_low, h_low, d_cross,
        (dg_one, dg_two, dg_three), sub == 1,
    )
    d_mixed, rest_other, rest, chosen_other, d_chosen = lax.optimization_barrier(
        (d_mixed, rest_other, rest, chosen_other, d_chosen)
    )
    rest = with_core(rest, lax.ppermute(rest_other, "dp", swap))
    d_chosen = with_core(d_chosen, lax.ppermute(chosen_other, "dp", swap))
    rest, d_mixed, d_chosen = lax.optimization_barrier((rest, d_mixed, d_chosen))
    rest = rest.reshape(rows, cols, part_width, -1)
    rest = lax.psum_scatter(rest, "row", scatter_dimension=0, tiled=False)
    d_chosen = d_chosen.reshape(rows, sub * width, c_tokens)
    d_chosen = lax.all_to_all(d_chosen, "row", 0, 0, tiled=True)

    types = [f32] + [bf16] * (len(kv_list) - 1) if sub == 1 else [bf16] * len(kv_list)
    d_query, *d_kv = attend_back(
        meta, query, kv_list, d_mixed, mixed, lse, True, types, "self_attention_back"
    )
    d_query, d_chosen, rest, large_grad = lax.optimization_barrier(
        (d_query, d_chosen, rest, large_grad)
    )
    joined = jnp.concatenate([large_grad, rest], axis=2)
    joined, d_query = lax.optimization_barrier((joined, d_query))
    joined = lax.psum_scatter(joined, "col", scatter_dimension=0, tiled=False)
    if sub == 1:
        d_kv = [d_kv[0], lax.ppermute(d_kv[1], "dp", swap)]
    else:
        d_kv = jnp.stack(d_kv).reshape((dp, sub) + kv_own.shape)
        d_kv = lax.psum_scatter(d_kv, "dp", scatter_dimension=0, tiled=True)
        d_kv = lax.psum_scatter(
            d_kv, "col", scatter_dimension=1, tiled=True, axis_index_groups=groups
        )
        d_kv = [d_kv]
    kv_shape = (rows, dp, 2, feat, tokens)
    d_kv = [value.reshape(kv_shape) for value in d_kv]
    dx_part, qkv_other, g_qkv = project_back(
        place, near, x_rows, d_query.reshape(rows, dp, feat, tokens), d_kv
    )
    dx_part = lax.all_to_all(dx_part, "row", 0, 0, tiled=True)
    dx_part, joined = lax.optimization_barrier((dx_part, joined))
    joined = joined.astype(f32)
    dx = dy_one + jnp.sum(dx_part.astype(f32), axis=0)
    x_moved = home_cols(dx.astype(bf16))

    d_chosen = jnp.sum(d_chosen.astype(f32), axis=0).astype(bf16)
    if sub > 1:
        d_chosen = lax.psum_scatter(
            d_chosen.reshape(sub, width, c_tokens), "col", scatter_dimension=0, tiled=True,
            axis_index_groups=groups,
        )
    d_chosen = d_chosen.reshape(width, c_tokens)
    d_chosen = jnp.concatenate(row_gather(to_home(d_chosen)), axis=2)
    pick_rows = jnp.concatenate(
        [
            lax.dynamic_slice_in_dim(bank_rows, (r_pos ^ k) * picked, picked, 1)
            for k in range(rows)
        ],
        axis=1,
    )
    hot_all = (pick_rows[:, :, None] == bank_ids[None, None, :]).astype(bf16)
    bank_grad = mm("swp,spn->swn", d_chosen, hot_all)
    x_moved, bank_grad = lax.optimization_barrier((x_moved, bank_grad))
    x_grad = home_cores(x_moved).astype(f32)

    qkv = with_core(g_qkv, lax.ppermute(qkv_other, "dp", swap))
    qkv_grad = lax.psum_scatter(
        qkv.reshape(cols, part_width, -1), "col", scatter_dimension=0, tiled=False
    ).astype(f32)
    large_grad, rest = joined[:, : 2 * units], joined[:, 2 * units :]

    return (
        home_cores(block_out),
        x_grad,
        bank_grad,
        qkv_grad[:, : 3 * feat].reshape(w_qkv.shape),
        rest[:, 2 * feat : 3 * feat].T.reshape(w_out.shape),
        rest[:, 3 * feat : 4 * feat].reshape(w_cross_q.shape),
        rest[:, : 2 * feat].reshape(w_cross_kv.shape),
        rest[:, 4 * feat : 5 * feat].T.reshape(w_cross_out.shape),
        large_grad[:, :units],
        large_grad[:, units:].T,
        rest[:, 5 * feat : 5 * feat + 3].T,
    )


def solution(mesh):
    placed = (
        P("dp", "col", "row"),
        P("dp"),
        P("dp", "col", None),
        P("dp", None),
        P("col", None, "row", "dp"),
        P("row", "dp", "col"),
        P("col", "row", "dp"),
        P("col", None, "row", "dp"),
        P("row", "dp", "col"),
        P("col", ("dp", "row")),
        P(("dp", "row"), "col"),
        P(None, "col"),
        P("dp", "col", "row"),
    )
    return jax.shard_map(
        per_device,
        mesh=mesh,
        in_specs=placed,
        out_specs=(
            P("dp", "col", "row"),
            P("dp", "col", "row"),
            P("dp", "col", None),
            P("col", None, "row", "dp"),
            P("row", "dp", "col"),
            P("col", "row", "dp"),
            P("col", None, "row", "dp"),
            P("row", "dp", "col"),
            P("col", ("dp", "row")),
            P(("dp", "row"), "col"),
            P(None, "col"),
        ),
        check_vma=False,
    )
```

```python
import functools

import jax
import jax.numpy as jnp
from jax import lax
from jax.experimental import pallas as pl
from jax.experimental.layout import Layout, with_layout_constraint
from jax.experimental.pallas import tpu as pltpu
from jax.sharding import PartitionSpec as P

bf16 = jnp.bfloat16
f32 = jnp.float32
HD = 64
HALF = 32
NORM_EPS = 1e-05
NEG = -1e30
LIMIT = 90.0
LN2 = 0.6931471805599453
LOG2E = 1.4426950408889634
KB = 512


def dot(left, right, left_dim, right_dim):
    return lax.dot_general(
        left, right, (((left_dim,), (right_dim,)), ((), ())), preferred_element_type=f32
    )


def ones_rows(count, shape, dim):
    return jnp.where(lax.broadcasted_iota(jnp.int32, shape, dim) < count, 1.0, 0.0).astype(bf16)


def allowed_block(meta, i, start, width, cols):
    k_pos = start + lax.broadcasted_iota(jnp.int32, (width, cols), 0)
    q_pos = meta[1 + i] + lax.broadcasted_iota(jnp.int32, (1, cols), 1)
    return k_pos <= jnp.maximum(q_pos, meta[0] - 1)


def block_range(meta, i, cols):
    full = jnp.maximum(meta[1 + i], meta[0]) // KB
    total = (jnp.maximum(meta[1 + i] + cols, meta[0]) + KB - 1) // KB
    return full, total


def over_keys(meta, i, cols, keys, masked, step, carry):
    if not masked:
        for start in range(0, keys, KB):
            carry = step(start, carry, False, KB)
        return carry
    full, total = block_range(meta, i, cols)
    pairs = full // 2
    carry = lax.fori_loop(0, pairs, lambda j, c: step(j * 2 * KB, c, False, 2 * KB), carry)
    carry = lax.fori_loop(2 * pairs, full, lambda j, c: step(j * KB, c, False, KB), carry)
    return lax.fori_loop(full, total, lambda j, c: step(j * KB, c, True, KB), carry)


def pieces(kv_refs, masked):
    out = []
    for ref in kv_refs:
        count = ref.shape[0]
        for b in range(count):
            out.append((ref, b))
    return out


def piece_start(meta, n_query, index, length, masked):
    if masked:
        return pl.multiple_of(meta[1 + n_query + index] * length, length)
    return index * length


def attend_kernel(*refs, sources, n_query, masked):
    meta, q_ref = refs[:2]
    kv_refs = refs[2 : 2 + sources]
    o_ref, l_ref, key_rows, val_cols = refs[2 + sources :]
    i = pl.program_id(1)
    cols = q_ref.shape[-1]
    keys = val_cols.shape[-1]

    @pl.when(i == 0)
    def _():
        key_rows[:, HD:] = ones_rows(1, (keys, 16), 1)
        val_cols[HD:, :] = ones_rows(1, (16, keys), 0)
        for index, (ref, b) in enumerate(pieces(kv_refs, masked)):
            length = ref.shape[-1]
            at = pl.ds(piece_start(meta, n_query, index, length, masked), length)
            key_rows[at, :HD] = ref[b, :, 0, 0].reshape(HD, length).T
            val_cols[:HD, at] = ref[b, :, 1, 0].reshape(HD, length)

    query = q_ref[0, :, 0].reshape(HD, cols)
    first = dot(key_rows[0:128, :HD], query, 1, 0)
    shift = jnp.max(first, axis=0, keepdims=True).astype(bf16).astype(f32)
    row = lax.broadcasted_iota(jnp.int32, (16, cols), 0)
    query_more = jnp.concatenate([query, jnp.where(row == 0, -shift, 0.0).astype(bf16)], axis=0)

    def step(start, carry, mask, width):
        top, acc = carry
        at = pl.ds(pl.multiple_of(start, KB), width)
        scores = dot(key_rows[at, :], query_more, 1, 0)
        if mask:
            scores = jnp.where(allowed_block(meta, i, start, width, cols), scores, NEG)
        top = jnp.maximum(top, jnp.max(scores, axis=0, keepdims=True))
        acc = acc + dot(val_cols[:, at], jnp.exp2(scores).astype(bf16), 1, 0)
        return top, acc

    def put(shift, acc):
        total = acc[HD : HD + 1, :]
        mixed = (acc[:HD] * (1.0 / total)).astype(bf16)
        o_ref[0, :, 0] = mixed.reshape(2, HALF, cols)
        l_ref[0, 0] = shift + jnp.log2(total)

    start = (jnp.full((1, cols), NEG, f32), jnp.zeros((HD + 16, cols), f32))
    top, acc = over_keys(meta, i, cols, keys, masked, step, start)
    put(shift, acc)

    @pl.when(jnp.max(top) > LIMIT)
    def _():
        def careful(j, carry):
            high, acc = carry
            at = pl.ds(pl.multiple_of(j * KB, KB), KB)
            scores = dot(key_rows[at, :HD], query, 1, 0)
            if masked:
                scores = jnp.where(allowed_block(meta, i, j * KB, KB, cols), scores, NEG)
            new = jnp.maximum(high, jnp.max(scores, axis=0, keepdims=True))
            part = dot(val_cols[:, at], jnp.exp2(scores - new).astype(bf16), 1, 0)
            return new, acc * jnp.exp2(high - new) + part

        total = block_range(meta, i, cols)[1] if masked else keys // KB
        put(*lax.fori_loop(0, total, careful, start))


def attend_back_kernel(*refs, sources, n_query, masked):
    meta, q_ref = refs[:2]
    kv_refs = refs[2 : 2 + sources]
    g_ref, o_ref, l_ref = refs[2 + sources : 5 + sources]
    dq_ref = refs[5 + sources]
    dkv_refs = refs[6 + sources : 6 + 2 * sources]
    key_rows, val_rows, key_cols, dk_acc, dv_acc = refs[6 + 2 * sources :]
    i = pl.program_id(1)
    cols = q_ref.shape[-1]
    keys = key_cols.shape[-1]

    @pl.when(i == 0)
    def _():
        key_rows[:, HD:] = ones_rows(3, (keys, 16), 1)
        val_rows[:, HD:] = ones_rows(3, (keys, 16), 1)
        for index, (ref, b) in enumerate(pieces(kv_refs, masked)):
            length = ref.shape[-1]
            at = pl.ds(piece_start(meta, n_query, index, length, masked), length)
            k_part = ref[b, :, 0, 0].reshape(HD, length)
            key_cols[:, at] = k_part
            key_rows[at, :HD] = k_part.T
            val_rows[at, :HD] = ref[b, :, 1, 0].reshape(HD, length).T
        dk_acc[...] = jnp.zeros_like(dk_acc)
        dv_acc[...] = jnp.zeros_like(dv_acc)

    query = q_ref[0, :, 0].reshape(HD, cols)
    grad = g_ref[0, :, 0].reshape(HD, cols)
    delta = jnp.sum(
        grad.astype(f32) * o_ref[0, :, 0].reshape(HD, cols).astype(f32), axis=0, keepdims=True
    )

    def with_shift(value, shift):
        high = shift.astype(bf16).astype(f32)
        mid = (shift - high).astype(bf16).astype(f32)
        low = shift - high - mid
        row = lax.broadcasted_iota(jnp.int32, (16, cols), 0)
        more = jnp.where(row == 0, -high, jnp.where(row == 1, -mid, jnp.where(row == 2, -low, 0.0)))
        return jnp.concatenate([value, more.astype(bf16)], axis=0)

    query_more = with_shift(query, l_ref[0, 0])
    grad_more = with_shift(grad, delta)

    def step(start, dq, mask, width):
        at = pl.ds(pl.multiple_of(start, KB), width)
        scores = dot(key_rows[at, :], query_more, 1, 0)
        if mask:
            scores = jnp.where(allowed_block(meta, i, start, width, cols), scores, NEG)
        probs = jnp.exp2(scores)
        grad_scores = (probs * dot(val_rows[at, :], grad_more, 1, 0)).astype(bf16)
        dv_acc[:, at] += dot(grad, probs.astype(bf16), 1, 1)
        dk_acc[:, at] += dot(query, grad_scores, 1, 1)
        return dq + dot(key_cols[:, at], grad_scores, 1, 0)

    dq = over_keys(meta, i, cols, keys, masked, step, jnp.zeros((HD, cols), f32))
    dq_ref[0, :, 0] = (dq * 0.125).astype(bf16).reshape(2, HALF, cols)

    @pl.when(i == n_query - 1)
    def _():
        for index, (ref, b) in enumerate(pieces(dkv_refs, masked)):
            length = ref.shape[-1]
            at = pl.ds(piece_start(meta, n_query, index, length, masked), length)
            ref[b, :, 0, 0] = (dk_acc[:, at] * LN2).astype(ref.dtype).reshape(2, HALF, length)
            ref[b, :, 1, 0] = dv_acc[:, at].astype(ref.dtype).reshape(2, HALF, length)


def attention_specs(query, kv_list, masked):
    cols = query.shape[-1]
    if masked:
        n_query, _, heads = query.shape[:3]
        grid = (heads, n_query)
        q_spec = pl.BlockSpec((1, 2, 1, HALF, cols), lambda h, i, m: (i, 0, h, 0, 0))
        kv_specs = [
            pl.BlockSpec(kv.shape[:3] + (1,) + kv.shape[4:], lambda h, i, m: (0, 0, 0, h, 0, 0))
            for kv in kv_list
        ]
        l_spec = pl.BlockSpec((1, 1, 1, cols), lambda h, i, m: (h, i, 0, 0))
        l_shape = (heads, n_query, 1, cols)
        keys = sum(kv.shape[0] * kv.shape[-1] for kv in kv_list)
    else:
        n_query = 1
        _, _, rows, heads = query.shape[:4]
        grid = (rows * heads, 1)
        q_spec = pl.BlockSpec(
            (1, 2, None, 1, HALF, cols), lambda g, i, m: (0, 0, g // heads, g % heads, 0, 0)
        )
        kv_specs = [
            pl.BlockSpec(
                (kv.shape[0], 2, None, 2, 1) + kv.shape[5:],
                lambda g, i, m: (0, 0, g // heads, 0, g % heads, 0, 0),
            )
            for kv in kv_list
        ]
        l_spec = pl.BlockSpec((1, 1, 1, cols), lambda g, i, m: (g, 0, 0, 0))
        l_shape = (rows * heads, 1, 1, cols)
        keys = sum(kv.shape[0] * kv.shape[-1] for kv in kv_list)
    return n_query, grid, q_spec, kv_specs, l_spec, l_shape, keys


def cost(query, keys, dots):
    pairs = query.size // HD * keys
    return pl.CostEstimate(
        flops=2 * pairs * 256 * dots // 2, bytes_accessed=query.size * 16, transcendentals=pairs
    )


def attend(meta, query, kv_list, masked, name):
    n_query, grid, q_spec, kv_specs, l_spec, l_shape, keys = attention_specs(query, kv_list, masked)
    return pl.pallas_call(
        functools.partial(attend_kernel, sources=len(kv_list), n_query=n_query, masked=masked),
        grid_spec=pltpu.PrefetchScalarGridSpec(
            num_scalar_prefetch=1,
            grid=grid,
            in_specs=[q_spec] + kv_specs,
            out_specs=[q_spec, l_spec],
            scratch_shapes=[pltpu.VMEM((keys, HD + 16), bf16), pltpu.VMEM((HD + 16, keys), bf16)],
        ),
        out_shape=[
            jax.ShapeDtypeStruct(query.shape, bf16),
            jax.ShapeDtypeStruct(l_shape, f32),
        ],
        compiler_params=pltpu.CompilerParams(vmem_limit_bytes=48 << 20),
        cost_estimate=cost(query, keys, 2),
        name=name,
    )(meta, query, *kv_list)


def attend_back(meta, query, kv_list, grad, out, lse, masked, types, name):
    n_query, grid, q_spec, kv_specs, l_spec, l_shape, keys = attention_specs(query, kv_list, masked)
    return pl.pallas_call(
        functools.partial(attend_back_kernel, sources=len(kv_list), n_query=n_query, masked=masked),
        grid_spec=pltpu.PrefetchScalarGridSpec(
            num_scalar_prefetch=1,
            grid=grid,
            in_specs=[q_spec] + kv_specs + [q_spec, q_spec, l_spec],
            out_specs=[q_spec] + kv_specs,
            scratch_shapes=[
                pltpu.VMEM((keys, HD + 16), bf16),
                pltpu.VMEM((keys, HD + 16), bf16),
                pltpu.VMEM((HD, keys), bf16),
                pltpu.VMEM((HD, keys), f32),
                pltpu.VMEM((HD, keys), f32),
            ],
        ),
        out_shape=[jax.ShapeDtypeStruct(query.shape, bf16)]
        + [jax.ShapeDtypeStruct(kv.shape, t) for kv, t in zip(kv_list, types)],
        compiler_params=pltpu.CompilerParams(vmem_limit_bytes=48 << 20),
        cost_estimate=cost(query, keys, 5),
        name=name,
    )(meta, query, *kv_list, grad, out, lse)


def gain_of(w_ref, first, k):
    return w_ref[0, :, first + k : first + k + 1].astype(f32)


def other_first(i, place, half):
    return jnp.where(i < half, (1 - place[1]) * half + i, place[1] * half + i - half)


def kernel_params():
    return pltpu.CompilerParams(vmem_limit_bytes=60 << 20)


def whole(value):
    return pl.BlockSpec(value.shape, lambda *i: (0,) * value.ndim)


def by_columns(count, body):
    step = min(128, count)

    def one(j, carry):
        body(pl.ds(pl.multiple_of(j * step, step), step))
        return carry

    lax.fori_loop(0, count // step, one, 0)


def norm_stats(resid):
    width = resid.shape[0]
    mean = jnp.sum(resid, 0, keepdims=True) / width
    square = jnp.sum(resid * resid, 0, keepdims=True) / width
    inv_std = lax.rsqrt(square - mean * mean + NORM_EPS)
    return (resid - mean) * inv_std, inv_std


def norm_back(grad, gain, normed, inv_std):
    width = grad.shape[0]
    scaled = grad * gain
    total = jnp.sum(scaled, 0, keepdims=True) / width
    cross = jnp.sum(scaled * normed, 0, keepdims=True) / width
    return inv_std * (scaled - total - normed * cross)


def project_kernel(place_ref, near_ref, *refs, rows):
    x_refs = refs[:rows]
    q_ref, kv_ref, near_t = refs[rows:]
    feat = q_ref.shape[2]
    step = pl.program_id(0)

    @pl.when(step == 0)
    def _():
        for d in range(near_ref.shape[0]):
            near_t[d] = near_ref[d].T

    for k, x_ref in enumerate(x_refs):

        @pl.when(step == k)
        def _():
            for d in range(near_ref.shape[0]):
                proj = dot(near_t[d, : 3 * feat, :], x_ref[...], 1, 0)
                q_ref[0, d] = (proj[:feat] * (0.125 * LOG2E)).astype(bf16)
                kv_ref[0, d, 0] = proj[feat : 2 * feat].astype(bf16)
                kv_ref[0, d, 1] = proj[2 * feat :].astype(bf16)


def project(place, near, x_rows, feat):
    dp, width, cols = near.shape
    rows = len(x_rows)
    tokens = x_rows[0].shape[1]
    return pl.pallas_call(
        functools.partial(project_kernel, rows=rows),
        grid_spec=pltpu.PrefetchScalarGridSpec(
            num_scalar_prefetch=1,
            grid=(rows,),
            in_specs=[whole(near)] + [whole(x) for x in x_rows],
            out_specs=[
                pl.BlockSpec((1, dp, feat, tokens), lambda k, p: (p[0] ^ k, 0, 0, 0)),
                pl.BlockSpec((1, dp, 2, feat, tokens), lambda k, p: (p[0] ^ k, 0, 0, 0, 0)),
            ],
            scratch_shapes=[pltpu.VMEM((dp, cols, width), bf16)],
        ),
        out_shape=[
            jax.ShapeDtypeStruct((rows, dp, feat, tokens), bf16),
            jax.ShapeDtypeStruct((rows, dp, 2, feat, tokens), bf16),
        ],
        compiler_params=kernel_params(),
        name="project",
    )(place, near, *x_rows)


def project_back_kernel(place_ref, near_ref, *refs, rows, sources):
    x_refs, dq_ref = refs[:rows], refs[rows]
    dkv_refs = refs[rows + 1 : rows + 1 + sources]
    dx_ref, gother_ref, gown_ref, acc = refs[rows + 1 + sources :]
    step = pl.program_id(0)
    feat = dq_ref.shape[2]

    @pl.when(step == 0)
    def _():
        acc[...] = jnp.zeros_like(acc)

    for k, x_ref in enumerate(x_refs):

        @pl.when(step == k)
        def _():
            total = None
            for d in range(near_ref.shape[0]):
                parts = [dq_ref[0, d]]
                for kind in range(2):
                    value = sum(ref[0, d, kind].astype(f32) for ref in dkv_refs)
                    parts.append(value.astype(bf16))
                grad = jnp.concatenate(parts, axis=0)
                acc[d, :, : 3 * feat] += dot(x_ref[...], grad, 1, 1)
                part = dot(near_ref[d, :, : 3 * feat], grad, 1, 0)
                total = part if total is None else total + part
            dx_ref[0] = total.astype(bf16)

    @pl.when(step == rows - 1)
    def _():
        gown_ref[...] = acc[place_ref[1]].astype(bf16)
        gother_ref[...] = acc[1 - place_ref[1]].astype(bf16)


def project_back(place, near, x_rows, d_query, d_kv):
    dp, width, cols = near.shape
    rows = len(x_rows)
    tokens = x_rows[0].shape[1]
    feat = d_query.shape[2]
    kv_spec = pl.BlockSpec((1, dp, 2, feat, tokens), lambda k, p: (p[0] ^ k, 0, 0, 0, 0))
    half = jax.ShapeDtypeStruct((width, cols), bf16)
    return pl.pallas_call(
        functools.partial(project_back_kernel, rows=rows, sources=len(d_kv)),
        grid_spec=pltpu.PrefetchScalarGridSpec(
            num_scalar_prefetch=1,
            grid=(rows,),
            in_specs=[whole(near)]
            + [whole(x) for x in x_rows]
            + [pl.BlockSpec((1, dp, feat, tokens), lambda k, p: (p[0] ^ k, 0, 0, 0))]
            + [kv_spec] * len(d_kv),
            out_specs=[
                pl.BlockSpec((1, width, tokens), lambda k, p: (p[0] ^ k, 0, 0)),
                whole(half),
                whole(half),
            ],
            scratch_shapes=[pltpu.VMEM(near.shape, f32)],
        ),
        out_shape=[
            jax.ShapeDtypeStruct((rows, width, tokens), bf16),
            half,
            half,
        ],
        compiler_params=kernel_params(),
        cost_estimate=pl.CostEstimate(
            flops=12 * rows * dp * width * feat * tokens, bytes_accessed=16 << 20, transcendentals=0
        ),
        name="project_back",
    )(place, near, *x_rows, d_query, *d_kv)


def side_by_side(chosen_ref, wide):
    count, _, tokens = chosen_ref.shape
    for n in range(count):
        wide[:, n * tokens : (n + 1) * tokens] = chosen_ref[n]


def cross_kv_kernel(w_ref, chosen_ref, o_ref, wide):
    @pl.when(pl.program_id(0) == 0)
    def _():
        side_by_side(chosen_ref, wide)

    weight = w_ref[0][:, : o_ref.shape[1]].T
    o_ref[0] = dot(weight, wide[...], 1, 0).astype(bf16)


def cross_kv(small, chosen, feat):
    groups, width, cols = small.shape
    keys = chosen.shape[0] * chosen.shape[2]
    return pl.pallas_call(
        cross_kv_kernel,
        grid=(groups,),
        in_specs=[pl.BlockSpec((1, width, 2 * 128), lambda g: (g, 0, 0)), whole(chosen)],
        out_specs=pl.BlockSpec((1, 2 * feat, keys), lambda g: (g, 0, 0)),
        out_shape=jax.ShapeDtypeStruct((groups, 2 * feat, keys), bf16),
        scratch_shapes=[pltpu.VMEM((width, keys), bf16)],
        compiler_params=kernel_params(),
        name="cross_kv",
    )(small, chosen)


def attn_place(g, rows):
    return g % rows, g // rows


def after_self_kernel(x_ref, attn_ref, w_ref, normed_ref, inv_ref, low_ref, cq_ref, acc):
    groups, feat, tokens = cq_ref.shape
    rows = attn_ref.shape[0]
    total = x_ref[...].astype(f32)
    for g in range(groups):
        r, d = attn_place(g, rows)
        total = total + dot(w_ref[g, :, 2 * feat : 3 * feat], attn_ref[r, d], 1, 0)
    acc[...] = total

    def body(at):
        normed, inv_std = norm_stats(acc[:, at])
        normed_ref[:, at] = normed
        inv_ref[:, at] = inv_std
        low_ref[:, at] = (normed * gain_of(w_ref, 5 * feat, 0)).astype(bf16)

    by_columns(tokens, body)
    low = low_ref[...]
    for g in range(groups):
        query = dot(w_ref[g, :, 3 * feat : 4 * feat], low, 0, 0)
        cq_ref[g] = (query * (0.125 * LOG2E)).astype(bf16)


def after_self(x_own, attn, small, feat):
    width, tokens = x_own.shape
    groups = small.shape[0]
    args = (x_own, attn, small)
    outs = [
        jax.ShapeDtypeStruct((width, tokens), f32),
        jax.ShapeDtypeStruct((1, tokens), f32),
        jax.ShapeDtypeStruct((width, tokens), bf16),
        jax.ShapeDtypeStruct((groups, feat, tokens), bf16),
    ]
    return pl.pallas_call(
        after_self_kernel,
        grid=(1,),
        in_specs=[whole(a) for a in args],
        out_specs=[whole(o) for o in outs],
        out_shape=outs,
        scratch_shapes=[pltpu.VMEM((width, tokens), f32)],
        compiler_params=kernel_params(),
        name="after_self",
    )(*args)


def middle_kernel(
    normed_one_ref, catt_ref, wc_ref, up_ref, down_ref, cot_ref,
    out_ref, dcatt_ref, dy_ref, dcross_ref, glarge_ref, dg_two_ref, dg_three_ref,
    acc, normed_two, inv_two, act, slope, h_fm, h_tm, d_fm, d_tm,
):
    i = pl.program_id(0)
    groups, feat, tokens = catt_ref.shape
    units = up_ref.shape[2]
    step = min(256, tokens)

    @pl.when(i == 0)
    def _():
        total = normed_one_ref[...] * gain_of(wc_ref, feat, 0)
        for g in range(groups):
            total = total + dot(wc_ref[g, :, :feat], catt_ref[g], 1, 0)
        acc[...] = total

        def body(at):
            normed, inv_std = norm_stats(acc[:, at])
            normed_two[:, at] = normed
            inv_two[:, at] = inv_std
            value = normed * gain_of(wc_ref, feat, 1)
            acc[:, at] = value
            h_fm[:, at] = value.astype(bf16)

        by_columns(tokens, body)
        h_tm[...] = h_fm[...].T

    @pl.when(i < groups)
    def _():
        for t in range(0, tokens, step):
            upper = dot(h_tm[t : t + step, :], up_ref[0], 1, 0)
            cdf = 0.5 * (1.0 + lax.erf(upper * 0.7071067811865476))
            density = jnp.exp(-0.5 * upper * upper) * 0.3989422804014327
            act[i, t : t + step, :] = (upper * cdf).astype(bf16)
            slope[i, t : t + step, :] = (cdf + upper * density).astype(bf16)
        acc[...] += dot(down_ref[0], act[i], 1, 1)

    @pl.when(i == groups - 1)
    def _():
        dg_three_ref[...] = jnp.zeros_like(dg_three_ref)
        dg_two_ref[...] = jnp.zeros_like(dg_two_ref)

        def body(at):
            normed, inv_std = norm_stats(acc[:, at])
            gain = gain_of(wc_ref, feat, 2)
            out_ref[:, at] = (normed * gain).astype(bf16)
            grad = cot_ref[:, at].astype(f32)
            dg_three_ref[...] += grad * normed
            value = norm_back(grad, gain, normed, inv_std)
            acc[:, at] = value
            d_fm[:, at] = value.astype(bf16)

        by_columns(tokens, body)
        d_tm[...] = d_fm[...].T

    @pl.when(i >= groups)
    def _():
        g = i - groups
        for t in range(0, tokens, step):
            at = slice(t, t + step)
            back = dot(d_tm[at, :], down_ref[0], 1, 0) * slope[g, at, :].astype(f32)
            slope[g, at, :] = back.astype(bf16)
        glarge_ref[0, :, units:] = dot(d_fm[...], act[g], 1, 0).astype(bf16)
        glarge_ref[0, :, :units] = dot(h_fm[...], slope[g], 1, 0).astype(bf16)
        acc[...] += dot(up_ref[0], slope[g], 1, 1)

    @pl.when(i == 2 * groups - 1)
    def _():
        def body(at):
            grad = acc[:, at]
            normed = normed_two[:, at]
            dg_two_ref[...] += grad * normed
            value = norm_back(grad, gain_of(wc_ref, feat, 1), normed, inv_two[:, at])
            dy_ref[:, at] = value
            dcross_ref[:, at] = value.astype(bf16)

        by_columns(tokens, body)
        low = dcross_ref[...]
        for g in range(groups):
            dcatt_ref[g] = dot(wc_ref[g, :, :feat], low, 0, 0).astype(bf16)


def middle(normed_one, catt, small, large, cot):
    width, tokens = normed_one.shape
    groups, feat, _ = catt.shape
    units = large.shape[2] // 2
    lanes = min(128, tokens)

    def weight(kind):
        return pl.BlockSpec((1, width, units), lambda i: (i % groups, 0, kind))

    outs = [
        jax.ShapeDtypeStruct((width, tokens), bf16),
        jax.ShapeDtypeStruct(catt.shape, bf16),
        jax.ShapeDtypeStruct((width, tokens), f32),
        jax.ShapeDtypeStruct((width, tokens), bf16),
        jax.ShapeDtypeStruct(large.shape, bf16),
        jax.ShapeDtypeStruct((width, lanes), f32),
        jax.ShapeDtypeStruct((width, lanes), f32),
    ]
    specs = [whole(o) for o in outs]
    specs[4] = pl.BlockSpec(
        (1, width, 2 * units), lambda i: (jnp.maximum(i - groups, 0), 0, 0)
    )
    return pl.pallas_call(
        middle_kernel,
        grid=(2 * groups,),
        in_specs=[
            whole(normed_one),
            whole(catt),
            pl.BlockSpec((groups, width, 128), lambda i: (0, 0, 3)),
            weight(0),
            weight(1),
            whole(cot),
        ],
        out_specs=specs,
        scratch_shapes=[
            pltpu.VMEM((width, tokens), f32),
            pltpu.VMEM((width, tokens), f32),
            pltpu.VMEM((1, tokens), f32),
            pltpu.VMEM((groups, tokens, units), bf16),
            pltpu.VMEM((groups, tokens, units), bf16),
            pltpu.VMEM((width, tokens), bf16),
            pltpu.VMEM((tokens, width), bf16),
            pltpu.VMEM((width, tokens), bf16),
            pltpu.VMEM((tokens, width), bf16),
        ],
        out_shape=outs,
        compiler_params=kernel_params(),
        cost_estimate=pl.CostEstimate(
            flops=12 * groups * width * units * tokens, bytes_accessed=8 * large.size, transcendentals=0
        ),
        name="middle",
    )(normed_one, catt, small, large, large, cot)


def before_self_kernel(
    dcq_ref, w_ref, dy_ref, normed_ref, inv_ref,
    dattn_ref, dlow_ref, dy_one_ref, dg_ref, acc,
):
    groups, feat, tokens = dcq_ref.shape
    rows = dattn_ref.shape[0]
    total = dy_ref[...]
    for g in range(groups):
        total = total + dot(w_ref[g, :, 3 * feat : 4 * feat], dcq_ref[g], 1, 0)
    acc[...] = total
    dg_ref[...] = jnp.zeros_like(dg_ref)

    def body(at):
        grad = acc[:, at]
        normed = normed_ref[:, at]
        dg_ref[...] += grad * normed
        value = norm_back(grad, gain_of(w_ref, 5 * feat, 0), normed, inv_ref[:, at])
        dy_one_ref[:, at] = value
        dlow_ref[:, at] = value.astype(bf16)

    by_columns(tokens, body)
    low = dlow_ref[...]
    for g in range(groups):
        r, d = attn_place(g, rows)
        dattn_ref[r, d] = dot(w_ref[g, :, 2 * feat : 3 * feat], low, 0, 0).astype(bf16)


def before_self(d_cq, small, dy_two, normed_one, inv_one, attn_shape):
    width, tokens = dy_two.shape
    args = (d_cq, small, dy_two, normed_one, inv_one)
    outs = [
        jax.ShapeDtypeStruct(attn_shape, bf16),
        jax.ShapeDtypeStruct((width, tokens), bf16),
        jax.ShapeDtypeStruct((width, tokens), f32),
        jax.ShapeDtypeStruct((width, min(128, tokens)), f32),
    ]
    return pl.pallas_call(
        before_self_kernel,
        grid=(1,),
        in_specs=[whole(a) for a in args],
        out_specs=[whole(o) for o in outs],
        out_shape=outs,
        scratch_shapes=[pltpu.VMEM((width, tokens), f32)],
        compiler_params=kernel_params(),
        name="before_self",
    )(*args)


def small_grads_kernel(
    place_ref, w_ref, chosen_ref, dckv_ref, attn_ref, dcq_ref, catt_ref, dlow_ref, h_ref,
    dcross_ref, dg_one_ref, dg_two_ref, dg_three_ref, rother_ref, rown_ref, cother_ref, cown_ref,
    wide, acc, gain_cols, *, paired,
):
    g = pl.program_id(0)
    feat2 = dckv_ref.shape[1]
    feat = feat2 // 2
    count, width, tokens = chosen_ref.shape
    share = count // 2
    half = pl.num_programs(0) // 2

    @pl.when(g == 0)
    def _():
        side_by_side(chosen_ref, wide)
        col = lax.broadcasted_iota(jnp.int32, gain_cols.shape, 1)
        total = jnp.zeros(gain_cols.shape, f32)
        for k, ref in enumerate((dg_one_ref, dg_two_ref, dg_three_ref)):
            total = jnp.where(col == k, jnp.sum(ref[...], axis=1, keepdims=True), total)
        gain_cols[...] = total.astype(bf16)
        acc[...] = jnp.zeros_like(acc)

    grad = dckv_ref[0]
    acc[...] += dot(w_ref[0][:, :feat2], grad, 1, 0)
    parts = [dot(wide[...], grad, 1, 1).astype(bf16)]
    pairs = ((dlow_ref, attn_ref[0, 0]), (h_ref, dcq_ref[0]), (dcross_ref, catt_ref[0]))
    for left, right in pairs:
        parts.append(dot(left[...], right, 1, 1).astype(bf16))
    parts.append(gain_cols[...])

    def put(ref):
        at = 0
        for part in parts:
            ref[0, :, at : at + part.shape[1]] = part
            at += part.shape[1]

    @pl.when(g < half)
    def _():
        put(rother_ref)

    @pl.when(g >= half)
    def _():
        put(rown_ref)

    @pl.when(g == pl.num_programs(0) - 1)
    def _():
        for n in range(count):
            piece = acc[:, n * tokens : (n + 1) * tokens].astype(bf16)
            if paired:
                ref = cother_ref if n % 2 else cown_ref
                ref[n // 2] = piece
                continue
            mine = place_ref[1] == n // share

            @pl.when(mine)
            def _():
                cown_ref[n % share] = piece

            @pl.when(jnp.logical_not(mine))
            def _():
                cother_ref[n % share] = piece


def small_grads(place, small, chosen, d_ckv, attn, d_cq, catt, d_low, h_low, d_cross, dgs, paired):
    groups, width, cols = small.shape
    _, feat2, keys = d_ckv.shape
    feat = feat2 // 2
    tokens = d_low.shape[1]
    rows = attn.shape[0]
    half = groups // 2

    def order(g, p):
        return other_first(g, p, half)

    def rest_out(first):
        return pl.BlockSpec((1, width, cols), lambda g, p: (jnp.clip(g - first, 0, half - 1), 0, 0))

    piece = pl.BlockSpec((1, feat, tokens), lambda g, p: (order(g, p), 0, 0))
    share = jax.ShapeDtypeStruct((chosen.shape[0] // 2,) + chosen.shape[1:], bf16)
    rest_shape = jax.ShapeDtypeStruct((half, width, cols), bf16)
    return pl.pallas_call(
        functools.partial(small_grads_kernel, paired=paired),
        grid_spec=pltpu.PrefetchScalarGridSpec(
            num_scalar_prefetch=1,
            grid=(groups,),
            in_specs=[
                pl.BlockSpec((1, width, 2 * 128), lambda g, p: (order(g, p), 0, 0)),
                whole(chosen),
                pl.BlockSpec((1, feat2, keys), lambda g, p: (order(g, p), 0, 0)),
                pl.BlockSpec(
                    (1, 1, feat, tokens),
                    lambda g, p: (order(g, p) % rows, order(g, p) // rows, 0, 0),
                ),
                piece,
                piece,
                whole(d_low),
                whole(h_low),
                whole(d_cross),
            ]
            + [whole(v) for v in dgs],
            out_specs=[rest_out(0), rest_out(half), whole(share), whole(share)],
            scratch_shapes=[
                pltpu.VMEM((width, keys), bf16),
                pltpu.VMEM((width, keys), f32),
                pltpu.VMEM((width, cols - 5 * feat), bf16),
            ],
        ),
        out_shape=[rest_shape, rest_shape, share, share],
        compiler_params=kernel_params(),
        cost_estimate=pl.CostEstimate(
            flops=groups * width * (4 * feat2 * keys + 6 * feat * tokens),
            bytes_accessed=4 * small.size,
            transcendentals=0,
        ),
        name="small_grads",
    )(place, small, chosen, d_ckv, attn, d_cq, catt, d_low, h_low, d_cross, *dgs)


def row_major(value):
    return with_layout_constraint(value, Layout(tuple(range(value.ndim))))


def mm(spec, left, right):
    return jnp.einsum(spec, left, right, preferred_element_type=f32)


def per_device(
    x_in, prefix, enc_bank, bank_rows, w_qkv, w_out, w_cross_q, w_cross_kv, w_cross_out,
    w_up, w_down, ln_gains, out_grad,
):
    dp, rows, cols = lax.axis_size("dp"), lax.axis_size("row"), lax.axis_size("col")
    d_pos, r_pos, c_pos = lax.axis_index("dp"), lax.axis_index("row"), lax.axis_index("col")
    own_seqs, part_width, row_len = x_in.shape
    seqs = own_seqs * dp
    sub = cols // seqs
    parts = dp * sub
    width = part_width * cols
    tokens = row_len // parts
    heads = w_qkv.shape[2]
    feat = heads * HALF
    units = w_up.shape[1]
    odd = (r_pos % 2) == 1
    seq_pos = c_pos // sub
    part_pos = d_pos * sub + c_pos % sub
    groups = [[s * sub + k for k in range(sub)] for s in range(seqs)]
    everywhere = ("dp", "row", "col")
    swap = [(0, 1), (1, 0)]
    first_core = d_pos == 0

    def flip(value):
        return jnp.where(odd, value[:, :, ::-1], value)

    def swap_cores(value):
        take = value.shape[-1] // parts
        if parts == 2:
            low, high = value[..., :take], value[..., take:]
            upper = first_core == odd
            got = lax.ppermute(jnp.where(upper, low, high), "dp", swap)
            kept = jnp.where(upper, high, low)
            value = jnp.concatenate(
                [jnp.where(first_core, kept, got), jnp.where(first_core, got, kept)], axis=0
            )
        else:
            value = flip(value.reshape(own_seqs, part_width, parts, take))
            value = value.reshape(own_seqs, part_width, dp, sub, take)
            value = lax.all_to_all(value, "dp", 2, 0, tiled=True)
            value = value.reshape(seqs, part_width, sub, take).transpose(0, 2, 1, 3)
        return value.reshape(cols, part_width, take)

    def across_cols(value):
        return lax.all_to_all(value, "col", 0, 0, tiled=True).reshape(width, value.shape[-1])

    def to_tokens(value):
        return across_cols(swap_cores(value))

    def row_gather(value):
        if rows != 4:
            every = lax.all_gather(value, "row", axis=0)
            return [lax.dynamic_index_in_dim(every, r_pos ^ k, 0, False) for k in range(rows)]

        def send(v, k):
            return lax.ppermute(v, "row", [(i, i ^ k) for i in range(rows)])

        near_one, near_two = send(value, 1), send(value, 2)
        half = value.shape[0] // 2
        far = jnp.concatenate([send(near_two[:half], 1), send(near_one[half:], 2)], axis=0)
        return [value, near_one, near_two, far]

    def home_cols(value):
        value = value.reshape(cols, part_width, value.shape[-1])
        return lax.all_to_all(value, "col", 0, 0, tiled=True)

    def to_home(value):
        return home_cores(home_cols(value))

    def home_cores(value):
        take = value.shape[-1]
        if parts == 2:
            early, late = value[:own_seqs], value[own_seqs:]
            got = lax.ppermute(jnp.where(first_core, late, early), "dp", swap)
            kept = jnp.where(first_core, early, late)
            upper = first_core == odd
            return jnp.concatenate(
                [jnp.where(upper, got, kept), jnp.where(upper, kept, got)], axis=-1
            )
        value = value.reshape(seqs, sub, part_width, take).transpose(0, 2, 1, 3)
        value = value.reshape(seqs, part_width, 1, sub, take)
        value = lax.all_to_all(value, "dp", 0, 2, tiled=True)
        value = flip(value.reshape(own_seqs, part_width, parts, take))
        return value.reshape(own_seqs, part_width, parts * take)

    place = jnp.stack([r_pos, d_pos]).astype(jnp.int32)
    qkv = jnp.pad(w_qkv.reshape(part_width, 3 * feat), ((0, 0), (0, 384 - 3 * feat)))
    near = lax.all_gather(qkv, ("dp", "col"), axis=0).reshape(dp, width, qkv.shape[1])
    x_swapped = swap_cores(x_in)
    x_own = across_cols(x_swapped)
    x_rows = row_gather(x_own)
    tied, _ = lax.optimization_barrier(
        ((w_cross_kv, w_out, w_cross_q, w_cross_out, w_up, w_down, ln_gains), x_swapped)
    )
    small = jnp.concatenate(
        [
            tied[0].reshape(part_width, 2 * feat),
            tied[1].reshape(feat, part_width).T,
            tied[2].reshape(part_width, feat),
            tied[3].reshape(feat, part_width).T,
            tied[6].T,
            jnp.zeros((part_width, 512 - 5 * feat - 3), bf16),
        ],
        axis=1,
    )
    blocks = dp * rows

    def gather_all(value):
        value = lax.all_gather(value, everywhere, axis=0)
        return value.reshape(blocks, width, value.shape[-1])

    small_all = gather_all(small)
    large, _ = lax.optimization_barrier((jnp.concatenate([tied[4], tied[5].T], axis=1), x_own))
    large_all = gather_all(large)

    query, kv_own = project(place, near, x_rows, feat)
    query = query.reshape(rows, dp, heads, HALF, tokens)
    kv_own = kv_own.reshape(rows, dp, 2, heads, HALF, tokens)

    def index_of(row, part):
        return jnp.where(row % 2 == 1, parts - 1 - part, part) + row * parts

    row_ids = jnp.arange(rows, dtype=jnp.int32)
    if sub == 1:
        kv_list = [kv_own, lax.ppermute(kv_own, "dp", swap)]
        owners = [part_pos, 1 - part_pos]
    else:
        kv_all = lax.all_gather(kv_own, "col", axis=0, axis_index_groups=groups)
        kv_all = lax.all_gather(kv_all, "dp", axis=0).reshape((parts,) + kv_own.shape)
        kv_list = [kv_all[j] for j in range(parts)]
        owners = list(range(parts))
    q_start = index_of(row_ids, part_pos) * tokens
    places = [index_of(row_ids, owner) for owner in owners]
    seq_prefix = lax.all_gather(prefix, "dp", axis=0, tiled=True)[seq_pos]
    meta = jnp.concatenate([seq_prefix[None], q_start] + places).astype(jnp.int32)
    mixed, lse = attend(meta, query, kv_list, True, "self_attention")
    attn = lax.all_to_all(mixed, "row", 0, 0, tiled=True).reshape(rows, dp, feat, tokens)
    normed_one, inv_one, h_low, cross_q = after_self(x_own, attn, small_all, feat)
    cross_q = cross_q.reshape(1, dp, rows, heads, HALF, tokens)

    picked = bank_rows.shape[1] // rows
    row_pick = lax.dynamic_slice_in_dim(bank_rows, r_pos * picked, picked, 1)
    bank_ids = jnp.arange(enc_bank.shape[2], dtype=jnp.int32)
    hot = (bank_ids[None, :, None] == row_pick[:, None, :]).astype(bf16)
    chosen = to_tokens(mm("swn,snp->swp", enc_bank, hot).astype(bf16))
    c_tokens = chosen.shape[1]
    if sub > 1:
        chosen = lax.all_gather(chosen, "col", axis=0, axis_index_groups=groups)
        chosen = lax.all_gather(chosen, ("dp", "row"), axis=0)
        chosen = chosen.reshape(blocks * sub, width, c_tokens)
    else:
        pair = jnp.stack([chosen, lax.ppermute(chosen, "dp", swap)])
        chosen = jnp.concatenate(row_gather(pair), axis=0)
    ckv = cross_kv(small_all, chosen, feat)
    ckv = ckv.reshape(1, dp, rows, 2, heads, HALF, ckv.shape[-1])
    catt, lse_cross = attend(meta, cross_q, [ckv], False, "cross_attention")
    catt_flat = catt.reshape(blocks, feat, tokens)

    cot = to_tokens(out_grad)
    block_out, d_catt, dy_two, d_cross, g_large, dg_two, dg_three = middle(
        normed_one, catt_flat, small_all, large_all, cot
    )
    block_out = home_cols(block_out)


    def with_core(own, got):
        return (own.astype(f32) + got.astype(f32)).astype(bf16)

    large_grad = g_large.reshape(dp, rows, cols, part_width, 2 * units)
    large_grad = lax.psum_scatter(large_grad, "dp", scatter_dimension=0, tiled=False)
    d_cq, d_ckv = attend_back(
        meta, cross_q, [ckv], d_catt.reshape(catt.shape), catt, lse_cross, False, [bf16],
        "cross_attention_back",
    )
    large_grad, d_cq, block_out = lax.optimization_barrier((large_grad, d_cq, block_out))
    large_grad = lax.psum_scatter(large_grad, "row", scatter_dimension=0, tiled=False)
    d_cq = d_cq.reshape(blocks, feat, tokens)
    d_ckv = d_ckv.reshape(blocks, 2 * feat, d_ckv.shape[-1])
    d_attn, d_low, dy_one, dg_one = before_self(
        d_cq, small_all, dy_two, normed_one, inv_one, attn.shape
    )
    d_mixed = lax.all_to_all(d_attn, "row", 0, 0, tiled=True).reshape(mixed.shape)
    rest_other, rest, chosen_other, d_chosen = small_grads(
        place, small_all, chosen, d_ckv, attn, d_cq, catt_flat, d_low, h_low, d_cross,
        (dg_one, dg_two, dg_three), sub == 1,
    )
    d_mixed, rest_other, rest, chosen_other, d_chosen = lax.optimization_barrier(
        (d_mixed, rest_other, rest, chosen_other, d_chosen)
    )
    rest = with_core(rest, lax.ppermute(rest_other, "dp", swap))
    d_chosen = with_core(d_chosen, lax.ppermute(chosen_other, "dp", swap))
    rest, d_mixed, d_chosen = lax.optimization_barrier((rest, d_mixed, d_chosen))
    rest = rest.reshape(rows, cols, part_width, -1)
    rest = lax.psum_scatter(rest, "row", scatter_dimension=0, tiled=False)
    if sub == 1:
        d_chosen = [d_chosen[0]] + [
            lax.ppermute(d_chosen[k], "row", [(i, i ^ k) for i in range(rows)])
            for k in range(1, rows)
        ]
    else:
        d_chosen = d_chosen.reshape(rows, sub * width, c_tokens)
        d_chosen = list(lax.all_to_all(d_chosen, "row", 0, 0, tiled=True))

    types = [f32] + [bf16] * (len(kv_list) - 1) if sub == 1 else [bf16] * len(kv_list)
    d_query, *d_kv = attend_back(
        meta, query, kv_list, d_mixed, mixed, lse, True, types, "self_attention_back"
    )
    d_query, d_kv, d_chosen, large_grad = lax.optimization_barrier(
        (d_query, d_kv, d_chosen, large_grad)
    )
    large_grad = lax.psum_scatter(large_grad, "col", scatter_dimension=0, tiled=False)
    large_grad = row_major(large_grad)
    if sub == 1:
        d_kv = [d_kv[0], lax.ppermute(d_kv[1], "dp", swap)]
    else:
        d_kv = jnp.stack(d_kv).reshape((dp, sub) + kv_own.shape)
        d_kv = lax.psum_scatter(d_kv, "dp", scatter_dimension=0, tiled=True)
        d_kv = lax.psum_scatter(
            d_kv, "col", scatter_dimension=1, tiled=True, axis_index_groups=groups
        )
        d_kv = [d_kv]
    kv_shape = (rows, dp, 2, feat, tokens)
    d_kv = [value.reshape(kv_shape) for value in d_kv]
    dx_part, qkv_other, g_qkv = project_back(
        place, near, x_rows, d_query.reshape(rows, dp, feat, tokens), d_kv
    )
    dx_part = lax.all_to_all(dx_part, "row", 0, 0, tiled=True)
    dx_part, large_grad = lax.optimization_barrier((dx_part, large_grad))
    large_grad = large_grad.astype(f32)
    dx = dy_one + jnp.sum(dx_part.astype(f32), axis=0)
    x_moved = home_cols(dx.astype(bf16))

    d_chosen = sum(piece.astype(f32) for piece in d_chosen).astype(bf16)
    if sub > 1:
        d_chosen = lax.psum_scatter(
            d_chosen.reshape(sub, width, c_tokens), "col", scatter_dimension=0, tiled=True,
            axis_index_groups=groups,
        )
    d_chosen = d_chosen.reshape(width, c_tokens)
    d_chosen = jnp.concatenate(row_gather(to_home(d_chosen)), axis=2)
    pick_rows = jnp.concatenate(
        [
            lax.dynamic_slice_in_dim(bank_rows, (r_pos ^ k) * picked, picked, 1)
            for k in range(rows)
        ],
        axis=1,
    )
    hot_all = (pick_rows[:, :, None] == bank_ids[None, None, :]).astype(bf16)
    bank_grad = mm("swp,spn->swn", d_chosen, hot_all)
    x_moved, bank_grad = lax.optimization_barrier((x_moved, bank_grad))
    x_grad = home_cores(x_moved).astype(f32)

    qkv = with_core(g_qkv, lax.ppermute(qkv_other, "dp", swap))
    last = jnp.concatenate([rest, qkv.reshape(cols, part_width, -1)], axis=2)
    last = lax.psum_scatter(last, "col", scatter_dimension=0, tiled=False).astype(f32)
    rest, qkv_grad = last[:, :512], last[:, 512:]

    return (
        home_cores(block_out),
        x_grad,
        bank_grad,
        qkv_grad[:, : 3 * feat].reshape(w_qkv.shape),
        rest[:, 2 * feat : 3 * feat].T.reshape(w_out.shape),
        rest[:, 3 * feat : 4 * feat].reshape(w_cross_q.shape),
        rest[:, : 2 * feat].reshape(w_cross_kv.shape),
        rest[:, 4 * feat : 5 * feat].T.reshape(w_cross_out.shape),
        large_grad[:, :units],
        large_grad[:, units:].T,
        rest[:, 5 * feat : 5 * feat + 3].T,
    )


def solution(mesh):
    placed = (
        P("dp", "col", "row"),
        P("dp"),
        P("dp", "col", None),
        P("dp", None),
        P("col", None, "row", "dp"),
        P("row", "dp", "col"),
        P("col", "row", "dp"),
        P("col", None, "row", "dp"),
        P("row", "dp", "col"),
        P("col", ("dp", "row")),
        P(("dp", "row"), "col"),
        P(None, "col"),
        P("dp", "col", "row"),
    )
    return jax.shard_map(
        per_device,
        mesh=mesh,
        in_specs=placed,
        out_specs=(
            P("dp", "col", "row"),
            P("dp", "col", "row"),
            P("dp", "col", None),
            P("col", None, "row", "dp"),
            P("row", "dp", "col"),
            P("col", "row", "dp"),
            P("col", None, "row", "dp"),
            P("row", "dp", "col"),
            P("col", ("dp", "row")),
            P(("dp", "row"), "col"),
            P(None, "col"),
        ),
        check_vma=False,
    )
```
